32 devices in a mesh: batch: 2 (over x), rows: 16 (over z, y, core).
Axes of the slice: x: 2, y: 2, z: 4, core: 2. Of those that a mesh axis runs over, the one named last changes fastest.
Arguments:
- layer_input: bfloat16 [2, 64, 64, 2048], P('batch', 'rows'), may hold values from -6 to 6
- pre_activation: bfloat16 [2, 64, 64, 2048], P('batch', 'rows'), may hold values from -6 to 6
- cotangent: bfloat16 [2, 64, 64, 2048], P('batch', 'rows'), may hold values from -6 to 6
- weight: bfloat16 [64, 64], replicated, may hold values from -0.75 to 0.75
- spectral: bfloat16 [2304, 64, 128], P('rows'), may hold values from -6 to 6
- slab_ids: int32 [2, 32], P('batch'), may hold values from 0 to 2047, as said below
- extents: int32 [2, 32], P('batch'), may hold values from 1 to 2048, as said below
Outputs:
- grad_input: bfloat16 [2, 64, 64, 2048], P('batch', 'rows')
- grad_spectral: float32 [2304, 64, 128], P('rows')
- grad_weight: float32 [64, 64], replicated
The draws below stay inside these ranges and needn't reach their ends.
Inputs may be any that keep to these rules, and one draw needn't show every extreme that they name: `slab_ids`: within a sample the 32 slab numbers are distinct and include 0 and 2047; slots 2 k to 2 k + 1 are stored on index k of rows. `extents`: A slot's extent counts its slab's live columns from column 0.
All inputs are finite; a program needn't handle non-finite values.
Results may differ from the reference program's by a relative error of at most 0.0085.
Values may be sent and summed in bfloat16 or wider, within the bound.
No kernel may reach another device: no remote copies, remote signals or barrier semaphores. Data moves between devices by JAX's collectives and lax.ppermute only.
A program may use at most 128 MiB of HBM per device.

```python
import math
import jax
import jax.numpy as jnp
from jax import lax

C = 64
PA = 48
SLAB = 2
NC = 2048
NR = 4096
MODES = 96
BATCH = 2
NACT = 32
NSLAB = 2048
PMODES = 2304


def active_slabs(key):
    base = jax.random.fold_in(key, 7)

    def one_sample(sample):
        sample_key = jax.random.fold_in(base, sample)
        inner = jax.random.permutation(jax.random.fold_in(sample_key, 1), NSLAB - 2)[:NACT - 2] + 1
        chosen = jnp.concatenate([jnp.array([0, NSLAB - 1], dtype=jnp.int32), inner.astype(jnp.int32)])
        return jax.random.permutation(jax.random.fold_in(sample_key, 2), chosen)
    return jax.vmap(one_sample)(jnp.arange(BATCH, dtype=jnp.int32)).astype(jnp.int32)


def draw_slab_ids(key, part):
    return active_slabs(key)


def draw_extents(key, part):
    slab_list = active_slabs(key)
    widths = jax.random.randint(jax.random.fold_in(key, 11), (BATCH, NSLAB), 1, NC + 1, dtype=jnp.int32)
    widths = widths.at[:, NSLAB - 1].set(NC).at[:, 0].set(1)
    return jnp.take_along_axis(widths, slab_list, axis=1).astype(jnp.int32)


def block_scale(key, shape, cuts, least, largest):
    loudness = 1.0
    for axis_at, blocks in cuts:
        heights = jax.random.uniform(jax.random.fold_in(jax.random.fold_in(key, 6), axis_at), (blocks,), jnp.float32, least / len(cuts), largest / len(cuts))
        loudness = loudness * jnp.repeat(jnp.exp(heights), shape[axis_at] // blocks).reshape((-1,) + (1,) * (len(shape) - 1 - axis_at))
    return loudness


def centred(rng, shape, scale, limit, pieces=(), held_as=jnp.bfloat16):
    values = scale * jax.random.normal(rng, shape, jnp.float32)
    if pieces:
        values = values * block_scale(rng, shape, pieces, -0.22, 0.18)
    return jnp.clip(values, -limit, limit).astype(held_as)


def setup_inputs(seed: int = 0) -> dict:
    seeds = jax.random.split(jax.random.key(seed), 8)
    layer_input = centred(seeds[0], (BATCH, NACT * SLAB, C, NC), 1.0, 6.0, ((0, 2), (1, 16)))
    pre_activation = centred(seeds[1], (BATCH, NACT * SLAB, C, NC), 1.0, 6.0, ((0, 2), (1, 16)))
    cotangent = centred(seeds[2], (BATCH, NACT * SLAB, C, NC), 1.0, 6.0, ((0, 2), (1, 16)))
    weight = centred(seeds[3], (C, C), C ** -0.5, 0.75)
    spectral = centred(seeds[4], (PMODES, C, 2 * C), 1.0, 6.0, ((0, 16),))
    slab_ids = draw_slab_ids(jax.random.fold_in(seeds[7], 71), 0)
    extents = draw_extents(jax.random.fold_in(seeds[7], 71), 0)
    return {"layer_input": layer_input, "pre_activation": pre_activation, "cotangent": cotangent, "weight": weight, "spectral": spectral, "slab_ids": slab_ids, "extents": extents}


def column_table(column_count, freq_count):
    column_index = jnp.arange(column_count, dtype=jnp.int32)
    freq_index = jnp.arange(freq_count, dtype=jnp.int32)
    phase = column_index[:, None] * freq_index[None, :] % column_count
    angle = phase.astype(jnp.float32) * (2.0 * math.pi / column_count)
    return jnp.concatenate([jnp.cos(angle), -jnp.sin(angle)], axis=1).astype(jnp.bfloat16)

def row_table(positions, row_total, freq_count):
    freq_index = jnp.arange(freq_count, dtype=jnp.int32) - freq_count // 2
    phase = jnp.mod(freq_index[:, None] * positions[None, :], row_total)
    angle = phase.astype(jnp.float32) * (2.0 * math.pi / row_total)
    return jnp.concatenate([jnp.cos(angle), jnp.sin(angle)], axis=0).astype(jnp.bfloat16)

def stored_positions(slab_list, slab_rows):
    offsets = jnp.tile(jnp.arange(slab_rows, dtype=jnp.int32), slab_list.shape[0])
    return (jnp.repeat(slab_list, slab_rows) * slab_rows + offsets).astype(jnp.int32)

def gelu_slope(values):
    return 0.5 * (1.0 + lax.erf(values * 0.7071067811865476)) + values * jnp.exp(-0.5 * values * values) * 0.3989422804014327

def row_combine(row_sums, scale):
    upper = row_sums[0]
    lower = row_sums[1]
    real_part = upper[:, :, 0] + lower[:, :, 1]
    imag_part = upper[:, :, 1] - lower[:, :, 0]
    return (jnp.stack([real_part, imag_part], axis=2) * scale).astype(jnp.bfloat16)

def to_blocks(spectra, half_modes):
    chans = spectra.shape[1]
    shaped = spectra.reshape(half_modes, 2, chans, 2, half_modes, 2)
    return shaped.transpose(2, 3, 1, 5, 0, 4).reshape(chans, 2, 2, 2, half_modes * half_modes)

def from_blocks(blocked, half_modes):
    chans = blocked.shape[0]
    shaped = blocked.reshape(chans, 2, 2, 2, half_modes, half_modes)
    return shaped.transpose(4, 2, 0, 1, 5, 3).reshape(2 * half_modes, chans, 2, 2 * half_modes)

def factor_pair(owned, chans):
    input_modes = owned[:chans]
    grad_out = owned[chans:]
    factor_left = input_modes.transpose(4, 0, 1, 2, 3).reshape(owned.shape[4], chans, 8)
    real_out = grad_out[:, 0]
    imag_out = grad_out[:, 1]
    first_half = jnp.stack([real_out, imag_out], axis=1)
    second_half = jnp.stack([imag_out, -real_out], axis=1)
    stacked = jnp.concatenate([first_half, second_half], axis=0)
    factor_right = stacked.transpose(4, 0, 1, 2, 3).reshape(owned.shape[4], 2 * chans, 8)
    return (factor_left, factor_right)

def modes_to_channels(grad_modes):
    blocks = grad_modes.shape[0]
    chans = grad_modes.shape[1]
    return grad_modes.reshape(blocks, chans, 2, 2, 2).transpose(1, 2, 3, 4, 0)

def row_adjoint(rowtab, grad_grid, scale):
    real_part = grad_grid[:, :, 0]
    imag_part = grad_grid[:, :, 1]
    upper = jnp.stack([real_part, imag_part], axis=2)
    lower = jnp.stack([-imag_part, real_part], axis=2)
    joined = jnp.concatenate([upper, lower], axis=0)
    summed = jnp.dot(rowtab.T, joined.reshape(joined.shape[0], -1), preferred_element_type=jnp.float32)
    return (summed * scale).astype(jnp.bfloat16)

def reference(layer_input, pre_activation, cotangent, weight, spectral, slab_ids, extents):
    scale = 1.0 / math.sqrt(NR * NC)
    coltab = column_table(NC, MODES)
    column_index = jnp.arange(NC, dtype=jnp.int32)
    grad_spectral = jnp.zeros((PMODES, C, 2 * C), jnp.float32)
    grad_weight = jnp.zeros((C, C), jnp.float32)
    results = []
    for sample in range(BATCH):
        alive = column_index[None, :] < jnp.repeat(extents[sample], SLAB)[:, None]
        mask_half = alive.astype(jnp.bfloat16)
        mask_full = alive.astype(jnp.float32)
        masked_in = layer_input[sample] * mask_half[:, None, :]
        grad_pre = (cotangent[sample].astype(jnp.float32) * mask_full[:, None, :] * gelu_slope(pre_activation[sample].astype(jnp.float32))).astype(jnp.bfloat16)
        stacked = jnp.concatenate([masked_in, grad_pre], axis=1)
        row_count = stacked.shape[0]
        colspec = jnp.dot(stacked.reshape(-1, NC), coltab, preferred_element_type=jnp.float32)
        colspec = colspec.reshape(row_count, 2 * C * 2 * MODES).astype(jnp.bfloat16)
        rowtab = row_table(stored_positions(slab_ids[sample], SLAB), NR, MODES)
        row_sums = jnp.dot(rowtab, colspec, preferred_element_type=jnp.float32).reshape(2, MODES, 2 * C, 2, MODES)
        spectra = row_combine(row_sums, scale)
        factor_left, factor_right = factor_pair(to_blocks(spectra, PA), C)
        grad_spectral = grad_spectral + jnp.einsum('bik,bxk->bix', factor_left.astype(jnp.float32), factor_right.astype(jnp.float32))
        grad_modes = jnp.einsum('bix,bxk->bik', spectral.astype(jnp.float32), factor_right.astype(jnp.float32)).astype(jnp.bfloat16)
        grad_grid = from_blocks(modes_to_channels(grad_modes), PA)
        rowback = row_adjoint(rowtab, grad_grid, scale)
        spatial = jnp.dot(rowback.reshape(-1, 2 * MODES), coltab.T, preferred_element_type=jnp.float32).reshape(row_count, C, NC)
        direct = jnp.einsum('io,roc->ric', weight.astype(jnp.float32), grad_pre.astype(jnp.float32))
        results.append(((spatial + direct) * mask_full[:, None, :]).astype(jnp.bfloat16))
        grad_weight = grad_weight + jnp.einsum('ric,roc->io', masked_in.astype(jnp.float32), grad_pre.astype(jnp.float32))
    grad_weight = grad_weight * (1.0 / math.sqrt(BATCH * NACT * SLAB * NC))
    return (jnp.stack(results), grad_spectral, grad_weight)
```

```python
import functools
import math

import jax
import jax.numpy as jnp
import numpy as np
from jax import lax
from jax.experimental import pallas as pl
from jax.experimental.pallas import tpu as pltpu
from jax.sharding import PartitionSpec as P

PA = 48
SLAB = 2
NR = 4096
MODES = 96
F32 = jnp.float32
BF16 = jnp.bfloat16
VMEM_LIMIT = 56 * 1024 * 1024


class Plan:
    def __init__(self, ranks, local_rows, channels, columns, held):
        self.ranks = ranks
        self.local_rows = local_rows
        self.channels = channels
        self.columns = columns
        self.held = held
        self.pairs = -(-PA // ranks)
        first = [(held * k) // PA for k in range(ranks)]
        last = [(held * (k + 1) - 1) // PA for k in range(ranks)]
        self.first = np.array(first, np.int32)
        self.steps = max(b - a for a, b in zip(first, last)) + 1
        self.exact = held == self.steps * PA and self.pairs * ranks == PA
        self.both = 2 * channels
        self.half = self.pairs * self.both
        self.group = 2 * local_rows
        self.share = channels // ranks
        self.scale = 1.0 / math.sqrt(NR * columns)

    def column_table(self):
        pair, part, odd, owner = np.meshgrid(
            np.arange(self.pairs),
            np.arange(2),
            np.arange(2),
            np.arange(self.ranks),
            indexing="ij",
        )
        freq = 2 * (self.pairs * owner + pair) + odd
        freq, part = freq.reshape(-1, 1), part.reshape(-1, 1)
        phase = (freq * np.arange(self.columns)[None, :]) % self.columns
        angle = 2.0 * math.pi * phase / self.columns
        table = np.where(part == 0, np.cos(angle), -np.sin(angle))
        return np.where(freq < MODES, table, 0.0).astype(np.float32).astype(jnp.bfloat16)

    def spread(self):
        out = np.zeros((self.ranks * self.group, self.group * self.ranks), np.float32)
        for owner in range(self.ranks):
            for e in range(self.group):
                out[owner * self.group + e, e * self.ranks + owner] = 1.0
        return out.astype(jnp.bfloat16)

    def gather_back(self):
        return self.spread().T

    def share_out(self):
        out = np.zeros((self.ranks * self.group, self.channels), np.float32)
        for i in range(self.channels):
            out[(i // self.share) * self.group + i % self.share, i] = 1.0
        return out.astype(jnp.bfloat16)

    def share_in(self):
        out = np.zeros((self.channels, self.ranks * 8), np.float32)
        for i in range(self.channels):
            base = (i // self.share) * 8 + i % self.share
            out[i, base] = 1.0
            out[i, base + self.share] = 1.0
        return out.astype(jnp.bfloat16)


def turn_table(freq, mode_part, mode_odd, positions, row_part, row_odd, mode_major):
    turn = lambda a, b: (a[:, None], b[None, :]) if mode_major else (a[None, :], b[:, None])
    f, pos = turn(jnp.asarray(freq), positions)
    mp, rp = turn(jnp.asarray(mode_part), jnp.asarray(row_part))
    mo, ro = turn(jnp.asarray(mode_odd), jnp.asarray(row_odd))
    phase = jnp.mod(f * pos + (mp - rp) * (NR // 4), NR)
    value = jnp.cos(phase.astype(F32) * (2.0 * math.pi / NR))
    return jnp.where(mo == ro, value, 0.0).astype(BF16)


def turn_tables(plan, slab_list):
    rows = plan.ranks * plan.local_rows
    row_index = np.arange(rows)
    positions = jnp.repeat(slab_list, SLAB) * SLAB + jnp.asarray(row_index % SLAB, jnp.int32)

    def modes(order):
        k, step, part, odd, low = np.meshgrid(
            *(np.arange(n) for n in (plan.ranks, plan.steps, 2, 2, 2)), indexing="ij"
        )
        freq = 2 * (plan.first[k] + step) + low - MODES // 2
        return [x.transpose(order).reshape(-1).astype(np.int32) for x in (freq, part, odd)]

    def rows_side(shape_order):
        odd, row, part = np.meshgrid(np.arange(2), row_index, np.arange(2), indexing="ij")
        odd, part = (x.transpose(shape_order).reshape(-1).astype(np.int32) for x in (odd, part))
        spread = jnp.broadcast_to(positions[None, :, None], (2, rows, 2))
        return spread.transpose(shape_order).reshape(-1), part, odd

    forward = turn_table(*modes((0, 1, 2, 3, 4)), *rows_side((0, 1, 2)), True)
    backward = turn_table(*modes((1, 0, 2, 3, 4)), *rows_side((2, 1, 0)), False)
    return forward, backward


def gelu_slope(values):
    return (
        0.5 * (1.0 + lax.erf(values * 0.7071067811865476))
        + values * jnp.exp(-0.5 * values * values) * 0.3989422804014327
    )


NT = (((1,), (1,)), ((), ()))
TN = (((0,), (0,)), ((), ()))


def column_kernel(
    plan, ext_ref, x_ref, pre_ref, cot_ref, tab_ref, spread_ref, share_ref,
    gp_ref, out_ref, v_ref, stage_ref, gw_ref,
):
    row = pl.program_id(0)
    chans, ranks = plan.channels, plan.ranks
    slots = plan.local_rows // SLAB
    extent = ext_ref[0, lax.axis_index("rows") * slots + row // SLAB]
    step = 256
    for start in range(0, plan.columns, step):
        cols = slice(start, start + step)
        live = lax.broadcasted_iota(jnp.int32, (chans, step), 1) + start < extent
        kept = jnp.where(live, x_ref[0, 0, :, cols].astype(F32), 0.0).astype(BF16)
        slope = gelu_slope(pre_ref[0, 0, :, cols].astype(F32))
        grad = jnp.where(live, cot_ref[0, 0, :, cols].astype(F32) * slope, 0.0).astype(BF16)
        v_ref[:chans, cols] = kept
        v_ref[chans:, cols] = grad
        gp_ref[0, :, cols] = grad
    spec = lax.dot_general(tab_ref[...], v_ref[...], NT, preferred_element_type=F32).astype(BF16)
    weight = lax.dot_general(v_ref[:chans], v_ref[chans:], NT, preferred_element_type=F32)
    for pair in range(plan.pairs):
        for part in range(2):
            for odd in range(2):
                base = ((pair * 2 + part) * 2 + odd) * ranks
                lane = (odd * plan.pairs + pair) * plan.both
                stage_ref[row, part, :, lane : lane + plan.both] = spec[base : base + ranks]

    @pl.when(row == 0)
    def _():
        gw_ref[...] = weight

    @pl.when(row > 0)
    def _():
        gw_ref[...] += weight

    @pl.when(row == plan.local_rows - 1)
    def _():
        wide = 2 * plan.half
        staged = stage_ref[...].reshape(plan.group * ranks, wide)
        out_ref[:, :wide] = jnp.dot(
            spread_ref[...], staged, preferred_element_type=F32
        ).astype(BF16)
        total = gw_ref[...]
        high = total.astype(BF16)
        low = (total - high.astype(F32)).astype(BF16)
        split = jnp.concatenate([high, low], axis=1)
        out_ref[:, wide:] = jnp.dot(
            share_ref[...], split, preferred_element_type=F32
        ).astype(BF16)


def row_kernel(plan, turn_ref, in_ref, out_ref, share_ref):
    half = plan.half
    stacked = jnp.concatenate([in_ref[:, :half], in_ref[:, half : 2 * half]], axis=0)
    sums = jnp.dot(turn_ref[...], stacked, preferred_element_type=F32)
    out_ref[...] = (sums * plan.scale).astype(BF16)
    pieces = in_ref[:, 2 * half :].astype(F32).reshape(plan.ranks, plan.group, plan.both)
    summed = jnp.sum(pieces, axis=0)
    share_ref[...] = summed + pltpu.roll(summed, plan.channels, axis=1)


def out_pair(tile, chans):
    lane = lax.broadcasted_iota(jnp.int32, tile.shape, 1)
    row = lax.broadcasted_iota(jnp.int32, tile.shape, 0)
    across = pltpu.roll(tile, chans, axis=1)
    other = pltpu.roll(tile, 4, axis=0)
    return jnp.where(lane < chans, across, jnp.where(row < 4, other, -other))


def where_held(plan, owner, step, pair, offset):
    place = step * PA + plan.pairs * owner + pair - offset
    ok = (place >= 0) & (place < plan.held) & (plan.pairs * owner + pair < PA)
    return jnp.clip(place, 0, plan.held - 1), ok


def mode_offset(plan):
    k = lax.axis_index("rows")
    return lax.rem(k * plan.held, PA)


def mix_kernel(plan, owners, samples, *refs):
    share_refs, (in_ref, spec_ref, out_ref) = refs[:samples], refs[samples:]
    chans = plan.channels
    total = share_refs[0][...]
    for ref in share_refs[1:]:
        total = total + ref[...]
    total = total[:8, :chans]
    high = total.astype(BF16).astype(F32)
    low = pltpu.roll(total - high, plan.share, axis=0)
    row = lax.broadcasted_iota(jnp.int32, total.shape, 0)
    zero = jnp.zeros_like(total)
    shared = jnp.where(row < plan.share, high, jnp.where(row < 2 * plan.share, low, zero))

    def body(local, carry):
        owner = pl.program_id(0) * owners + local
        pieces = []
        for step in range(plan.steps):
            for pair in range(plan.pairs):
                start = pl.multiple_of(local * (8 * plan.steps) + 8 * step, 8)
                tile = in_ref[pl.ds(start, 8), pair * plan.both : (pair + 1) * plan.both]
                left = out_pair(tile.astype(F32), chans).astype(BF16)
                if plan.exact:
                    right = spec_ref[step, local * plan.pairs + pair]
                else:
                    place, ok = where_held(plan, owner, step, pair, mode_offset(plan))
                    right = spec_ref[0, place]
                piece = lax.dot_general(left, right, NT, preferred_element_type=F32)
                if not plan.exact:
                    piece = jnp.where(ok, piece, 0.0)
                pieces.append(piece)
        if len(pieces) % 2 == 0:
            pieces.append(jnp.zeros_like(shared))
        pieces.append(shared)
        joined = jnp.concatenate(pieces[:-2] + [pieces[-2], pieces[-1]], axis=1)
        out_ref[pl.ds(pl.multiple_of(local * 8, 8), 8), :] = joined.astype(BF16)
        return carry

    lax.fori_loop(0, owners, body, 0)


def outer_kernel(plan, owners, samples, *refs):
    in_refs, out_ref = refs[:samples], refs[samples]
    chans = plan.channels
    swap = lax.axis_index("batch") != 0

    def body(local, carry):
        owner = pl.program_id(0) * owners + local
        for step in range(plan.steps):
            for pair in range(plan.pairs):
                start = pl.multiple_of(local * (8 * plan.steps) + 8 * step, 8)
                cols = slice(pair * plan.both, (pair + 1) * plan.both)
                tiles = [ref[pl.ds(start, 8), cols].astype(F32) for ref in in_refs]
                if samples == 2:
                    tiles = [
                        jnp.where(swap, tiles[1], tiles[0]),
                        jnp.where(swap, tiles[0], tiles[1]),
                    ]
                left = jnp.concatenate([t[:, :chans] for t in tiles], axis=0).astype(BF16)
                right = jnp.concatenate([out_pair(t, chans) for t in tiles], axis=0).astype(BF16)
                value = lax.dot_general(left, right, TN, preferred_element_type=F32)
                if plan.exact:
                    out_ref[step, local * plan.pairs + pair] = value
                else:
                    place, ok = where_held(plan, owner, step, pair, mode_offset(plan))

                    @pl.when(ok)
                    def _():
                        out_ref[0, place] = value
        return carry

    lax.fori_loop(0, owners, body, 0)


def adjoint_kernel(plan, weight_scale, turn_ref, in_ref, share_ref, out_ref, gw_ref):
    chans = plan.channels
    span = plan.pairs * chans
    parts = [in_ref[:, s * span : (s + 1) * span] for s in range(plan.steps)]
    sums = jnp.dot(turn_ref[...], jnp.concatenate(parts, axis=0), preferred_element_type=F32)
    sums = sums * plan.scale
    real, imag = sums[: sums.shape[0] // 2], sums[sums.shape[0] // 2 :]
    pieces = []
    for pair in range(plan.pairs):
        cols = slice(pair * chans, (pair + 1) * chans)
        pieces += [real[:, cols], imag[:, cols]]
    out_ref[...] = jnp.concatenate(pieces, axis=1).astype(BF16)
    shared = in_ref[:, in_ref.shape[1] - chans :]
    total = jnp.dot(share_ref[...], shared, preferred_element_type=F32)
    gw_ref[...] = total * weight_scale


def spatial_kernel(plan, step, ext_ref, in_ref, back_ref, w_ref, tab_ref, gp_ref, out_ref, left_ref):
    chans, rows = plan.channels, plan.local_rows
    block = 2 * plan.ranks
    slots = rows // SLAB
    first = lax.axis_index("rows") * slots

    @pl.when(pl.program_id(0) == 0)
    def _():
        ordered = jnp.dot(back_ref[...], in_ref[...], preferred_element_type=F32)
        for row in range(rows):
            lines = ordered[row * block : (row + 1) * block]
            pieces = [
                lines[:, b * chans : (b + 1) * chans] for b in range(2 * plan.pairs)
            ]
            stacked = jnp.concatenate(pieces, axis=0)
            left_ref[row * chans : (row + 1) * chans] = stacked.T.astype(BF16)

    spatial = jnp.dot(left_ref[...], tab_ref[...], preferred_element_type=F32)
    column = lax.broadcasted_iota(jnp.int32, (chans, step), 1) + pl.program_id(0) * step
    for row in range(rows):
        direct = jnp.dot(w_ref[...], gp_ref[row], preferred_element_type=F32)
        value = spatial[row * chans : (row + 1) * chans] + direct
        live = column < ext_ref[0, first + row // SLAB]
        out_ref[0, row] = jnp.where(live, value, 0.0).astype(BF16)


def whole(array):
    return pl.BlockSpec(array.shape, lambda *_: (0,) * array.ndim)


def call(body, args, outs, name, flops, **kw):
    size = sum(a.size * a.dtype.itemsize for a in (*args, *outs))
    return pl.pallas_call(
        body,
        out_shape=outs,
        name=name,
        cost_estimate=pl.CostEstimate(flops=flops, bytes_accessed=size, transcendentals=0),
        compiler_params=pltpu.CompilerParams(vmem_limit_bytes=VMEM_LIMIT),
        **kw,
    )(*args)


def exchange(value):
    return lax.all_to_all(value, "rows", split_axis=0, concat_axis=0, tiled=True)


def every_sample(value, count):
    if count == 1:
        return [value]
    if count == 2:
        return [value, lax.ppermute(value, "batch", [(0, 1), (1, 0)])]
    gathered = lax.all_gather(value, "batch")
    return [gathered[i] for i in range(count)]


def shards(layer_input, pre_activation, cotangent, weight, spectral, slab_ids, extents):
    samples = lax.axis_size("batch")
    _, local_rows, chans, columns = layer_input.shape
    plan = Plan(lax.axis_size("rows"), local_rows, chans, columns, spectral.shape[0])
    ranks, active = plan.ranks, slab_ids.shape[1]
    sds = jax.ShapeDtypeStruct
    smem = pl.BlockSpec(memory_space=pltpu.SMEM)
    table = jnp.asarray(plan.column_table())
    forward_turn, backward_turn = turn_tables(plan, slab_ids[0])

    row_block = pl.BlockSpec((1, 1, chans, columns), lambda r: (0, r, 0, 0))
    spread, share_out = jnp.asarray(plan.spread()), jnp.asarray(plan.share_out())
    lines, wide = ranks * plan.group, 2 * plan.half + plan.both
    grad_pre, sent = call(
        functools.partial(column_kernel, plan),
        (extents, layer_input, pre_activation, cotangent, table, spread, share_out),
        (sds((local_rows, chans, columns), BF16), sds((lines, wide), BF16)),
        "columns",
        2 * local_rows * 2 * chans * columns * 2 * MODES,
        grid=(local_rows,),
        in_specs=[smem, row_block, row_block, row_block, whole(table), whole(spread), whole(share_out)],
        out_specs=(
            pl.BlockSpec((1, chans, columns), lambda r: (r, 0, 0)),
            pl.BlockSpec((lines, wide), lambda r: (0, 0)),
        ),
        scratch_shapes=[
            pltpu.VMEM((2 * chans, columns), BF16),
            pltpu.VMEM((local_rows, 2, ranks, 2 * plan.half), BF16),
            pltpu.VMEM((chans, chans), F32),
        ],
    )
    received = exchange(sent)

    mode_lines = ranks * plan.steps * 8
    sent, weight_share = call(
        functools.partial(row_kernel, plan),
        (forward_turn, received),
        (sds((mode_lines, plan.half), BF16), sds((plan.group, plan.both), F32)),
        "rows",
        2 * forward_turn.size * plan.half,
    )
    modes = exchange(sent)
    shares = every_sample(weight_share, samples)
    if samples > 2:
        shares = [sum(shares[1:], shares[0])]

    chunks = 4 if plan.exact and ranks % 4 == 0 else 1
    owners = ranks // chunks
    if plan.exact:
        held_shape, held_block = (plan.steps, PA), (plan.steps, owners * plan.pairs)
    else:
        held_shape, held_block = (1, plan.held), (1, plan.held)
    held_spec = pl.BlockSpec(
        held_block + (chans, plan.both), lambda n: (0, n if plan.exact else 0, 0, 0)
    )
    mode_block = pl.BlockSpec((owners * plan.steps * 8, plan.half), lambda n: (n, 0))
    mixed = plan.steps * plan.pairs
    back_width = -(-(mixed + 1) // 2) * plan.both
    held = spectral.reshape(held_shape + spectral.shape[1:])
    sent = call(
        functools.partial(mix_kernel, plan, owners, len(shares)),
        (*shares, modes, held),
        (sds((ranks * 8, back_width), BF16),),
        "mix",
        16 * spectral.size,
        grid=(chunks,),
        in_specs=[*(whole(s) for s in shares), mode_block, held_spec],
        out_specs=(pl.BlockSpec((owners * 8, back_width), lambda n: (n, 0)),),
    )[0]
    returned = exchange(sent)

    every = every_sample(modes, samples)
    grad_spectral = call(
        functools.partial(outer_kernel, plan, owners, samples),
        tuple(every),
        (sds(held_shape + spectral.shape[1:], F32),),
        "outer",
        16 * samples * spectral.size,
        grid=(chunks,),
        in_specs=[mode_block] * samples,
        out_specs=(held_spec,),
    )[0].reshape(spectral.shape)

    weight_scale = 1.0 / math.sqrt(samples * active * SLAB * columns)
    share_in = jnp.asarray(plan.share_in())
    sent, grad_weight = call(
        functools.partial(adjoint_kernel, plan, weight_scale),
        (backward_turn, returned, share_in),
        (sds((lines, plan.half), BF16), sds((chans, chans), F32)),
        "adjoint",
        2 * backward_turn.size * plan.pairs * chans,
    )
    local_back = exchange(sent)

    step = 512
    gather_back = jnp.asarray(plan.gather_back())
    grad_input = call(
        functools.partial(spatial_kernel, plan, step),
        (extents, local_back, gather_back, weight, table, grad_pre),
        (sds(layer_input.shape, BF16),),
        "spatial",
        2 * local_rows * chans * columns * (table.shape[0] + chans),
        grid=(columns // step,),
        in_specs=[
            smem,
            whole(local_back),
            whole(gather_back),
            whole(weight),
            pl.BlockSpec((table.shape[0], step), lambda n: (0, n)),
            pl.BlockSpec((local_rows, chans, step), lambda n: (0, 0, n)),
        ],
        out_specs=(pl.BlockSpec((1, local_rows, chans, step), lambda n: (0, 0, 0, n)),),
        scratch_shapes=[pltpu.VMEM((local_rows * chans, table.shape[0]), BF16)],
    )[0]
    return (grad_input, grad_spectral, grad_weight)


def solution(mesh):
    return jax.shard_map(
        shards,
        mesh=mesh,
        in_specs=(
            P("batch", "rows", None, None),
            P("batch", "rows", None, None),
            P("batch", "rows", None, None),
            P(),
            P("rows", None, None),
            P("batch", None),
            P("batch", None),
        ),
        out_specs=(P("batch", "rows", None, None), P("rows", None, None), P()),
        check_vma=False,
    )
```

```python
import functools
import math

import jax
import jax.numpy as jnp
import numpy as np
from jax import lax
from jax.experimental import pallas as pl
from jax.experimental.pallas import tpu as pltpu
from jax.sharding import PartitionSpec as P

PA = 48
SLAB = 2
NR = 4096
MODES = 96
F32 = jnp.float32
BF16 = jnp.bfloat16


class Plan:
    def __init__(self, ranks, local_rows, channels, columns, held):
        self.ranks = ranks
        self.local_rows = local_rows
        self.channels = channels
        self.columns = columns
        self.held = held
        self.pairs = -(-PA // ranks)
        first = [(held * k) // PA for k in range(ranks)]
        last = [(held * (k + 1) - 1) // PA for k in range(ranks)]
        self.first = np.array(first, np.int32)
        self.steps = max(b - a for a, b in zip(first, last)) + 1
        self.exact = held == self.steps * PA and self.pairs * ranks == PA
        self.both = 2 * channels
        self.half = self.pairs * self.both
        self.group = 2 * local_rows
        self.share = channels // ranks
        self.scale = 1.0 / math.sqrt(NR * columns)

    def column_table(self):
        pair, part, odd, owner = np.meshgrid(
            np.arange(self.pairs),
            np.arange(2),
            np.arange(2),
            np.arange(self.ranks),
            indexing="ij",
        )
        freq = 2 * (self.pairs * owner + pair) + odd
        freq, part = freq.reshape(-1, 1), part.reshape(-1, 1)
        phase = (freq * np.arange(self.columns)[None, :]) % self.columns
        angle = 2.0 * math.pi * phase / self.columns
        table = np.where(part == 0, np.cos(angle), -np.sin(angle))
        return np.where(freq < MODES, table, 0.0).astype(np.float32).astype(jnp.bfloat16)

    def spread(self):
        out = np.zeros((self.ranks * self.group, self.group * self.ranks), np.float32)
        for owner in range(self.ranks):
            for e in range(self.group):
                out[owner * self.group + e, e * self.ranks + owner] = 1.0
        return out.astype(jnp.bfloat16)

    def gather_back(self):
        return self.spread().T

    def share_out(self):
        out = np.zeros((self.ranks * self.group, self.channels), np.float32)
        for i in range(self.channels):
            out[(i // self.share) * self.group + i % self.share, i] = 1.0
        return out.astype(jnp.bfloat16)

    def share_in(self):
        out = np.zeros((self.channels, self.ranks * 8), np.float32)
        for i in range(self.channels):
            base = (i // self.share) * 8 + i % self.share
            out[i, base] = 1.0
            out[i, base + self.share] = 1.0
        return out.astype(jnp.bfloat16)


def turn_table(freq, mode_part, mode_odd, positions, row_part, row_odd, mode_major):
    turn = lambda a, b: (a[:, None], b[None, :]) if mode_major else (a[None, :], b[:, None])
    f, pos = turn(jnp.asarray(freq), positions)
    mp, rp = turn(jnp.asarray(mode_part), jnp.asarray(row_part))
    mo, ro = turn(jnp.asarray(mode_odd), jnp.asarray(row_odd))
    phase = jnp.mod(f * pos + (mp - rp) * (NR // 4), NR)
    value = jnp.cos(phase.astype(F32) * (2.0 * math.pi / NR))
    return jnp.where(mo == ro, value, 0.0).astype(BF16)


def turn_tables(plan, slab_list):
    rows = plan.ranks * plan.local_rows
    row_index = np.arange(rows)
    positions = jnp.repeat(slab_list, SLAB) * SLAB + jnp.asarray(row_index % SLAB, jnp.int32)

    def modes(order):
        k, step, part, odd, low = np.meshgrid(
            *(np.arange(n) for n in (plan.ranks, plan.steps, 2, 2, 2)), indexing="ij"
        )
        freq = 2 * (plan.first[k] + step) + low - MODES // 2
        return [x.transpose(order).reshape(-1).astype(np.int32) for x in (freq, part, odd)]

    def rows_side(shape_order):
        odd, row, part = np.meshgrid(np.arange(2), row_index, np.arange(2), indexing="ij")
        odd, part = (x.transpose(shape_order).reshape(-1).astype(np.int32) for x in (odd, part))
        spread = jnp.broadcast_to(positions[None, :, None], (2, rows, 2))
        return spread.transpose(shape_order).reshape(-1), part, odd

    forward = turn_table(*modes((0, 1, 2, 3, 4)), *rows_side((0, 1, 2)), True)
    backward = turn_table(*modes((1, 0, 2, 3, 4)), *rows_side((2, 1, 0)), False)
    return forward, backward


LOG_PEAK = math.log2(0.3989422804014327)
NT = (((1,), (1,)), ((), ()))
TN = (((0,), (0,)), ((), ()))


def mask_rows(extent, start, width, rows):
    column = lax.broadcasted_iota(jnp.int32, (16, width), 1) + start
    few = jnp.where(column < extent, 1.0, 0.0).astype(BF16)
    return jnp.concatenate([few] * (rows // 16), axis=0)


def column_kernel(
    plan, ext_ref, x_hbm, pre_hbm, cot_hbm, tab_hbm, spread_hbm, share_hbm, gp_hbm, out_ref,
    x_ref, pre_ref, cot_ref, lines_ref, spread_ref, share_ref, stage_ref, in_sems, misc_sems,
):
    chans, ranks = plan.channels, plan.ranks
    slots = plan.local_rows // SLAB
    freqs = tab_hbm.shape[0]
    first = lax.axis_index("rows") * slots
    loads, tables, saves = [], [], []
    for slot in range(slots):
        rows = pl.ds(slot * SLAB, SLAB)
        loads.append(
            [
                pltpu.make_async_copy(src.at[0, rows], dst.at[slot], in_sems.at[slot, n])
                for n, (src, dst) in enumerate(
                    ((pre_hbm, pre_ref), (cot_hbm, cot_ref), (x_hbm, x_ref))
                )
            ]
        )
        tables.append(
            pltpu.make_async_copy(tab_hbm, lines_ref.at[slot, pl.ds(0, freqs)], in_sems.at[slot, 3])
        )
        saves.append(
            pltpu.make_async_copy(
                lines_ref.at[slot, pl.ds(freqs + SLAB * chans, SLAB * chans)],
                gp_hbm.at[pl.ds(slot * SLAB * chans, SLAB * chans)],
                in_sems.at[slot, 4],
            )
        )
    small = [
        pltpu.make_async_copy(spread_hbm, spread_ref, misc_sems.at[0]),
        pltpu.make_async_copy(share_hbm, share_ref, misc_sems.at[1]),
    ]
    for slot in range(slots):
        for copy in loads[slot]:
            copy.start()
        tables[slot].start()
    for copy in small:
        copy.start()

    width = 256
    lane = lax.broadcasted_iota(jnp.int32, (freqs, plan.both), 1)
    total = jnp.zeros((chans, chans), F32)
    for slot in range(slots):
        extent = ext_ref[0, first + slot]
        for copy in loads[slot]:
            copy.wait()
        for start in range(0, plan.columns, width):
            cols = slice(start, start + width)
            live = mask_rows(extent, start, width, chans)
            for row in range(SLAB):
                value = pre_ref[slot, row, :, cols].astype(F32)
                turned = value * 0.7071067811865476
                bell = jnp.exp2(turned * turned * -1.4426950408889634 + LOG_PEAK)
                slope = value * bell + (0.5 + 0.5 * lax.erf(turned))
                cot = (cot_ref[slot, row, :, cols] * live).astype(F32)
                base = freqs + row * chans
                lines_ref[slot, base : base + chans, cols] = x_ref[slot, row, :, cols] * live
                base += SLAB * chans
                lines_ref[slot, base : base + chans, cols] = (cot * slope).astype(BF16)
        saves[slot].start()
        tables[slot].wait()
        edge = freqs + SLAB * chans
        sums = lax.dot_general(
            lines_ref[slot, :edge], lines_ref[slot, freqs:], NT, preferred_element_type=F32
        )
        for row in range(SLAB):
            base = freqs + row * chans
            side = SLAB * chans + row * chans
            total = total + sums[base : base + chans, side : side + chans]
        inputs, grads = sums[:freqs, : plan.both], sums[:freqs, plan.both :]
        near = jnp.where(lane < chans, inputs, pltpu.roll(grads, chans, axis=1)).astype(BF16)
        far = jnp.where(lane < chans, pltpu.roll(inputs, chans, axis=1), grads).astype(BF16)
        for row, spec in enumerate((near, far)):
            for pair in range(plan.pairs):
                for part in range(2):
                    for odd in range(2):
                        base = ((pair * 2 + part) * 2 + odd) * ranks
                        lanes = (odd * plan.pairs + pair) * plan.both
                        line = ((slot * SLAB + row) * 2 + part) * ranks
                        stage_ref[line : line + ranks, lanes : lanes + plan.both] = spec[
                            base : base + ranks
                        ]
    for copy in small:
        copy.wait()
    wide = 2 * plan.half
    out_ref[:, :wide] = jnp.dot(
        spread_ref[...], stage_ref[...], preferred_element_type=F32
    ).astype(BF16)
    high = total.astype(BF16)
    low = (total - high.astype(F32)).astype(BF16)
    split = jnp.concatenate([high, low], axis=1)
    out_ref[:, wide:] = jnp.dot(share_ref[...], split, preferred_element_type=F32).astype(BF16)
    for copy in saves:
        copy.wait()


def row_kernel(plan, turn_ref, in_ref, out_ref, share_ref):
    half = plan.half
    stacked = jnp.concatenate([in_ref[:, :half], in_ref[:, half : 2 * half]], axis=0)
    sums = jnp.dot(turn_ref[...], stacked, preferred_element_type=F32)
    out_ref[...] = (sums * plan.scale).astype(BF16)
    pieces = in_ref[:, 2 * half :].astype(F32).reshape(plan.ranks, plan.group, plan.both)
    summed = jnp.sum(pieces, axis=0)
    share_ref[...] = summed + pltpu.roll(summed, plan.channels, axis=1)


def out_pair(tile, chans):
    lane = lax.broadcasted_iota(jnp.int32, tile.shape, 1)
    row = lax.broadcasted_iota(jnp.int32, tile.shape, 0)
    across = pltpu.roll(tile, chans, axis=1)
    other = pltpu.roll(tile, 4, axis=0)
    return jnp.where(lane < chans, across, jnp.where(row < 4, other, -other))


def where_held(plan, owner, step, pair, offset):
    place = step * PA + plan.pairs * owner + pair - offset
    ok = (place >= 0) & (place < plan.held) & (plan.pairs * owner + pair < PA)
    return jnp.clip(place, 0, plan.held - 1), ok


def mode_offset(plan):
    k = lax.axis_index("rows")
    return lax.rem(k * plan.held, PA)


def slot_order(plan):
    order = []
    for step in range(plan.steps):
        order += [(step, pair) for pair in range(plan.pairs - plan.pairs % 2)]
    if plan.pairs % 2:
        order += [(step, plan.pairs - 1) for step in range(plan.steps)]
    return order


def mix_kernel(plan, samples, *refs):
    share_refs, (in_ref, spec_ref, out_hbm, out_ref, sems) = refs[:samples], refs[samples:]
    chans, both = plan.channels, plan.both
    total = share_refs[0][...]
    for ref in share_refs[1:]:
        total = total + ref[...]
    total = total[:8, :]
    high = total.astype(BF16).astype(F32)
    low = pltpu.roll(total - high, plan.share, axis=0)
    row = lax.broadcasted_iota(jnp.int32, total.shape, 0)
    lane = lax.broadcasted_iota(jnp.int32, total.shape, 1)
    zero = jnp.zeros_like(total)
    shared = jnp.where(row < plan.share, high, jnp.where(row < 2 * plan.share, low, zero))
    order = slot_order(plan)

    def one_owner(owner):
        blocks = {}
        for step in range(plan.steps):
            start = (owner * plan.steps + step) * 8
            left = [
                out_pair(in_ref[start : start + 8, p * both : (p + 1) * both].astype(F32), chans)
                for p in range(plan.pairs)
            ]
            if plan.exact:
                base = (step * PA + owner * plan.pairs) * chans
                right = spec_ref[base : base + plan.pairs * chans]
                value = lax.dot_general(
                    jnp.concatenate(left, axis=0).astype(BF16), right, NT,
                    preferred_element_type=F32,
                )
                for p in range(plan.pairs):
                    cols = slice((p // 2) * both, (p // 2) * both + both)
                    piece = value[8 * p : 8 * p + 8]
                    if (p // 2) * both + both > piece.shape[1]:
                        piece = piece[:, (p // 2) * both :]
                        piece = jnp.concatenate([piece, jnp.zeros_like(piece)], axis=1)
                    else:
                        piece = piece[:, cols]
                    blocks[step, p] = (piece, p % 2)
            else:
                for p in range(plan.pairs):
                    place, ok = where_held(plan, owner, step, p, mode_offset(plan))
                    right = spec_ref[pl.ds(pl.multiple_of(place * chans, chans), chans)]
                    piece = lax.dot_general(
                        left[p].astype(BF16), right, NT, preferred_element_type=F32
                    )
                    piece = jnp.where(ok, piece, 0.0)
                    blocks[step, p] = (jnp.concatenate([piece, piece], axis=1), 0)
        places = [blocks[key] for key in order]
        while len(places) % 2 == 0:
            places.append((zero, 0))
        places.append((shared, 0))

        def at(block, side):
            value, held = block
            return value if held == side else pltpu.roll(value, chans, axis=1)

        tiles = [
            jnp.where(lane < chans, at(places[n], 0), at(places[n + 1], 1))
            for n in range(0, len(places), 2)
        ]
        out_ref[owner * 8 : owner * 8 + 8, :] = jnp.concatenate(tiles, axis=1).astype(BF16)

    chunks = sems.shape[0]
    each = plan.ranks // chunks
    copies = []
    for chunk in range(chunks):
        for owner in range(chunk * each, (chunk + 1) * each):
            one_owner(owner)
        lines = pl.ds(chunk * each * 8, each * 8)
        copy = pltpu.make_async_copy(out_ref.at[lines], out_hbm.at[lines], sems.at[chunk])
        copy.start()
        copies.append(copy)
    for copy in copies:
        copy.wait()


def outer_kernel(plan, owners, samples, *refs):
    in_refs, out_ref = refs[:samples], refs[samples]
    chans = plan.channels
    swap = lax.axis_index("batch") != 0

    def body(local, carry):
        owner = pl.program_id(0) * owners + local
        for step in range(plan.steps):
            for pair in range(plan.pairs):
                start = pl.multiple_of(local * (8 * plan.steps) + 8 * step, 8)
                cols = slice(pair * plan.both, (pair + 1) * plan.both)
                tiles = [ref[pl.ds(start, 8), cols].astype(F32) for ref in in_refs]
                if samples == 2:
                    tiles = [
                        jnp.where(swap, tiles[1], tiles[0]),
                        jnp.where(swap, tiles[0], tiles[1]),
                    ]
                left = jnp.concatenate([t[:, :chans] for t in tiles], axis=0).astype(BF16)
                right = jnp.concatenate([out_pair(t, chans) for t in tiles], axis=0).astype(BF16)
                value = lax.dot_general(left, right, TN, preferred_element_type=F32)
                if plan.exact:
                    out_ref[step, local * plan.pairs + pair] = value
                else:
                    place, ok = where_held(plan, owner, step, pair, mode_offset(plan))

                    @pl.when(ok)
                    def _():
                        out_ref[0, place] = value
        return carry

    lax.fori_loop(0, owners, body, 0)


def adjoint_kernel(plan, weight_scale, turn_ref, in_ref, share_ref, out_ref, gw_ref):
    chans = plan.channels
    order = slot_order(plan)
    parts = []
    for step in range(plan.steps):
        places = [order.index((step, pair)) for pair in range(plan.pairs)]
        parts.append(
            jnp.concatenate([in_ref[:, n * chans : (n + 1) * chans] for n in places], axis=1)
        )
    sums = jnp.dot(turn_ref[...], jnp.concatenate(parts, axis=0), preferred_element_type=F32)
    sums = sums * plan.scale
    real, imag = sums[: sums.shape[0] // 2], sums[sums.shape[0] // 2 :]
    pieces = []
    for pair in range(plan.pairs):
        cols = slice(pair * chans, (pair + 1) * chans)
        pieces += [real[:, cols], imag[:, cols]]
    out_ref[...] = jnp.concatenate(pieces, axis=1).astype(BF16)
    shared = in_ref[:, in_ref.shape[1] - chans :]
    total = jnp.dot(share_ref[...], shared, preferred_element_type=F32)
    gw_ref[...] = total * weight_scale


def spatial_kernel(
    plan, step, ext_ref, in_ref, back_ref, w_ref, tab_ref, gp_ref, out_hbm, left_ref, out_ref, sems
):
    chans, rows = plan.channels, plan.local_rows
    block = 2 * plan.ranks
    slots = rows // SLAB
    first = lax.axis_index("rows") * slots
    ordered = jnp.dot(back_ref[...], in_ref[...], preferred_element_type=F32)
    for row in range(rows):
        lines = ordered[row * block : (row + 1) * block]
        pieces = [lines[:, b * chans : (b + 1) * chans] for b in range(2 * plan.pairs)]
        stacked = jnp.concatenate(pieces, axis=0)
        left_ref[row * chans : (row + 1) * chans] = stacked.T.astype(BF16)
    copies = []
    for n in range(plan.columns // step):
        cols = slice(n * step, (n + 1) * step)
        spatial = jnp.dot(left_ref[...], tab_ref[:, cols], preferred_element_type=F32)
        for slot in range(slots):
            live = mask_rows(ext_ref[0, first + slot], n * step, step, chans)
            for row in range(slot * SLAB, (slot + 1) * SLAB):
                lines = slice(row * chans, (row + 1) * chans)
                direct = jnp.dot(w_ref[...], gp_ref[lines, cols], preferred_element_type=F32)
                out_ref[row, :, cols] = (spatial[lines] + direct).astype(BF16) * live
        copy = pltpu.make_async_copy(
            out_ref.at[:, :, pl.ds(n * step, step)],
            out_hbm.at[0, :, :, pl.ds(n * step, step)],
            sems.at[n],
        )
        copy.start()
        copies.append(copy)
    for copy in copies:
        copy.wait()


def whole(array):
    return pl.BlockSpec(array.shape, lambda *_: (0,) * array.ndim)


def call(body, args, outs, name, flops, mib, **kw):
    size = sum(a.size * a.dtype.itemsize for a in (*args, *outs))
    return pl.pallas_call(
        body,
        out_shape=outs,
        name=name,
        cost_estimate=pl.CostEstimate(flops=flops, bytes_accessed=size, transcendentals=0),
        compiler_params=pltpu.CompilerParams(vmem_limit_bytes=mib * 1024 * 1024),
        **kw,
    )(*args)


def exchange(value):
    return lax.all_to_all(value, "rows", split_axis=0, concat_axis=0, tiled=True)


def every_sample(value, count):
    if count == 1:
        return [value]
    if count == 2:
        return [value, lax.ppermute(value, "batch", [(0, 1), (1, 0)])]
    gathered = lax.all_gather(value, "batch")
    return [gathered[i] for i in range(count)]


def shards(layer_input, pre_activation, cotangent, weight, spectral, slab_ids, extents):
    samples = lax.axis_size("batch")
    _, local_rows, chans, columns = layer_input.shape
    plan = Plan(lax.axis_size("rows"), local_rows, chans, columns, spectral.shape[0])
    ranks, active = plan.ranks, slab_ids.shape[1]
    sds = jax.ShapeDtypeStruct
    smem = pl.BlockSpec(memory_space=pltpu.SMEM)
    table = jnp.asarray(plan.column_table())
    forward_turn, backward_turn = turn_tables(plan, slab_ids[0])

    spread, share_out = jnp.asarray(plan.spread()), jnp.asarray(plan.share_out())
    lines, wide = ranks * plan.group, 2 * plan.half + plan.both
    slots = local_rows // SLAB
    freqs = table.shape[0]
    hbm = pl.BlockSpec(memory_space=pltpu.HBM)
    vmem = pl.BlockSpec(memory_space=pltpu.VMEM)
    stored = (slots, SLAB, chans, columns)
    grad_pre, sent = call(
        functools.partial(column_kernel, plan),
        (extents, layer_input, pre_activation, cotangent, table, spread, share_out),
        (sds((local_rows * chans, columns), BF16), sds((lines, wide), BF16)),
        "columns",
        2 * local_rows * 2 * chans * columns * 2 * MODES,
        62,
        in_specs=[smem] + [hbm] * 6,
        out_specs=(hbm, vmem),
        scratch_shapes=[
            pltpu.VMEM(stored, BF16),
            pltpu.VMEM(stored, BF16),
            pltpu.VMEM(stored, BF16),
            pltpu.VMEM((slots, freqs + 2 * SLAB * chans, columns), BF16),
            pltpu.VMEM(spread.shape, BF16),
            pltpu.VMEM(share_out.shape, BF16),
            pltpu.VMEM((plan.group * ranks, 2 * plan.half), BF16),
            pltpu.SemaphoreType.DMA((slots, 5)),
            pltpu.SemaphoreType.DMA((2,)),
        ],
    )
    received = exchange(sent)

    mode_lines = ranks * plan.steps * 8
    sent, weight_share = call(
        functools.partial(row_kernel, plan),
        (forward_turn, received),
        (sds((mode_lines, plan.half), BF16), sds((plan.group, plan.both), F32)),
        "rows",
        2 * forward_turn.size * plan.half,
        16,
    )
    modes = exchange(sent)
    shares = every_sample(weight_share, samples)
    if samples > 2:
        shares = [sum(shares[1:], shares[0])]

    chunks = 4 if plan.exact and ranks % 4 == 0 else 1
    owners = ranks // chunks
    if plan.exact:
        held_shape, held_block = (plan.steps, PA), (plan.steps, owners * plan.pairs)
    else:
        held_shape, held_block = (1, plan.held), (1, plan.held)
    held_spec = pl.BlockSpec(
        held_block + (chans, plan.both), lambda n: (0, n if plan.exact else 0, 0, 0)
    )
    mode_block = pl.BlockSpec((owners * plan.steps * 8, plan.half), lambda n: (n, 0))
    mixed = plan.steps * plan.pairs
    back_width = -(-(mixed + 1) // 2) * plan.both
    sent = call(
        functools.partial(mix_kernel, plan, len(shares)),
        (*shares, modes, spectral.reshape(-1, plan.both)),
        (sds((ranks * 8, back_width), BF16),),
        "mix",
        16 * spectral.size,
        16,
        in_specs=[vmem] * (len(shares) + 2),
        out_specs=(hbm,),
        scratch_shapes=[pltpu.VMEM((ranks * 8, back_width), BF16)]
        + [pltpu.SemaphoreType.DMA((chunks,))],
    )[0]
    returned = exchange(sent)

    every = every_sample(modes, samples)
    grad_spectral = call(
        functools.partial(outer_kernel, plan, owners, samples),
        tuple(every),
        (sds(held_shape + spectral.shape[1:], F32),),
        "outer",
        16 * samples * spectral.size,
        16,
        grid=(chunks,),
        in_specs=[mode_block] * samples,
        out_specs=(held_spec,),
    )[0].reshape(spectral.shape)

    weight_scale = 1.0 / math.sqrt(samples * active * SLAB * columns)
    share_in = jnp.asarray(plan.share_in())
    sent, grad_weight = call(
        functools.partial(adjoint_kernel, plan, weight_scale),
        (backward_turn, returned, share_in),
        (sds((lines, plan.half), BF16), sds((chans, chans), F32)),
        "adjoint",
        2 * backward_turn.size * plan.pairs * chans,
        16,
    )
    local_back = exchange(sent)

    step = 512
    gather_back = jnp.asarray(plan.gather_back())
    grad_input = call(
        functools.partial(spatial_kernel, plan, step),
        (extents, local_back, gather_back, weight, table, grad_pre),
        (sds(layer_input.shape, BF16),),
        "spatial",
        2 * local_rows * chans * columns * (table.shape[0] + chans),
        16,
        in_specs=[smem] + [vmem] * 5,
        out_specs=(hbm,),
        scratch_shapes=[
            pltpu.VMEM((local_rows * chans, table.shape[0]), BF16),
            pltpu.VMEM((local_rows, chans, columns), BF16),
            pltpu.SemaphoreType.DMA((columns // step,)),
        ],
    )[0]
    return (grad_input, grad_spectral, grad_weight)


def solution(mesh):
    return jax.shard_map(
        shards,
        mesh=mesh,
        in_specs=(
            P("batch", "rows", None, None),
            P("batch", "rows", None, None),
            P("batch", "rows", None, None),
            P(),
            P("rows", None, None),
            P("batch", None),
            P("batch", None),
        ),
        out_specs=(P("batch", "rows", None, None), P("rows", None, None), P()),
        check_vma=False,
    )
```

```python
import functools
import math

import jax
import jax.numpy as jnp
import numpy as np
from jax import lax
from jax.experimental import pallas as pl
from jax.experimental.pallas import tpu as pltpu
from jax.sharding import PartitionSpec as P

PA = 48
SLAB = 2
NR = 4096
MODES = 96
F32 = jnp.float32
BF16 = jnp.bfloat16
COLUMN_PARTS = 2


class Plan:
    def __init__(self, ranks, local_rows, channels, columns, held):
        self.ranks = ranks
        self.local_rows = local_rows
        self.channels = channels
        self.columns = columns
        self.held = held
        self.pairs = -(-PA // ranks)
        first = [(held * k) // PA for k in range(ranks)]
        last = [(held * (k + 1) - 1) // PA for k in range(ranks)]
        self.first = np.array(first, np.int32)
        self.steps = max(b - a for a, b in zip(first, last)) + 1
        self.exact = held == self.steps * PA and self.pairs * ranks == PA
        self.both = 2 * channels
        self.half = self.pairs * self.both
        self.group = 2 * local_rows
        self.share = channels // ranks
        self.scale = 1.0 / math.sqrt(NR * columns)

    def column_table(self):
        pair, part, odd, owner = np.meshgrid(
            np.arange(self.pairs),
            np.arange(2),
            np.arange(2),
            np.arange(self.ranks),
            indexing="ij",
        )
        freq = 2 * (self.pairs * owner + pair) + odd
        freq, part = freq.reshape(-1, 1), part.reshape(-1, 1)
        phase = (freq * np.arange(self.columns)[None, :]) % self.columns
        angle = 2.0 * math.pi * phase / self.columns
        table = np.where(part == 0, np.cos(angle), -np.sin(angle))
        return np.where(freq < MODES, table, 0.0).astype(np.float32).astype(jnp.bfloat16)

    def spread(self):
        out = np.zeros((self.ranks * self.group, self.group * self.ranks), np.float32)
        for owner in range(self.ranks):
            for e in range(self.group):
                out[owner * self.group + e, e * self.ranks + owner] = 1.0
        return out.astype(jnp.bfloat16)

    def gather_back(self):
        return self.spread().T

    def share_in(self):
        out = np.zeros((self.channels, self.ranks * 8), np.float32)
        for i in range(self.channels):
            base = (i // self.share) * 8 + i % self.share
            out[i, base] = 1.0
            out[i, base + self.share] = 1.0
        return out.astype(jnp.bfloat16)


def turn_table(freq, mode_part, mode_odd, positions, row_part, row_odd, mode_major):
    turn = lambda a, b: (a[:, None], b[None, :]) if mode_major else (a[None, :], b[:, None])
    f, pos = turn(jnp.asarray(freq), positions)
    mp, rp = turn(jnp.asarray(mode_part), jnp.asarray(row_part))
    mo, ro = turn(jnp.asarray(mode_odd), jnp.asarray(row_odd))
    phase = jnp.mod(f * pos + (mp - rp) * (NR // 4), NR)
    value = jnp.cos(phase.astype(F32) * (2.0 * math.pi / NR))
    return jnp.where(mo == ro, value, 0.0).astype(BF16)


def turn_tables(plan, slab_list):
    rows = plan.ranks * plan.local_rows
    row_index = np.arange(rows)
    positions = jnp.repeat(slab_list, SLAB) * SLAB + jnp.asarray(row_index % SLAB, jnp.int32)

    def modes(order):
        k, step, part, odd, low = np.meshgrid(
            *(np.arange(n) for n in (plan.ranks, plan.steps, 2, 2, 2)), indexing="ij"
        )
        freq = 2 * (plan.first[k] + step) + low - MODES // 2
        return [x.transpose(order).reshape(-1).astype(np.int32) for x in (freq, part, odd)]

    def rows_side(shape_order):
        odd, row, part = np.meshgrid(np.arange(2), row_index, np.arange(2), indexing="ij")
        odd, part = (x.transpose(shape_order).reshape(-1).astype(np.int32) for x in (odd, part))
        spread = jnp.broadcast_to(positions[None, :, None], (2, rows, 2))
        return spread.transpose(shape_order).reshape(-1), part, odd

    forward = turn_table(*modes((0, 1, 2, 3, 4)), *rows_side((0, 1, 2)), True)
    backward = turn_table(*modes((1, 0, 2, 3, 4)), *rows_side((2, 1, 0)), False)
    return forward, backward


LOG_PEAK = math.log2(2.0 * 0.3989422804014327)
NT = (((1,), (1,)), ((), ()))
TN = (((0,), (0,)), ((), ()))


def mask_rows(extent, start, width, rows, value=1.0):
    column = lax.broadcasted_iota(jnp.int32, (16, width), 1) + start
    few = jnp.where(column < extent, value, 0.0).astype(BF16)
    return jnp.concatenate([few] * (rows // 16), axis=0)


def column_kernel(
    plan, ext_hbm, x_hbm, pre_hbm, cot_hbm, tab_hbm, spread_hbm, gp_hbm, out_ref,
    ext_ref, x_ref, pre_ref, cot_ref, lines_ref, tab_ref, spread_ref, stage_ref, in_sems,
    out_sems, misc_sems,
):
    chans, ranks = plan.channels, plan.ranks
    slots = plan.local_rows // SLAB
    freqs = tab_hbm.shape[0]
    side, part_width, width = SLAB * chans, plan.columns // COLUMN_PARTS, 256
    first = lax.axis_index("rows") * slots
    units = [
        (slot, begin) for slot in range(slots) for begin in range(0, plan.columns, part_width)
    ]
    loads = {}
    for slot, begin in units:
        rows, cols = pl.ds(slot * SLAB, SLAB), pl.ds(begin, part_width)
        loads[slot, begin] = [
            pltpu.make_async_copy(
                src.at[0, rows, :, cols],
                dst.at[slot, :, :, cols],
                in_sems.at[slot, begin // part_width, n],
            )
            for n, (src, dst) in enumerate(
                ((pre_hbm, pre_ref), (cot_hbm, cot_ref), (x_hbm, x_ref))
            )
        ]
    table = pltpu.make_async_copy(tab_hbm, tab_ref, misc_sems.at[1])
    saves = [
        pltpu.make_async_copy(
            lines_ref.at[slot, pl.ds(side, side)], gp_hbm.at[pl.ds(slot * side, side)],
            out_sems.at[slot],
        )
        for slot in range(slots)
    ]
    small = pltpu.make_async_copy(spread_hbm, spread_ref, misc_sems.at[0])
    extents = pltpu.make_async_copy(ext_hbm, ext_ref, misc_sems.at[2])
    extents.start()
    for slot, begin in units:
        for copy in loads[slot, begin]:
            copy.start()
        if (slot, begin) == units[COLUMN_PARTS - 1]:
            table.start()
    small.start()
    lane = lax.broadcasted_iota(jnp.int32, (freqs, plan.both), 1)

    def prepare(slot, begin):
        extent = ext_ref[0, first + slot]
        for start in range(begin, begin + part_width, width):
            cols = slice(start, start + width)
            ones = mask_rows(extent, start, width, chans)
            halves = mask_rows(extent, start, width, chans, 0.5)
            for row in range(SLAB):
                value = pre_ref[slot, row, :, cols].astype(F32)
                turned = value * 0.7071067811865476
                bell = jnp.exp2(turned * turned * -1.4426950408889634 + LOG_PEAK)
                slope = value * bell + (1.0 + lax.erf(turned))
                half_cot = (cot_ref[slot, row, :, cols] * halves).astype(F32)
                base = row * chans
                lines_ref[slot, base : base + chans, cols] = x_ref[slot, row, :, cols] * ones
                base += side
                lines_ref[slot, base : base + chans, cols] = (half_cot * slope).astype(BF16)

    def contract(slot):
        return lax.dot_general(
            tab_ref[...], lines_ref[slot], NT, preferred_element_type=F32
        )

    extents.wait()
    sums_of = {}
    for slot in range(slots):
        begins = range(0, plan.columns, part_width)
        if slot == 0:
            for begin in begins:
                for copy in loads[slot, begin]:
                    copy.wait()
                prepare(slot, begin)
            table.wait()
        else:
            for begin in begins:
                for copy in loads[slot, begin]:
                    copy.wait()
            for begin in begins:
                prepare(slot, begin)
            sums_of[slot - 1] = contract(slot - 1)
        saves[slot].start()
    sums_of[slots - 1] = contract(slots - 1)
    for slot in range(slots):
        inputs, grads = sums_of[slot][:, :side], sums_of[slot][:, side:]
        near = jnp.where(lane < chans, inputs, pltpu.roll(grads, chans, axis=1)).astype(BF16)
        far = jnp.where(lane < chans, pltpu.roll(inputs, chans, axis=1), grads).astype(BF16)
        for row, spec in enumerate((near, far)):
            for pair in range(plan.pairs):
                for part in range(2):
                    for odd in range(2):
                        base = ((pair * 2 + part) * 2 + odd) * ranks
                        lanes = (odd * plan.pairs + pair) * plan.both
                        line = ((slot * SLAB + row) * 2 + part) * ranks
                        stage_ref[line : line + ranks, lanes : lanes + plan.both] = spec[
                            base : base + ranks
                        ]
    small.wait()
    out_ref[...] = jnp.dot(spread_ref[...], stage_ref[...], preferred_element_type=F32).astype(BF16)
    for copy in saves:
        copy.wait()


def weight_kernel(x_ref, gp_ref, out_ref):
    part = lax.dot_general(x_ref[0, 0], gp_ref[...], NT, preferred_element_type=F32)

    @pl.when(pl.program_id(0) == 0)
    def _():
        out_ref[...] = part

    @pl.when(pl.program_id(0) > 0)
    def _():
        out_ref[...] += part


def in_two(total):
    high = total.astype(BF16).astype(F32)
    return high, (total - high).astype(BF16).astype(F32)


def row_kernel(plan, turn_ref, in_ref, out_ref):
    half = plan.half
    stacked = jnp.concatenate([in_ref[:, :half], in_ref[:, half:]], axis=0)
    sums = jnp.dot(turn_ref[...], stacked, preferred_element_type=F32)
    out_ref[...] = (sums * plan.scale).astype(BF16)


def out_pair(tile, chans):
    lane = lax.broadcasted_iota(jnp.int32, tile.shape, 1)
    row = lax.broadcasted_iota(jnp.int32, tile.shape, 0)
    across = pltpu.roll(tile, chans, axis=1)
    other = pltpu.roll(tile, 4, axis=0)
    return jnp.where(lane < chans, across, jnp.where(row < 4, other, -other))


def where_held(plan, owner, step, pair, offset):
    place = step * PA + plan.pairs * owner + pair - offset
    ok = (place >= 0) & (place < plan.held) & (plan.pairs * owner + pair < PA)
    return jnp.clip(place, 0, plan.held - 1), ok


def mode_offset(plan):
    k = lax.axis_index("rows")
    return lax.rem(k * plan.held, PA)


def slot_order(plan):
    order = []
    for step in range(plan.steps):
        order += [(step, pair) for pair in range(plan.pairs - plan.pairs % 2)]
    if plan.pairs % 2:
        order += [(step, plan.pairs - 1) for step in range(plan.steps)]
    return order


def mix_kernel(plan, samples, *refs):
    share_refs = refs[:samples]
    in_ref, head_ref, rest_hbm, out_hbm, rest_ref, out_ref, last_ref, sems, spec_sems = refs[samples:]
    chans, both = plan.channels, plan.both
    total = share_refs[0][...]
    for ref in share_refs[1:]:
        total = total + ref[...]
    high, low = in_two(total)
    lane = lax.broadcasted_iota(jnp.int32, (8, both), 1)
    share = plan.share
    order = slot_order(plan)
    head = head_ref.shape[0]

    def left_of(owner, step):
        start = (owner * plan.steps + step) * 8
        tiles = [
            out_pair(in_ref[start : start + 8, p * both : (p + 1) * both].astype(F32), chans)
            for p in range(plan.pairs)
        ]
        return jnp.concatenate(tiles, axis=0).astype(BF16)

    def weights_of(base, count):
        if base + count <= head:
            return head_ref[base : base + count]
        return rest_ref[base - head : base - head + count]

    def put(owner, step, pair, piece):
        value, held = piece
        place = order.index((step, pair))
        if held != place % 2:
            value = pltpu.roll(value, chans, axis=1)
        lanes = slice(place * chans, (place + 1) * chans)
        half = slice((place % 2) * chans, (place % 2 + 1) * chans)
        out_ref[owner * 8 : owner * 8 + 8, lanes] = value[:, half]

    def mix_general(owner):
        for step in range(plan.steps):
            left = left_of(owner, step)
            for p in range(plan.pairs):
                place, ok = where_held(plan, owner, step, p, mode_offset(plan))
                right = head_ref[pl.ds(pl.multiple_of(place * chans, chans), chans)]
                piece = lax.dot_general(
                    left[8 * p : 8 * p + 8], right, NT, preferred_element_type=F32
                )
                piece = jnp.where(ok, piece, 0.0)
                put(owner, step, p, (jnp.concatenate([piece, piece], axis=1), 0))

    def mix_two(owners, step):
        rows = 8 * plan.pairs
        lefts, rights = [], []
        for m, owner in enumerate(owners):
            left = left_of(owner, step)
            blank = jnp.zeros_like(left)
            lefts.append(
                jnp.concatenate([left if k == m else blank for k in range(len(owners))], axis=1)
            )
            base = (step * PA + owner * plan.pairs) * chans
            rights.append(weights_of(base, plan.pairs * chans))
        values = lax.dot_general(
            jnp.concatenate(lefts, axis=0), jnp.concatenate(rights, axis=1), NT,
            preferred_element_type=F32,
        )
        for m, owner in enumerate(owners):
            for p in range(0, plan.pairs, 2):
                piece = values[m * rows + 8 * p : m * rows + 8 * p + 8, (p // 2) * both :]
                if p + 1 < plan.pairs:
                    after = values[
                        m * rows + 8 * p + 8 : m * rows + 8 * p + 16, (p // 2) * both :
                    ]
                    tile = jnp.where(lane < chans, piece[:, :both], after[:, :both])
                    place = order.index((step, p)) * chans
                    out_ref[owner * 8 : owner * 8 + 8, place : place + both] = tile
                else:
                    single = piece[:, :chans]
                    put(owner, step, p, (jnp.concatenate([single, single], axis=1), 0))

    loads = [
        pltpu.make_async_copy(
            rest_hbm.at[pl.ds(head + n * PA * chans, PA * chans)],
            rest_ref.at[pl.ds(n * PA * chans, PA * chans)],
            spec_sems.at[n],
        )
        for n in range(plan.steps - head // (PA * chans) if plan.exact else 0)
    ]
    for copy in loads:
        copy.start()
    places = out_ref.shape[1] // chans
    for owner in range(plan.ranks):
        lines = slice(owner * 8, owner * 8 + 8)
        if places - 1 > len(order):
            out_ref[lines, len(order) * chans : (places - 1) * chans] = jnp.zeros(
                (8, (places - 1 - len(order)) * chans), F32
            )
        rows = slice(owner * share, (owner + 1) * share)
        pieces = [high[rows], low[rows]]
        if 2 * share < 8:
            pieces.append(jnp.zeros((8 - 2 * share, chans), F32))
        out_ref[lines, (places - 1) * chans :] = jnp.concatenate(pieces, axis=0)
    if plan.exact:
        for step in range(plan.steps):
            if step >= plan.steps - len(loads):
                loads[step - plan.steps + len(loads)].wait()
            for owner in range(0, plan.ranks, 2):
                mix_two(range(owner, min(owner + 2, plan.ranks)), step)
    else:
        for owner in range(plan.ranks):
            mix_general(owner)
    chunks = sems.shape[0]
    each = plan.ranks * 8 // chunks
    saves = []
    for chunk in range(chunks):
        lines = slice(chunk * each, (chunk + 1) * each)
        last_ref[lines] = out_ref[lines].astype(BF16)
        span = pl.ds(chunk * each, each)
        copy = pltpu.make_async_copy(last_ref.at[span], out_hbm.at[span], sems.at[chunk])
        copy.start()
        saves.append(copy)
    for copy in saves:
        copy.wait()


def outer_kernel(plan, owners, samples, *refs):
    in_refs, out_ref = refs[:samples], refs[samples]
    chans = plan.channels
    swap = lax.axis_index("batch") != 0

    def body(local, carry):
        owner = pl.program_id(0) * owners + local
        for step in range(plan.steps):
            for pair in range(plan.pairs):
                start = pl.multiple_of(local * (8 * plan.steps) + 8 * step, 8)
                cols = slice(pair * plan.both, (pair + 1) * plan.both)
                tiles = [ref[pl.ds(start, 8), cols].astype(F32) for ref in in_refs]
                if samples == 2:
                    tiles = [
                        jnp.where(swap, tiles[1], tiles[0]),
                        jnp.where(swap, tiles[0], tiles[1]),
                    ]
                left = jnp.concatenate([t[:, :chans] for t in tiles], axis=0).astype(BF16)
                right = jnp.concatenate([out_pair(t, chans) for t in tiles], axis=0).astype(BF16)
                value = lax.dot_general(left, right, TN, preferred_element_type=F32)
                if plan.exact:
                    out_ref[step, local * plan.pairs + pair] = value
                else:
                    place, ok = where_held(plan, owner, step, pair, mode_offset(plan))

                    @pl.when(ok)
                    def _():
                        out_ref[0, place] = value
        return carry

    lax.fori_loop(0, owners, body, 0)


def adjoint_kernel(plan, turn_ref, in_ref, out_ref):
    chans = plan.channels
    order = slot_order(plan)
    parts = []
    for step in range(plan.steps):
        places = [order.index((step, pair)) for pair in range(plan.pairs)]
        parts.append(
            jnp.concatenate([in_ref[:, n * chans : (n + 1) * chans] for n in places], axis=1)
        )
    sums = jnp.dot(turn_ref[...], jnp.concatenate(parts, axis=0), preferred_element_type=F32)
    sums = sums * plan.scale
    real, imag = sums[: sums.shape[0] // 2], sums[sums.shape[0] // 2 :]
    pieces = []
    for pair in range(plan.pairs):
        cols = slice(pair * chans, (pair + 1) * chans)
        pieces += [real[:, cols], imag[:, cols]]
    out_ref[:, : plan.half] = jnp.concatenate(pieces, axis=1).astype(BF16)
    shared = in_ref[:, in_ref.shape[1] - chans :].astype(F32)
    summed = jnp.sum(shared.reshape(plan.ranks, 8, chans), axis=0)
    share = plan.share
    high, low = in_two(summed[:share] + summed[share : 2 * share])
    pieces = [high, low]
    if 2 * share < 8:
        pieces.append(jnp.zeros((8 - 2 * share, chans), F32))
    block = jnp.concatenate(pieces, axis=0)
    block = jnp.concatenate([block, jnp.zeros((8, plan.both - chans), F32)], axis=1)
    out_ref[:, plan.half :] = jnp.concatenate([block] * plan.ranks, axis=0).astype(BF16)


def spatial_kernel(
    plan, step, weight_scale, ext_hbm, in_ref, back_ref, share_ref, w_ref, tab_ref, gp_ref,
    out_hbm, gw_hbm, ext_ref, left_ref, out_ref, gw_ref, sems, ext_sem, gw_sem,
):
    chans, rows = plan.channels, plan.local_rows
    block = 2 * plan.ranks
    slots = rows // SLAB
    first = lax.axis_index("rows") * slots
    extents = pltpu.make_async_copy(ext_hbm, ext_ref, ext_sem)
    extents.start()
    ordered = jnp.dot(back_ref[...], in_ref[:, : plan.half], preferred_element_type=F32)
    for row in range(rows):
        lines = ordered[row * block : (row + 1) * block]
        pieces = [lines[:, b * chans : (b + 1) * chans] for b in range(2 * plan.pairs)]
        stacked = jnp.concatenate(pieces, axis=0)
        left_ref[row * chans : (row + 1) * chans] = stacked.T.astype(BF16)
    shared = in_ref[:, plan.half : plan.half + chans]
    total = jnp.dot(share_ref[...], shared, preferred_element_type=F32)
    gw_ref[...] = total * weight_scale
    copies = [pltpu.make_async_copy(gw_ref, gw_hbm, gw_sem)]
    copies[0].start()
    extents.wait()
    for n in range(plan.columns // step):
        cols = slice(n * step, (n + 1) * step)
        spatial = jnp.dot(left_ref[...], tab_ref[:, cols], preferred_element_type=F32)
        for slot in range(slots):
            live = mask_rows(ext_ref[0, first + slot], n * step, step, chans)
            for row in range(slot * SLAB, (slot + 1) * SLAB):
                lines = slice(row * chans, (row + 1) * chans)
                direct = jnp.dot(w_ref[...], gp_ref[lines, cols], preferred_element_type=F32)
                out_ref[row, :, cols] = (spatial[lines] + direct).astype(BF16) * live
        copy = pltpu.make_async_copy(
            out_ref.at[:, :, pl.ds(n * step, step)],
            out_hbm.at[0, :, :, pl.ds(n * step, step)],
            sems.at[n],
        )
        copy.start()
        copies.append(copy)
    for copy in copies:
        copy.wait()


def whole(array):
    return pl.BlockSpec(array.shape, lambda *_: (0,) * array.ndim)


def call(body, args, outs, name, flops, mib, **kw):
    size = sum(a.size * a.dtype.itemsize for a in (*args, *outs))
    return pl.pallas_call(
        body,
        out_shape=outs,
        name=name,
        cost_estimate=pl.CostEstimate(flops=flops, bytes_accessed=size, transcendentals=0),
        compiler_params=pltpu.CompilerParams(vmem_limit_bytes=mib * 1024 * 1024),
        **kw,
    )(*args)


def stay(value):
    return pltpu.with_memory_space_constraint(value, pltpu.HBM)


def exchange(value):
    return lax.all_to_all(value, "rows", split_axis=0, concat_axis=0, tiled=True)


def every_sample(value, count):
    if count == 1:
        return [value]
    if count == 2:
        return [value, lax.ppermute(value, "batch", [(0, 1), (1, 0)])]
    gathered = lax.all_gather(value, "batch")
    return [gathered[i] for i in range(count)]


def shards(layer_input, pre_activation, cotangent, weight, spectral, slab_ids, extents):
    samples = lax.axis_size("batch")
    _, local_rows, chans, columns = layer_input.shape
    plan = Plan(lax.axis_size("rows"), local_rows, chans, columns, spectral.shape[0])
    ranks, active = plan.ranks, slab_ids.shape[1]
    sds = jax.ShapeDtypeStruct
    table = jnp.asarray(plan.column_table())
    forward_turn, backward_turn = turn_tables(plan, slab_ids[0])

    spread = jnp.asarray(plan.spread())
    lines, wide = ranks * plan.group, 2 * plan.half
    slots = local_rows // SLAB
    freqs = table.shape[0]
    hbm = pl.BlockSpec(memory_space=pltpu.HBM)
    vmem = pl.BlockSpec(memory_space=pltpu.VMEM)
    stored = (slots, SLAB, chans, columns)
    grad_pre, sent = call(
        functools.partial(column_kernel, plan),
        (extents, layer_input, pre_activation, cotangent, table, spread),
        (sds((local_rows * chans, columns), BF16), sds((lines, wide), BF16)),
        "columns",
        2 * local_rows * 2 * chans * columns * 2 * MODES,
        62,
        in_specs=[hbm] * 6,
        out_specs=(hbm, vmem),
        scratch_shapes=[
            pltpu.SMEM(extents.shape, jnp.int32),
            pltpu.VMEM(stored, BF16),
            pltpu.VMEM(stored, BF16),
            pltpu.VMEM(stored, BF16),
            pltpu.VMEM((slots, 2 * SLAB * chans, columns), BF16),
            pltpu.VMEM(table.shape, BF16),
            pltpu.VMEM(spread.shape, BF16),
            pltpu.VMEM((plan.group * ranks, 2 * plan.half), BF16),
            pltpu.SemaphoreType.DMA((slots, COLUMN_PARTS, 3)),
            pltpu.SemaphoreType.DMA((slots,)),
            pltpu.SemaphoreType.DMA((3,)),
        ],
    )
    received = exchange(sent)
    local_weight = call(
        weight_kernel,
        (stay(layer_input), stay(grad_pre)),
        (sds((chans, chans), F32),),
        "weights",
        2 * layer_input.size * chans,
        16,
        grid=(local_rows,),
        in_specs=[
            pl.BlockSpec((1, 1, chans, columns), lambda r: (0, r, 0, 0)),
            pl.BlockSpec((chans, columns), lambda r: (r, 0)),
        ],
        out_specs=(pl.BlockSpec((chans, chans), lambda r: (0, 0)),),
    )[0]
    shares = every_sample(local_weight, samples)
    if samples > 2:
        shares = [sum(shares[1:], shares[0])]

    mode_lines = ranks * plan.steps * 8
    sent = call(
        functools.partial(row_kernel, plan),
        (forward_turn, received),
        (sds((mode_lines, plan.half), BF16),),
        "rows",
        2 * forward_turn.size * plan.half,
        16,
    )[0]
    modes = exchange(sent)

    chunks = 4 if plan.exact and ranks % 4 == 0 else 1
    owners = ranks // chunks
    if plan.exact:
        held_shape, held_block = (plan.steps, PA), (plan.steps, owners * plan.pairs)
    else:
        held_shape, held_block = (1, plan.held), (1, plan.held)
    held_spec = pl.BlockSpec(
        held_block + (chans, plan.both), lambda n: (0, n if plan.exact else 0, 0, 0)
    )
    mode_block = pl.BlockSpec((owners * plan.steps * 8, plan.half), lambda n: (n, 0))
    mixed = plan.steps * plan.pairs
    back_width = -(-(mixed + 1) // 2) * plan.both
    flat = spectral.reshape(-1, plan.both)
    resident = max(plan.steps - 1, 1)
    head = resident * PA * chans if plan.exact else flat.shape[0]
    sent = call(
        functools.partial(mix_kernel, plan, len(shares)),
        (*shares, modes, flat[:head], stay(flat)),
        (sds((ranks * 8, back_width), BF16),),
        "mix",
        16 * spectral.size,
        16,
        in_specs=[vmem] * (len(shares) + 2) + [hbm],
        out_specs=(hbm,),
        scratch_shapes=[
            pltpu.VMEM((max(flat.shape[0] - head, 8), plan.both), BF16),
            pltpu.VMEM((ranks * 8, back_width), F32),
            pltpu.VMEM((ranks * 8, back_width), BF16),
            pltpu.SemaphoreType.DMA((chunks,)),
            pltpu.SemaphoreType.DMA((plan.steps,)),
        ],
    )[0]
    returned = exchange(sent)

    every = every_sample(modes, samples)
    grad_spectral = call(
        functools.partial(outer_kernel, plan, owners, samples),
        tuple(every),
        (sds(held_shape + spectral.shape[1:], F32),),
        "outer",
        16 * samples * spectral.size,
        16,
        grid=(chunks,),
        in_specs=[mode_block] * samples,
        out_specs=(held_spec,),
    )[0].reshape(spectral.shape)

    weight_scale = 1.0 / math.sqrt(samples * active * SLAB * columns)
    sent = call(
        functools.partial(adjoint_kernel, plan),
        (backward_turn, returned),
        (sds((lines, plan.half + plan.both), BF16),),
        "adjoint",
        2 * backward_turn.size * plan.pairs * chans,
        16,
    )[0]
    local_back = exchange(sent)

    step = 512
    gather_back, share_in = jnp.asarray(plan.gather_back()), jnp.asarray(plan.share_in())
    grad_input, grad_weight = call(
        functools.partial(spatial_kernel, plan, step, weight_scale),
        (extents, local_back, gather_back, share_in, weight, table, grad_pre),
        (sds(layer_input.shape, BF16), sds((chans, chans), F32)),
        "spatial",
        2 * local_rows * chans * columns * (table.shape[0] + chans),
        16,
        in_specs=[hbm] + [vmem] * 6,
        out_specs=(hbm, hbm),
        scratch_shapes=[
            pltpu.SMEM(extents.shape, jnp.int32),
            pltpu.VMEM((local_rows * chans, table.shape[0]), BF16),
            pltpu.VMEM((local_rows, chans, columns), BF16),
            pltpu.VMEM((chans, chans), F32),
            pltpu.SemaphoreType.DMA((columns // step,)),
            pltpu.SemaphoreType.DMA,
            pltpu.SemaphoreType.DMA,
        ],
    )
    return (grad_input, grad_spectral, grad_weight)


def solution(mesh):
    return jax.shard_map(
        shards,
        mesh=mesh,
        in_specs=(
            P("batch", "rows", None, None),
            P("batch", "rows", None, None),
            P("batch", "rows", None, None),
            P(),
            P("rows", None, None),
            P("batch", None),
            P("batch", None),
        ),
        out_specs=(P("batch", "rows", None, None), P("rows", None, None), P()),
        check_vma=False,
    )
```

```python
import functools
import math

import jax
import jax.numpy as jnp
import numpy as np
from jax import lax
from jax.experimental import pallas as pl
from jax.experimental.pallas import tpu as pltpu
from jax.sharding import PartitionSpec as P

PA = 48
SLAB = 2
NR = 4096
MODES = 96
F32 = jnp.float32
BF16 = jnp.bfloat16
COLUMN_PARTS = 2


class Plan:
    def __init__(self, ranks, local_rows, channels, columns, held):
        self.ranks = ranks
        self.local_rows = local_rows
        self.channels = channels
        self.columns = columns
        self.held = held
        self.pairs = -(-PA // ranks)
        first = [(held * k) // PA for k in range(ranks)]
        last = [(held * (k + 1) - 1) // PA for k in range(ranks)]
        self.first = np.array(first, np.int32)
        self.steps = max(b - a for a, b in zip(first, last)) + 1
        self.exact = held == self.steps * PA and self.pairs * ranks == PA
        self.both = 2 * channels
        self.half = self.pairs * self.both
        self.group = 2 * local_rows
        self.share = channels // ranks
        self.scale = 1.0 / math.sqrt(NR * columns)

    def column_table(self):
        pair, part, odd, owner = np.meshgrid(
            np.arange(self.pairs),
            np.arange(2),
            np.arange(2),
            np.arange(self.ranks),
            indexing="ij",
        )
        freq = 2 * (self.pairs * owner + pair) + odd
        freq, part = freq.reshape(-1, 1), part.reshape(-1, 1)
        phase = (freq * np.arange(self.columns)[None, :]) % self.columns
        angle = 2.0 * math.pi * phase / self.columns
        table = np.where(part == 0, np.cos(angle), -np.sin(angle))
        return np.where(freq < MODES, table, 0.0).astype(np.float32).astype(jnp.bfloat16)

    def spread(self):
        out = np.zeros((self.ranks * self.group, self.group * self.ranks), np.float32)
        for owner in range(self.ranks):
            for e in range(self.group):
                out[owner * self.group + e, e * self.ranks + owner] = 1.0
        return out.astype(jnp.bfloat16)

    def gather_back(self):
        return self.spread().T

    def share_in(self):
        out = np.zeros((self.channels, self.ranks * 8), np.float32)
        for i in range(self.channels):
            base = (i // self.share) * 8 + i % self.share
            out[i, base] = 1.0
            out[i, base + self.share] = 1.0
        return out.astype(jnp.bfloat16)


def turn_table(freq, mode_part, mode_odd, positions, row_part, row_odd, mode_major):
    turn = lambda a, b: (a[:, None], b[None, :]) if mode_major else (a[None, :], b[:, None])
    f, pos = turn(jnp.asarray(freq), positions)
    mp, rp = turn(jnp.asarray(mode_part), jnp.asarray(row_part))
    mo, ro = turn(jnp.asarray(mode_odd), jnp.asarray(row_odd))
    phase = jnp.mod(f * pos + (mp - rp) * (NR // 4), NR)
    value = jnp.cos(phase.astype(F32) * (2.0 * math.pi / NR))
    return jnp.where(mo == ro, value, 0.0).astype(BF16)


def turn_tables(plan, slab_list):
    rows = plan.ranks * plan.local_rows
    row_index = np.arange(rows)
    positions = jnp.repeat(slab_list, SLAB) * SLAB + jnp.asarray(row_index % SLAB, jnp.int32)

    def modes(order):
        k, step, part, odd, low = np.meshgrid(
            *(np.arange(n) for n in (plan.ranks, plan.steps, 2, 2, 2)), indexing="ij"
        )
        freq = 2 * (plan.first[k] + step) + low - MODES // 2
        return [x.transpose(order).reshape(-1).astype(np.int32) for x in (freq, part, odd)]

    def rows_side(shape_order):
        odd, row, part = np.meshgrid(np.arange(2), row_index, np.arange(2), indexing="ij")
        odd, part = (x.transpose(shape_order).reshape(-1).astype(np.int32) for x in (odd, part))
        spread = jnp.broadcast_to(positions[None, :, None], (2, rows, 2))
        return spread.transpose(shape_order).reshape(-1), part, odd

    forward = turn_table(*modes((0, 1, 2, 3, 4)), *rows_side((0, 1, 2)), True)
    backward = turn_table(*modes((1, 0, 2, 3, 4)), *rows_side((2, 1, 0)), False)
    return forward, backward


LOG_PEAK = math.log2(2.0 * 0.3989422804014327)
NT = (((1,), (1,)), ((), ()))
TN = (((0,), (0,)), ((), ()))


def mask_rows(extent, start, width, rows):
    column = lax.broadcasted_iota(jnp.int32, (16, width), 1) + start
    few = jnp.where(column < extent, 1.0, 0.0).astype(BF16)
    return jnp.concatenate([few] * (rows // 16), axis=0)


def column_kernel(
    plan, ext_hbm, x_hbm, pre_hbm, cot_hbm, tab_hbm, spread_hbm, gp_hbm, out_ref,
    ext_ref, x_ref, pre_ref, cot_ref, lines_ref, tab_ref, spread_ref, stage_ref, in_sems,
    out_sems, misc_sems,
):
    chans, ranks = plan.channels, plan.ranks
    slots = plan.local_rows // SLAB
    part_width, width = plan.columns // COLUMN_PARTS, 256
    first = lax.axis_index("rows") * slots
    units = [
        (slot, begin) for slot in range(slots) for begin in range(0, plan.columns, part_width)
    ]
    loads = {}
    for slot, begin in units:
        rows, cols = pl.ds(slot * SLAB, SLAB), pl.ds(begin, part_width)
        loads[slot, begin] = [
            pltpu.make_async_copy(
                src.at[0, rows, :, cols],
                dst.at[slot, :, :, cols],
                in_sems.at[slot, begin // part_width, n],
            )
            for n, (src, dst) in enumerate(
                ((pre_hbm, pre_ref), (cot_hbm, cot_ref), (x_hbm, x_ref))
            )
        ]
    table = pltpu.make_async_copy(tab_hbm, tab_ref, misc_sems.at[1])
    saves = [
        [
            pltpu.make_async_copy(
                lines_ref.at[slot, pl.ds(row * plan.both + chans, chans)],
                gp_hbm.at[pl.ds((slot * SLAB + row) * chans, chans)],
                out_sems.at[slot, row],
            )
            for row in range(SLAB)
        ]
        for slot in range(slots)
    ]
    small = pltpu.make_async_copy(spread_hbm, spread_ref, misc_sems.at[0])
    extents = pltpu.make_async_copy(ext_hbm, ext_ref, misc_sems.at[2])
    extents.start()
    for slot, begin in units:
        for copy in loads[slot, begin]:
            copy.start()
        if (slot, begin) == units[COLUMN_PARTS - 1]:
            table.start()
    small.start()

    def prepare(slot, begin):
        extent = ext_ref[0, first + slot]
        for start in range(begin, begin + part_width, width):
            cols = slice(start, start + width)
            ones = mask_rows(extent, start, width, chans)
            halves = ones * BF16(0.5)
            for row in range(SLAB):
                value = pre_ref[slot, row, :, cols].astype(F32)
                turned = value * 0.7071067811865476
                bell = jnp.exp2(turned * turned * -1.4426950408889634 + LOG_PEAK)
                slope = value * bell + (1.0 + lax.erf(turned))
                half_cot = (cot_ref[slot, row, :, cols] * halves).astype(F32)
                base = row * plan.both
                lines_ref[slot, base : base + chans, cols] = x_ref[slot, row, :, cols] * ones
                base += chans
                lines_ref[slot, base : base + chans, cols] = (half_cot * slope).astype(BF16)

    def contract(slot):
        return lax.dot_general(
            tab_ref[...], lines_ref[slot], NT, preferred_element_type=F32
        )

    extents.wait()
    sums_of = {}
    for slot in range(slots):
        begins = range(0, plan.columns, part_width)
        if slot == 0:
            for begin in begins:
                for copy in loads[slot, begin]:
                    copy.wait()
                prepare(slot, begin)
            table.wait()
        else:
            for begin in begins:
                for copy in loads[slot, begin]:
                    copy.wait()
            for begin in begins:
                prepare(slot, begin)
            sums_of[slot - 1] = contract(slot - 1)
        for copy in saves[slot]:
            copy.start()
    sums_of[slots - 1] = contract(slots - 1)
    for slot in range(slots):
        for row in range(SLAB):
            spec = sums_of[slot][:, row * plan.both : (row + 1) * plan.both].astype(BF16)
            for pair in range(plan.pairs):
                for part in range(2):
                    for odd in range(2):
                        base = ((pair * 2 + part) * 2 + odd) * ranks
                        lanes = (odd * plan.pairs + pair) * plan.both
                        line = ((slot * SLAB + row) * 2 + part) * ranks
                        stage_ref[line : line + ranks, lanes : lanes + plan.both] = spec[
                            base : base + ranks
                        ]
    small.wait()
    out_ref[...] = jnp.dot(spread_ref[...], stage_ref[...], preferred_element_type=F32).astype(BF16)
    for copies in saves:
        for copy in copies:
            copy.wait()


def weight_kernel(x_ref, gp_ref, out_ref):
    part = lax.dot_general(x_ref[0, 0], gp_ref[...], NT, preferred_element_type=F32)

    @pl.when(pl.program_id(0) == 0)
    def _():
        out_ref[...] = part

    @pl.when(pl.program_id(0) > 0)
    def _():
        out_ref[...] += part


def in_two(total):
    high = total.astype(BF16).astype(F32)
    return high, (total - high).astype(BF16).astype(F32)


def row_kernel(plan, turn_ref, in_ref, out_ref):
    half = plan.half
    stacked = jnp.concatenate([in_ref[:, :half], in_ref[:, half:]], axis=0)
    sums = jnp.dot(turn_ref[...], stacked, preferred_element_type=F32)
    out_ref[...] = (sums * plan.scale).astype(BF16)


def out_pair(tile, chans):
    lane = lax.broadcasted_iota(jnp.int32, tile.shape, 1)
    row = lax.broadcasted_iota(jnp.int32, tile.shape, 0)
    across = pltpu.roll(tile, chans, axis=1)
    other = pltpu.roll(tile, 4, axis=0)
    return jnp.where(lane < chans, across, jnp.where(row < 4, other, -other))


def where_held(plan, owner, step, pair, offset):
    place = step * PA + plan.pairs * owner + pair - offset
    ok = (place >= 0) & (place < plan.held) & (plan.pairs * owner + pair < PA)
    return jnp.clip(place, 0, plan.held - 1), ok


def mode_offset(plan):
    k = lax.axis_index("rows")
    return lax.rem(k * plan.held, PA)


def slot_order(plan):
    order = []
    for step in range(plan.steps):
        order += [(step, pair) for pair in range(plan.pairs - plan.pairs % 2)]
    if plan.pairs % 2:
        order += [(step, plan.pairs - 1) for step in range(plan.steps)]
    return order


def mix_kernel(plan, samples, *refs):
    share_refs = refs[:samples]
    in_ref, head_ref, rest_hbm, out_hbm, rest_ref, out_ref, last_ref, sems, spec_sem = refs[samples:]
    chans, both = plan.channels, plan.both
    total = share_refs[0][...]
    for ref in share_refs[1:]:
        total = total + ref[...]
    high, low = in_two(total)
    lane = lax.broadcasted_iota(jnp.int32, (8, both), 1)
    share = plan.share
    order = slot_order(plan)
    head = head_ref.shape[0]

    def left_of(owner, step):
        start = (owner * plan.steps + step) * 8
        tiles = [
            out_pair(in_ref[start : start + 8, p * both : (p + 1) * both].astype(F32), chans)
            for p in range(plan.pairs)
        ]
        return jnp.concatenate(tiles, axis=0).astype(BF16)

    def weights_of(base, count):
        if base + count <= head:
            return head_ref[base : base + count]
        return rest_ref[base - head : base - head + count]

    def put(owner, step, pair, piece):
        value, held = piece
        place = order.index((step, pair))
        if held != place % 2:
            value = pltpu.roll(value, chans, axis=1)
        lanes = slice(place * chans, (place + 1) * chans)
        half = slice((place % 2) * chans, (place % 2 + 1) * chans)
        out_ref[owner * 8 : owner * 8 + 8, lanes] = value[:, half]

    def mix_general(owner):
        for step in range(plan.steps):
            left = left_of(owner, step)
            for p in range(plan.pairs):
                place, ok = where_held(plan, owner, step, p, mode_offset(plan))
                right = head_ref[pl.ds(pl.multiple_of(place * chans, chans), chans)]
                piece = lax.dot_general(
                    left[8 * p : 8 * p + 8], right, NT, preferred_element_type=F32
                )
                piece = jnp.where(ok, piece, 0.0)
                put(owner, step, p, (jnp.concatenate([piece, piece], axis=1), 0))

    def mix_two(owners, step):
        rows = 8 * plan.pairs
        lefts, rights = [], []
        for m, owner in enumerate(owners):
            left = left_of(owner, step)
            blank = jnp.zeros_like(left)
            lefts.append(
                jnp.concatenate([left if k == m else blank for k in range(len(owners))], axis=1)
            )
            base = (step * PA + owner * plan.pairs) * chans
            rights.append(weights_of(base, plan.pairs * chans))
        values = lax.dot_general(
            jnp.concatenate(lefts, axis=0), jnp.concatenate(rights, axis=1), NT,
            preferred_element_type=F32,
        )
        for m, owner in enumerate(owners):
            for p in range(0, plan.pairs, 2):
                piece = values[m * rows + 8 * p : m * rows + 8 * p + 8, (p // 2) * both :]
                if p + 1 < plan.pairs:
                    after = values[
                        m * rows + 8 * p + 8 : m * rows + 8 * p + 16, (p // 2) * both :
                    ]
                    tile = jnp.where(lane < chans, piece[:, :both], after[:, :both])
                    place = order.index((step, p)) * chans
                    out_ref[owner * 8 : owner * 8 + 8, place : place + both] = tile
                else:
                    single = piece[:, :chans]
                    put(owner, step, p, (jnp.concatenate([single, single], axis=1), 0))

    rest = plan.steps * PA * chans - head if plan.exact else 0
    if rest:
        load = pltpu.make_async_copy(rest_hbm.at[pl.ds(head, rest)], rest_ref, spec_sem)
        load.start()
    places = out_ref.shape[1] // chans
    for owner in range(plan.ranks):
        lines = slice(owner * 8, owner * 8 + 8)
        if places - 1 > len(order):
            out_ref[lines, len(order) * chans : (places - 1) * chans] = jnp.zeros(
                (8, (places - 1 - len(order)) * chans), F32
            )
        rows = slice(owner * share, (owner + 1) * share)
        pieces = [high[rows], low[rows]]
        if 2 * share < 8:
            pieces.append(jnp.zeros((8 - 2 * share, chans), F32))
        out_ref[lines, (places - 1) * chans :] = jnp.concatenate(pieces, axis=0)
    if plan.exact:
        waited = rest == 0
        for step in range(plan.steps):
            for owner in range(0, plan.ranks, 2):
                owners = range(owner, min(owner + 2, plan.ranks))
                end = (step * PA + (owners[-1] + 1) * plan.pairs) * chans
                if end > head and not waited:
                    load.wait()
                    waited = True
                mix_two(owners, step)
    else:
        for owner in range(plan.ranks):
            mix_general(owner)
    chunks = sems.shape[0]
    each = plan.ranks * 8 // chunks
    saves = []
    for chunk in range(chunks):
        lines = slice(chunk * each, (chunk + 1) * each)
        last_ref[lines] = out_ref[lines].astype(BF16)
        span = pl.ds(chunk * each, each)
        copy = pltpu.make_async_copy(last_ref.at[span], out_hbm.at[span], sems.at[chunk])
        copy.start()
        saves.append(copy)
    for copy in saves:
        copy.wait()


def outer_kernel(plan, owners, samples, *refs):
    in_refs, out_ref = refs[:samples], refs[samples]
    chans = plan.channels
    swap = lax.axis_index("batch") != 0

    def body(local, carry):
        owner = pl.program_id(0) * owners + local
        for step in range(plan.steps):
            for pair in range(plan.pairs):
                start = pl.multiple_of(local * (8 * plan.steps) + 8 * step, 8)
                cols = slice(pair * plan.both, (pair + 1) * plan.both)
                tiles = [ref[pl.ds(start, 8), cols].astype(F32) for ref in in_refs]
                if samples == 2:
                    tiles = [
                        jnp.where(swap, tiles[1], tiles[0]),
                        jnp.where(swap, tiles[0], tiles[1]),
                    ]
                left = jnp.concatenate([t[:, :chans] for t in tiles], axis=0).astype(BF16)
                right = jnp.concatenate([out_pair(t, chans) for t in tiles], axis=0).astype(BF16)
                value = lax.dot_general(left, right, TN, preferred_element_type=F32)
                if plan.exact:
                    out_ref[step, local * plan.pairs + pair] = value
                else:
                    place, ok = where_held(plan, owner, step, pair, mode_offset(plan))

                    @pl.when(ok)
                    def _():
                        out_ref[0, place] = value
        return carry

    lax.fori_loop(0, owners, body, 0)


def adjoint_kernel(plan, turn_ref, in_ref, out_ref):
    chans = plan.channels
    order = slot_order(plan)
    parts = []
    for step in range(plan.steps):
        places = [order.index((step, pair)) for pair in range(plan.pairs)]
        parts.append(
            jnp.concatenate([in_ref[:, n * chans : (n + 1) * chans] for n in places], axis=1)
        )
    sums = jnp.dot(turn_ref[...], jnp.concatenate(parts, axis=0), preferred_element_type=F32)
    sums = sums * plan.scale
    real, imag = sums[: sums.shape[0] // 2], sums[sums.shape[0] // 2 :]
    pieces = []
    for pair in range(plan.pairs):
        cols = slice(pair * chans, (pair + 1) * chans)
        pieces += [real[:, cols], imag[:, cols]]
    out_ref[:, : plan.half] = jnp.concatenate(pieces, axis=1).astype(BF16)
    shared = in_ref[:, in_ref.shape[1] - chans :].astype(F32)
    summed = jnp.sum(shared.reshape(plan.ranks, 8, chans), axis=0)
    share = plan.share
    high, low = in_two(summed[:share] + summed[share : 2 * share])
    pieces = [high, low]
    if 2 * share < 8:
        pieces.append(jnp.zeros((8 - 2 * share, chans), F32))
    block = jnp.concatenate(pieces, axis=0)
    block = jnp.concatenate([block, jnp.zeros((8, plan.both - chans), F32)], axis=1)
    out_ref[:, plan.half :] = jnp.concatenate([block] * plan.ranks, axis=0).astype(BF16)


def spatial_kernel(
    plan, step, weight_scale, ext_hbm, in_ref, back_ref, share_ref, w_ref, tab_ref, gp_ref,
    out_hbm, gw_hbm, ext_ref, left_ref, out_ref, gw_ref, sems, ext_sem, gw_sem,
):
    chans, rows = plan.channels, plan.local_rows
    block = 2 * plan.ranks
    slots = rows // SLAB
    first = lax.axis_index("rows") * slots
    extents = pltpu.make_async_copy(ext_hbm, ext_ref, ext_sem)
    extents.start()
    ordered = jnp.dot(back_ref[...], in_ref[:, : plan.half], preferred_element_type=F32)
    for row in range(rows):
        lines = ordered[row * block : (row + 1) * block]
        pieces = [lines[:, b * chans : (b + 1) * chans] for b in range(2 * plan.pairs)]
        stacked = jnp.concatenate(pieces, axis=0)
        left_ref[row * chans : (row + 1) * chans] = stacked.T.astype(BF16)
    shared = in_ref[:, plan.half : plan.half + chans]
    total = jnp.dot(share_ref[...], shared, preferred_element_type=F32)
    gw_ref[...] = total * weight_scale
    copies = [pltpu.make_async_copy(gw_ref, gw_hbm, gw_sem)]
    copies[0].start()
    extents.wait()
    for n in range(plan.columns // step):
        cols = slice(n * step, (n + 1) * step)
        spatial = jnp.dot(left_ref[...], tab_ref[:, cols], preferred_element_type=F32)
        for slot in range(slots):
            live = mask_rows(ext_ref[0, first + slot], n * step, step, chans)
            for row in range(slot * SLAB, (slot + 1) * SLAB):
                lines = slice(row * chans, (row + 1) * chans)
                direct = jnp.dot(w_ref[...], gp_ref[lines, cols], preferred_element_type=F32)
                out_ref[row, :, cols] = (spatial[lines] + direct).astype(BF16) * live
        copy = pltpu.make_async_copy(
            out_ref.at[:, :, pl.ds(n * step, step)],
            out_hbm.at[0, :, :, pl.ds(n * step, step)],
            sems.at[n],
        )
        copy.start()
        copies.append(copy)
    for copy in copies:
        copy.wait()


def whole(array):
    return pl.BlockSpec(array.shape, lambda *_: (0,) * array.ndim)


def call(body, args, outs, name, flops, mib, **kw):
    size = sum(a.size * a.dtype.itemsize for a in (*args, *outs))
    return pl.pallas_call(
        body,
        out_shape=outs,
        name=name,
        cost_estimate=pl.CostEstimate(flops=flops, bytes_accessed=size, transcendentals=0),
        compiler_params=pltpu.CompilerParams(vmem_limit_bytes=mib * 1024 * 1024),
        **kw,
    )(*args)


def stay(value):
    return pltpu.with_memory_space_constraint(value, pltpu.HBM)


def exchange(value):
    return lax.all_to_all(value, "rows", split_axis=0, concat_axis=0, tiled=True)


def every_sample(value, count):
    if count == 1:
        return [value]
    if count == 2:
        return [value, lax.ppermute(value, "batch", [(0, 1), (1, 0)])]
    gathered = lax.all_gather(value, "batch")
    return [gathered[i] for i in range(count)]


def shards(layer_input, pre_activation, cotangent, weight, spectral, slab_ids, extents):
    samples = lax.axis_size("batch")
    _, local_rows, chans, columns = layer_input.shape
    plan = Plan(lax.axis_size("rows"), local_rows, chans, columns, spectral.shape[0])
    ranks, active = plan.ranks, slab_ids.shape[1]
    sds = jax.ShapeDtypeStruct
    table = jnp.asarray(plan.column_table())
    forward_turn, backward_turn = turn_tables(plan, slab_ids[0])

    spread = jnp.asarray(plan.spread())
    lines, wide = ranks * plan.group, 2 * plan.half
    slots = local_rows // SLAB

    hbm = pl.BlockSpec(memory_space=pltpu.HBM)
    vmem = pl.BlockSpec(memory_space=pltpu.VMEM)
    stored = (slots, SLAB, chans, columns)
    grad_pre, sent = call(
        functools.partial(column_kernel, plan),
        (extents, layer_input, pre_activation, cotangent, table, spread),
        (sds((local_rows * chans, columns), BF16), sds((lines, wide), BF16)),
        "columns",
        2 * local_rows * 2 * chans * columns * 2 * MODES,
        62,
        in_specs=[hbm] * 6,
        out_specs=(hbm, vmem),
        scratch_shapes=[
            pltpu.SMEM(extents.shape, jnp.int32),
            pltpu.VMEM(stored, BF16),
            pltpu.VMEM(stored, BF16),
            pltpu.VMEM(stored, BF16),
            pltpu.VMEM((slots, 2 * SLAB * chans, columns), BF16),
            pltpu.VMEM(table.shape, BF16),
            pltpu.VMEM(spread.shape, BF16),
            pltpu.VMEM((plan.group * ranks, 2 * plan.half), BF16),
            pltpu.SemaphoreType.DMA((slots, COLUMN_PARTS, 3)),
            pltpu.SemaphoreType.DMA((slots, SLAB)),
            pltpu.SemaphoreType.DMA((3,)),
        ],
    )
    received = exchange(sent)
    local_weight = call(
        weight_kernel,
        (stay(layer_input), stay(grad_pre)),
        (sds((chans, chans), F32),),
        "weights",
        2 * layer_input.size * chans,
        16,
        grid=(local_rows,),
        in_specs=[
            pl.BlockSpec((1, 1, chans, columns), lambda r: (0, r, 0, 0)),
            pl.BlockSpec((chans, columns), lambda r: (r, 0)),
        ],
        out_specs=(pl.BlockSpec((chans, chans), lambda r: (0, 0)),),
    )[0]
    received, local_weight = lax.optimization_barrier((received, local_weight))
    shares = every_sample(local_weight, samples)
    if samples > 2:
        shares = [sum(shares[1:], shares[0])]

    mode_lines = ranks * plan.steps * 8
    sent = call(
        functools.partial(row_kernel, plan),
        (forward_turn, received),
        (sds((mode_lines, plan.half), BF16),),
        "rows",
        2 * forward_turn.size * plan.half,
        16,
    )[0]
    modes = exchange(sent)

    chunks = 4 if plan.exact and ranks % 4 == 0 else 1
    owners = ranks // chunks
    if plan.exact:
        held_shape, held_block = (plan.steps, PA), (plan.steps, owners * plan.pairs)
    else:
        held_shape, held_block = (1, plan.held), (1, plan.held)
    held_spec = pl.BlockSpec(
        held_block + (chans, plan.both), lambda n: (0, n if plan.exact else 0, 0, 0)
    )
    mode_block = pl.BlockSpec((owners * plan.steps * 8, plan.half), lambda n: (n, 0))
    mixed = plan.steps * plan.pairs
    back_width = -(-(mixed + 1) // 2) * plan.both
    flat = spectral.reshape(-1, plan.both)
    owners_two = ranks * plan.steps // 2
    head = (5 * owners_two // 3) * plan.pairs * chans if plan.exact else flat.shape[0]
    sent = call(
        functools.partial(mix_kernel, plan, len(shares)),
        (*shares, modes, flat[:head], stay(flat)),
        (sds((ranks * 8, back_width), BF16),),
        "mix",
        16 * spectral.size,
        16,
        in_specs=[vmem] * (len(shares) + 2) + [hbm],
        out_specs=(hbm,),
        scratch_shapes=[
            pltpu.VMEM((max(flat.shape[0] - head, 8), plan.both), BF16),
            pltpu.VMEM((ranks * 8, back_width), F32),
            pltpu.VMEM((ranks * 8, back_width), BF16),
            pltpu.SemaphoreType.DMA((chunks,)),
            pltpu.SemaphoreType.DMA,
        ],
    )[0]
    returned = exchange(sent)

    every = every_sample(modes, samples)
    grad_spectral = call(
        functools.partial(outer_kernel, plan, owners, samples),
        tuple(every),
        (sds(held_shape + spectral.shape[1:], F32),),
        "outer",
        16 * samples * spectral.size,
        16,
        grid=(chunks,),
        in_specs=[mode_block] * samples,
        out_specs=(held_spec,),
    )[0].reshape(spectral.shape)

    weight_scale = 1.0 / math.sqrt(samples * active * SLAB * columns)
    sent = call(
        functools.partial(adjoint_kernel, plan),
        (backward_turn, returned),
        (sds((lines, plan.half + plan.both), BF16),),
        "adjoint",
        2 * backward_turn.size * plan.pairs * chans,
        16,
    )[0]
    local_back = exchange(sent)

    step = 512
    gather_back, share_in = jnp.asarray(plan.gather_back()), jnp.asarray(plan.share_in())
    grad_input, grad_weight = call(
        functools.partial(spatial_kernel, plan, step, weight_scale),
        (extents, local_back, gather_back, share_in, weight, table, grad_pre),
        (sds(layer_input.shape, BF16), sds((chans, chans), F32)),
        "spatial",
        2 * local_rows * chans * columns * (table.shape[0] + chans),
        16,
        in_specs=[hbm] + [vmem] * 6,
        out_specs=(hbm, hbm),
        scratch_shapes=[
            pltpu.SMEM(extents.shape, jnp.int32),
            pltpu.VMEM((local_rows * chans, table.shape[0]), BF16),
            pltpu.VMEM((local_rows, chans, columns), BF16),
            pltpu.VMEM((chans, chans), F32),
            pltpu.SemaphoreType.DMA((columns // step,)),
            pltpu.SemaphoreType.DMA,
            pltpu.SemaphoreType.DMA,
        ],
    )
    return (grad_input, grad_spectral, grad_weight)


def solution(mesh):
    return jax.shard_map(
        shards,
        mesh=mesh,
        in_specs=(
            P("batch", "rows", None, None),
            P("batch", "rows", None, None),
            P("batch", "rows", None, None),
            P(),
            P("rows", None, None),
            P("batch", None),
            P("batch", None),
        ),
        out_specs=(P("batch", "rows", None, None), P("rows", None, None), P()),
        check_vma=False,
    )
```

```python
import functools
import math

import jax
import jax.numpy as jnp
import numpy as np
from jax import lax
from jax.experimental import pallas as pl
from jax.experimental.pallas import tpu as pltpu
from jax.sharding import PartitionSpec as P

PA = 48
SLAB = 2
NR = 4096
MODES = 96
F32 = jnp.float32
BF16 = jnp.bfloat16
COLUMN_PARTS = 2


class Plan:
    def __init__(self, ranks, local_rows, channels, columns, held):
        self.ranks = ranks
        self.local_rows = local_rows
        self.channels = channels
        self.columns = columns
        self.held = held
        self.pairs = -(-PA // ranks)
        first = [(held * k) // PA for k in range(ranks)]
        last = [(held * (k + 1) - 1) // PA for k in range(ranks)]
        self.first = np.array(first, np.int32)
        self.steps = max(b - a for a, b in zip(first, last)) + 1
        self.exact = held == self.steps * PA and self.pairs * ranks == PA
        self.both = 2 * channels
        self.half = self.pairs * self.both
        self.group = 2 * local_rows
        self.share = channels // ranks
        self.scale = 1.0 / math.sqrt(NR * columns)

    def column_table(self):
        pair, part, odd, owner = np.meshgrid(
            np.arange(self.pairs),
            np.arange(2),
            np.arange(2),
            np.arange(self.ranks),
            indexing="ij",
        )
        freq = 2 * (self.pairs * owner + pair) + odd
        freq, part = freq.reshape(-1, 1), part.reshape(-1, 1)
        phase = (freq * np.arange(self.columns)[None, :]) % self.columns
        angle = 2.0 * math.pi * phase / self.columns
        table = np.where(part == 0, np.cos(angle), -np.sin(angle))
        return np.where(freq < MODES, table, 0.0).astype(np.float32).astype(jnp.bfloat16)

    def spread(self):
        out = np.zeros((self.ranks * self.group, self.group * self.ranks), np.float32)
        for owner in range(self.ranks):
            for e in range(self.group):
                out[owner * self.group + e, e * self.ranks + owner] = 1.0
        return out.astype(jnp.bfloat16)

    def gather_back(self):
        return self.spread().T

    def share_in(self):
        out = np.zeros((self.channels, self.ranks * 8), np.float32)
        for i in range(self.channels):
            base = (i // self.share) * 8 + i % self.share
            out[i, base] = 1.0
            out[i, base + self.share] = 1.0
        return out.astype(jnp.bfloat16)


def turn_table(freq, mode_part, mode_odd, positions, row_part, row_odd, mode_major):
    turn = lambda a, b: (a[:, None], b[None, :]) if mode_major else (a[None, :], b[:, None])
    f, pos = turn(jnp.asarray(freq), positions)
    mp, rp = turn(jnp.asarray(mode_part), jnp.asarray(row_part))
    mo, ro = turn(jnp.asarray(mode_odd), jnp.asarray(row_odd))
    phase = jnp.mod(f * pos + (mp - rp) * (NR // 4), NR)
    value = jnp.cos(phase.astype(F32) * (2.0 * math.pi / NR))
    return jnp.where(mo == ro, value, 0.0).astype(BF16)


def turn_tables(plan, slab_list):
    rows = plan.ranks * plan.local_rows
    row_index = np.arange(rows)
    positions = jnp.repeat(slab_list, SLAB) * SLAB + jnp.asarray(row_index % SLAB, jnp.int32)

    def modes(order):
        k, step, part, odd, low = np.meshgrid(
            *(np.arange(n) for n in (plan.ranks, plan.steps, 2, 2, 2)), indexing="ij"
        )
        freq = 2 * (plan.first[k] + step) + low - MODES // 2
        return [x.transpose(order).reshape(-1).astype(np.int32) for x in (freq, part, odd)]

    def rows_side(shape_order):
        odd, row, part = np.meshgrid(np.arange(2), row_index, np.arange(2), indexing="ij")
        odd, part = (x.transpose(shape_order).reshape(-1).astype(np.int32) for x in (odd, part))
        spread = jnp.broadcast_to(positions[None, :, None], (2, rows, 2))
        return spread.transpose(shape_order).reshape(-1), part, odd

    forward = turn_table(*modes((0, 1, 2, 3, 4)), *rows_side((0, 1, 2)), True)
    backward = turn_table(*modes((1, 0, 2, 3, 4)), *rows_side((2, 1, 0)), False)
    return forward, backward


LOG_PEAK = math.log2(2.0 * 0.3989422804014327)
NT = (((1,), (1,)), ((), ()))
TN = (((0,), (0,)), ((), ()))


def mask_rows(extent, start, width, rows):
    column = lax.broadcasted_iota(jnp.int32, (16, width), 1) + start
    few = jnp.where(column < extent, 1.0, 0.0).astype(BF16)
    return jnp.concatenate([few] * (rows // 16), axis=0)


def column_kernel(
    plan, ext_hbm, x_hbm, pre_hbm, cot_hbm, tab_hbm, spread_hbm, gp_hbm, out_ref,
    ext_ref, x_ref, pre_ref, cot_ref, lines_ref, tab_ref, spread_ref, stage_ref, in_sems,
    out_sems, misc_sems,
):
    chans, ranks = plan.channels, plan.ranks
    slots = plan.local_rows // SLAB
    part_width, width = plan.columns // COLUMN_PARTS, 256
    first = lax.axis_index("rows") * slots
    units = [
        (slot, begin) for slot in range(slots) for begin in range(0, plan.columns, part_width)
    ]
    loads = {}
    for slot, begin in units:
        rows, cols = pl.ds(slot * SLAB, SLAB), pl.ds(begin, part_width)
        loads[slot, begin] = [
            pltpu.make_async_copy(
                src.at[0, rows, :, cols],
                dst.at[slot, :, :, cols],
                in_sems.at[slot, begin // part_width, n],
            )
            for n, (src, dst) in enumerate(
                ((pre_hbm, pre_ref), (cot_hbm, cot_ref), (x_hbm, x_ref))
            )
        ]
    table = pltpu.make_async_copy(tab_hbm, tab_ref, misc_sems.at[1])
    saves = [
        [
            pltpu.make_async_copy(
                lines_ref.at[slot, pl.ds(row * plan.both + chans, chans)],
                gp_hbm.at[pl.ds((slot * SLAB + row) * chans, chans)],
                out_sems.at[slot, row],
            )
            for row in range(SLAB)
        ]
        for slot in range(slots)
    ]
    small = pltpu.make_async_copy(spread_hbm, spread_ref, misc_sems.at[0])
    extents = pltpu.make_async_copy(ext_hbm, ext_ref, misc_sems.at[2])
    extents.start()
    for slot, begin in units:
        for copy in loads[slot, begin]:
            copy.start()
        if (slot, begin) == units[COLUMN_PARTS - 1]:
            table.start()
    small.start()

    def prepare(slot, begin):
        extent = ext_ref[0, first + slot]
        for start in range(begin, begin + part_width, width):
            cols = slice(start, start + width)
            ones = mask_rows(extent, start, width, chans)
            halves = ones * BF16(0.5)
            for row in range(SLAB):
                value = pre_ref[slot, row, :, cols].astype(F32)
                turned = value * 0.7071067811865476
                bell = jnp.exp2(turned * turned * -1.4426950408889634 + LOG_PEAK)
                slope = value * bell + (1.0 + lax.erf(turned))
                half_cot = (cot_ref[slot, row, :, cols] * halves).astype(F32)
                base = row * plan.both
                lines_ref[slot, base : base + chans, cols] = x_ref[slot, row, :, cols] * ones
                base += chans
                lines_ref[slot, base : base + chans, cols] = (half_cot * slope).astype(BF16)

    def contract(slot):
        return lax.dot_general(
            tab_ref[...], lines_ref[slot], NT, preferred_element_type=F32
        )

    extents.wait()
    sums_of = {}
    for slot in range(slots):
        begins = range(0, plan.columns, part_width)
        if slot == 0:
            for begin in begins:
                for copy in loads[slot, begin]:
                    copy.wait()
                prepare(slot, begin)
            table.wait()
        else:
            for begin in begins:
                for copy in loads[slot, begin]:
                    copy.wait()
            for begin in begins:
                prepare(slot, begin)
            sums_of[slot - 1] = contract(slot - 1)
        for copy in saves[slot]:
            copy.start()
    sums_of[slots - 1] = contract(slots - 1)
    for slot in range(slots):
        for row in range(SLAB):
            spec = sums_of[slot][:, row * plan.both : (row + 1) * plan.both].astype(BF16)
            for pair in range(plan.pairs):
                for part in range(2):
                    for odd in range(2):
                        base = ((pair * 2 + part) * 2 + odd) * ranks
                        lanes = (odd * plan.pairs + pair) * plan.both
                        line = ((slot * SLAB + row) * 2 + part) * ranks
                        stage_ref[line : line + ranks, lanes : lanes + plan.both] = spec[
                            base : base + ranks
                        ]
    small.wait()
    out_ref[...] = jnp.dot(spread_ref[...], stage_ref[...], preferred_element_type=F32).astype(BF16)
    for copies in saves:
        for copy in copies:
            copy.wait()


def weight_kernel(x_ref, gp_ref, out_ref):
    part = lax.dot_general(x_ref[0, 0], gp_ref[...], NT, preferred_element_type=F32)

    @pl.when(pl.program_id(0) == 0)
    def _():
        out_ref[...] = part

    @pl.when(pl.program_id(0) > 0)
    def _():
        out_ref[...] += part


def in_two(total):
    high = total.astype(BF16).astype(F32)
    return high, (total - high).astype(BF16).astype(F32)


def row_kernel(plan, turn_ref, in_ref, out_ref):
    half = plan.half
    stacked = jnp.concatenate([in_ref[:, :half], in_ref[:, half:]], axis=0)
    sums = jnp.dot(turn_ref[...], stacked, preferred_element_type=F32)
    out_ref[...] = (sums * plan.scale).astype(BF16)


def out_pair(tile, chans):
    lane = lax.broadcasted_iota(jnp.int32, tile.shape, 1)
    row = lax.broadcasted_iota(jnp.int32, tile.shape, 0)
    across = pltpu.roll(tile, chans, axis=1)
    other = pltpu.roll(tile, 4, axis=0)
    return jnp.where(lane < chans, across, jnp.where(row < 4, other, -other))


def where_held(plan, owner, step, pair, offset):
    place = step * PA + plan.pairs * owner + pair - offset
    ok = (place >= 0) & (place < plan.held) & (plan.pairs * owner + pair < PA)
    return jnp.clip(place, 0, plan.held - 1), ok


def mode_offset(plan):
    k = lax.axis_index("rows")
    return lax.rem(k * plan.held, PA)


def slot_order(plan):
    order = []
    for step in range(plan.steps):
        order += [(step, pair) for pair in range(plan.pairs - plan.pairs % 2)]
    if plan.pairs % 2:
        order += [(step, plan.pairs - 1) for step in range(plan.steps)]
    return order


def mix_kernel(plan, samples, *refs):
    share_refs = refs[:samples]
    in_ref, head_ref, rest_hbm, out_hbm, rest_ref, out_ref, sems, spec_sem, order_sem = refs[samples:]
    chans, both, head = plan.channels, plan.both, head_ref.shape[0]
    rest = plan.steps * PA * chans - head if plan.exact else 0
    if rest:
        load = pltpu.make_async_copy(rest_hbm.at[pl.ds(head, rest)], rest_ref, spec_sem)
        load.start()
        pl.semaphore_signal(order_sem, 1)
        pl.semaphore_wait(order_sem, 1)
    total = share_refs[0][...]
    for ref in share_refs[1:]:
        total = total + ref[...]
    high, low = in_two(total)
    lane = lax.broadcasted_iota(jnp.int32, (8, both), 1)
    share = plan.share
    order = slot_order(plan)

    def left_of(owner, step):
        start = (owner * plan.steps + step) * 8
        tiles = [
            out_pair(in_ref[start : start + 8, p * both : (p + 1) * both].astype(F32), chans)
            for p in range(plan.pairs)
        ]
        return jnp.concatenate(tiles, axis=0).astype(BF16)

    def weights_of(base, count):
        if base + count <= head:
            return head_ref[base : base + count]
        return rest_ref[base - head : base - head + count]

    def put(owner, step, pair, piece):
        value, held = piece
        place = order.index((step, pair))
        if held != place % 2:
            value = pltpu.roll(value, chans, axis=1)
        lanes = slice(place * chans, (place + 1) * chans)
        half = slice((place % 2) * chans, (place % 2 + 1) * chans)
        out_ref[owner * 8 : owner * 8 + 8, lanes] = value[:, half].astype(BF16)

    def mix_general(owner):
        for step in range(plan.steps):
            left = left_of(owner, step)
            for p in range(plan.pairs):
                place, ok = where_held(plan, owner, step, p, mode_offset(plan))
                right = head_ref[pl.ds(pl.multiple_of(place * chans, chans), chans)]
                piece = lax.dot_general(
                    left[8 * p : 8 * p + 8], right, NT, preferred_element_type=F32
                )
                piece = jnp.where(ok, piece, 0.0)
                put(owner, step, p, (jnp.concatenate([piece, piece], axis=1), 0))

    def mix_two(owners, step):
        rows = 8 * plan.pairs
        lefts, rights = [], []
        for m, owner in enumerate(owners):
            left = left_of(owner, step)
            blank = jnp.zeros_like(left)
            lefts.append(
                jnp.concatenate([left if k == m else blank for k in range(len(owners))], axis=1)
            )
            base = (step * PA + owner * plan.pairs) * chans
            rights.append(weights_of(base, plan.pairs * chans))
        values = lax.dot_general(
            jnp.concatenate(lefts, axis=0), jnp.concatenate(rights, axis=1), NT,
            preferred_element_type=F32,
        )
        for m, owner in enumerate(owners):
            for p in range(0, plan.pairs, 2):
                piece = values[m * rows + 8 * p : m * rows + 8 * p + 8, (p // 2) * both :]
                if p + 1 < plan.pairs:
                    after = values[
                        m * rows + 8 * p + 8 : m * rows + 8 * p + 16, (p // 2) * both :
                    ]
                    tile = jnp.where(lane < chans, piece[:, :both], after[:, :both])
                    place = order.index((step, p)) * chans
                    out_ref[owner * 8 : owner * 8 + 8, place : place + both] = tile.astype(BF16)
                else:
                    single = piece[:, :chans]
                    put(owner, step, p, (jnp.concatenate([single, single], axis=1), 0))

    places = out_ref.shape[1] // chans
    for owner in range(plan.ranks):
        lines = slice(owner * 8, owner * 8 + 8)
        if places - 1 > len(order):
            out_ref[lines, len(order) * chans : (places - 1) * chans] = jnp.zeros(
                (8, (places - 1 - len(order)) * chans), BF16
            )
        rows = slice(owner * share, (owner + 1) * share)
        pieces = [high[rows], low[rows]]
        if 2 * share < 8:
            pieces.append(jnp.zeros((8 - 2 * share, chans), F32))
        out_ref[lines, (places - 1) * chans :] = jnp.concatenate(pieces, axis=0).astype(BF16)
    if plan.exact:
        waited = rest == 0
        for step in range(plan.steps):
            for owner in range(0, plan.ranks, 2):
                owners = range(owner, min(owner + 2, plan.ranks))
                end = (step * PA + (owners[-1] + 1) * plan.pairs) * chans
                if end > head and not waited:
                    load.wait()
                    waited = True
                mix_two(owners, step)
    else:
        for owner in range(plan.ranks):
            mix_general(owner)
    chunks = sems.shape[0]
    each = plan.ranks * 8 // chunks
    saves = []
    for chunk in range(chunks):
        span = pl.ds(chunk * each, each)
        copy = pltpu.make_async_copy(out_ref.at[span], out_hbm.at[span], sems.at[chunk])
        copy.start()
        saves.append(copy)
    for copy in saves:
        copy.wait()


def outer_kernel(plan, owners, samples, *refs):
    in_refs, out_ref = refs[:samples], refs[samples]
    chans = plan.channels
    swap = lax.axis_index("batch") != 0

    def body(local, carry):
        owner = pl.program_id(0) * owners + local
        for step in range(plan.steps):
            for pair in range(plan.pairs):
                start = pl.multiple_of(local * (8 * plan.steps) + 8 * step, 8)
                cols = slice(pair * plan.both, (pair + 1) * plan.both)
                tiles = [ref[pl.ds(start, 8), cols].astype(F32) for ref in in_refs]
                if samples == 2:
                    tiles = [
                        jnp.where(swap, tiles[1], tiles[0]),
                        jnp.where(swap, tiles[0], tiles[1]),
                    ]
                left = jnp.concatenate([t[:, :chans] for t in tiles], axis=0).astype(BF16)
                right = jnp.concatenate([out_pair(t, chans) for t in tiles], axis=0).astype(BF16)
                value = lax.dot_general(left, right, TN, preferred_element_type=F32)
                if plan.exact:
                    out_ref[step, local * plan.pairs + pair] = value
                else:
                    place, ok = where_held(plan, owner, step, pair, mode_offset(plan))

                    @pl.when(ok)
                    def _():
                        out_ref[0, place] = value
        return carry

    lax.fori_loop(0, owners, body, 0)


def adjoint_kernel(plan, turn_ref, in_ref, out_ref):
    chans = plan.channels
    order = slot_order(plan)
    parts = []
    for step in range(plan.steps):
        places = [order.index((step, pair)) for pair in range(plan.pairs)]
        parts.append(
            jnp.concatenate([in_ref[:, n * chans : (n + 1) * chans] for n in places], axis=1)
        )
    sums = jnp.dot(turn_ref[...], jnp.concatenate(parts, axis=0), preferred_element_type=F32)
    sums = sums * plan.scale
    real, imag = sums[: sums.shape[0] // 2], sums[sums.shape[0] // 2 :]
    pieces = []
    for pair in range(plan.pairs):
        cols = slice(pair * chans, (pair + 1) * chans)
        pieces += [real[:, cols], imag[:, cols]]
    out_ref[:, : plan.half] = jnp.concatenate(pieces, axis=1).astype(BF16)
    shared = in_ref[:, in_ref.shape[1] - chans :].astype(F32)
    summed = jnp.sum(shared.reshape(plan.ranks, 8, chans), axis=0)
    share = plan.share
    high, low = in_two(summed[:share] + summed[share : 2 * share])
    pieces = [high, low]
    if 2 * share < 8:
        pieces.append(jnp.zeros((8 - 2 * share, chans), F32))
    block = jnp.concatenate(pieces, axis=0)
    block = jnp.concatenate([block, jnp.zeros((8, plan.both - chans), F32)], axis=1)
    out_ref[:, plan.half :] = jnp.concatenate([block] * plan.ranks, axis=0).astype(BF16)


def spatial_kernel(
    plan, step, weight_scale, ext_hbm, in_ref, back_ref, share_ref, w_ref, tab_ref, gp_ref,
    out_hbm, gw_hbm, ext_ref, left_ref, out_ref, gw_ref, sems, ext_sem, gw_sem,
):
    chans, rows = plan.channels, plan.local_rows
    block = 2 * plan.ranks
    slots = rows // SLAB
    first = lax.axis_index("rows") * slots
    extents = pltpu.make_async_copy(ext_hbm, ext_ref, ext_sem)
    extents.start()
    ordered = jnp.dot(back_ref[...], in_ref[:, : plan.half], preferred_element_type=F32)
    for row in range(rows):
        lines = ordered[row * block : (row + 1) * block]
        pieces = [lines[:, b * chans : (b + 1) * chans] for b in range(2 * plan.pairs)]
        stacked = jnp.concatenate(pieces, axis=0)
        left_ref[row * chans : (row + 1) * chans] = stacked.T.astype(BF16)
    shared = in_ref[:, plan.half : plan.half + chans]
    total = jnp.dot(share_ref[...], shared, preferred_element_type=F32)
    gw_ref[...] = total * weight_scale
    copies = [pltpu.make_async_copy(gw_ref, gw_hbm, gw_sem)]
    copies[0].start()
    extents.wait()
    for n in range(plan.columns // step):
        cols = slice(n * step, (n + 1) * step)
        spatial = jnp.dot(left_ref[...], tab_ref[:, cols], preferred_element_type=F32)
        for slot in range(slots):
            live = mask_rows(ext_ref[0, first + slot], n * step, step, chans)
            for row in range(slot * SLAB, (slot + 1) * SLAB):
                lines = slice(row * chans, (row + 1) * chans)
                direct = jnp.dot(w_ref[...], gp_ref[lines, cols], preferred_element_type=F32)
                out_ref[row, :, cols] = (spatial[lines] + direct).astype(BF16) * live
        copy = pltpu.make_async_copy(
            out_ref.at[:, :, pl.ds(n * step, step)],
            out_hbm.at[0, :, :, pl.ds(n * step, step)],
            sems.at[n],
        )
        copy.start()
        copies.append(copy)
    for copy in copies:
        copy.wait()


def whole(array):
    return pl.BlockSpec(array.shape, lambda *_: (0,) * array.ndim)


def call(body, args, outs, name, flops, mib, **kw):
    size = sum(a.size * a.dtype.itemsize for a in (*args, *outs))
    return pl.pallas_call(
        body,
        out_shape=outs,
        name=name,
        cost_estimate=pl.CostEstimate(flops=flops, bytes_accessed=size, transcendentals=0),
        compiler_params=pltpu.CompilerParams(vmem_limit_bytes=mib * 1024 * 1024),
        **kw,
    )(*args)


def stay(value):
    return pltpu.with_memory_space_constraint(value, pltpu.HBM)


def exchange(value):
    return lax.all_to_all(value, "rows", split_axis=0, concat_axis=0, tiled=True)


def every_sample(value, count):
    if count == 1:
        return [value]
    if count == 2:
        return [value, lax.ppermute(value, "batch", [(0, 1), (1, 0)])]
    gathered = lax.all_gather(value, "batch")
    return [gathered[i] for i in range(count)]


def shards(layer_input, pre_activation, cotangent, weight, spectral, slab_ids, extents):
    samples = lax.axis_size("batch")
    _, local_rows, chans, columns = layer_input.shape
    plan = Plan(lax.axis_size("rows"), local_rows, chans, columns, spectral.shape[0])
    ranks, active = plan.ranks, slab_ids.shape[1]
    sds = jax.ShapeDtypeStruct
    table = jnp.asarray(plan.column_table())
    forward_turn, backward_turn = turn_tables(plan, slab_ids[0])

    spread = jnp.asarray(plan.spread())
    lines, wide = ranks * plan.group, 2 * plan.half
    slots = local_rows // SLAB

    hbm = pl.BlockSpec(memory_space=pltpu.HBM)
    vmem = pl.BlockSpec(memory_space=pltpu.VMEM)
    stored = (slots, SLAB, chans, columns)
    grad_pre, sent = call(
        functools.partial(column_kernel, plan),
        (extents, layer_input, pre_activation, cotangent, table, spread),
        (sds((local_rows * chans, columns), BF16), sds((lines, wide), BF16)),
        "columns",
        2 * local_rows * 2 * chans * columns * 2 * MODES,
        62,
        in_specs=[hbm] * 6,
        out_specs=(hbm, vmem),
        scratch_shapes=[
            pltpu.SMEM(extents.shape, jnp.int32),
            pltpu.VMEM(stored, BF16),
            pltpu.VMEM(stored, BF16),
            pltpu.VMEM(stored, BF16),
            pltpu.VMEM((slots, 2 * SLAB * chans, columns), BF16),
            pltpu.VMEM(table.shape, BF16),
            pltpu.VMEM(spread.shape, BF16),
            pltpu.VMEM((plan.group * ranks, 2 * plan.half), BF16),
            pltpu.SemaphoreType.DMA((slots, COLUMN_PARTS, 3)),
            pltpu.SemaphoreType.DMA((slots, SLAB)),
            pltpu.SemaphoreType.DMA((3,)),
        ],
    )
    received = exchange(sent)
    local_weight = call(
        weight_kernel,
        (stay(layer_input), stay(grad_pre)),
        (sds((chans, chans), F32),),
        "weights",
        2 * layer_input.size * chans,
        16,
        grid=(local_rows,),
        in_specs=[
            pl.BlockSpec((1, 1, chans, columns), lambda r: (0, r, 0, 0)),
            pl.BlockSpec((chans, columns), lambda r: (r, 0)),
        ],
        out_specs=(pl.BlockSpec((chans, chans), lambda r: (0, 0)),),
    )[0]
    received, local_weight = lax.optimization_barrier((received, local_weight))
    shares = every_sample(local_weight, samples)
    if samples > 2:
        shares = [sum(shares[1:], shares[0])]

    mode_lines = ranks * plan.steps * 8
    sent = call(
        functools.partial(row_kernel, plan),
        (forward_turn, received),
        (sds((mode_lines, plan.half), BF16),),
        "rows",
        2 * forward_turn.size * plan.half,
        16,
    )[0]
    modes = exchange(sent)

    chunks = 4 if plan.exact and ranks % 4 == 0 else 1
    owners = ranks // chunks
    if plan.exact:
        held_shape, held_block = (plan.steps, PA), (plan.steps, owners * plan.pairs)
    else:
        held_shape, held_block = (1, plan.held), (1, plan.held)
    held_spec = pl.BlockSpec(
        held_block + (chans, plan.both), lambda n: (0, n if plan.exact else 0, 0, 0)
    )
    mode_block = pl.BlockSpec((owners * plan.steps * 8, plan.half), lambda n: (n, 0))
    mixed = plan.steps * plan.pairs
    back_width = -(-(mixed + 1) // 2) * plan.both
    flat = spectral.reshape(-1, plan.both)
    owners_two = ranks * plan.steps // 2
    head = (5 * owners_two // 3) * plan.pairs * chans if plan.exact else flat.shape[0]
    sent = call(
        functools.partial(mix_kernel, plan, len(shares)),
        (*shares, modes, flat[:head], stay(flat)),
        (sds((ranks * 8, back_width), BF16),),
        "mix",
        16 * spectral.size,
        16,
        in_specs=[vmem] * (len(shares) + 2) + [hbm],
        out_specs=(hbm,),
        scratch_shapes=[
            pltpu.VMEM((max(flat.shape[0] - head, 8), plan.both), BF16),
            pltpu.VMEM((ranks * 8, back_width), BF16),
            pltpu.SemaphoreType.DMA((chunks,)),
            pltpu.SemaphoreType.DMA,
            pltpu.SemaphoreType.REGULAR,
        ],
    )[0]
    returned = exchange(sent)

    every = every_sample(modes, samples)
    grad_spectral = call(
        functools.partial(outer_kernel, plan, owners, samples),
        tuple(every),
        (sds(held_shape + spectral.shape[1:], F32),),
        "outer",
        16 * samples * spectral.size,
        16,
        grid=(chunks,),
        in_specs=[mode_block] * samples,
        out_specs=(held_spec,),
    )[0].reshape(spectral.shape)

    weight_scale = 1.0 / math.sqrt(samples * active * SLAB * columns)
    sent = call(
        functools.partial(adjoint_kernel, plan),
        (backward_turn, returned),
        (sds((lines, plan.half + plan.both), BF16),),
        "adjoint",
        2 * backward_turn.size * plan.pairs * chans,
        16,
    )[0]
    local_back = exchange(sent)

    step = 512
    gather_back, share_in = jnp.asarray(plan.gather_back()), jnp.asarray(plan.share_in())
    grad_input, grad_weight = call(
        functools.partial(spatial_kernel, plan, step, weight_scale),
        (extents, local_back, gather_back, share_in, weight, table, grad_pre),
        (sds(layer_input.shape, BF16), sds((chans, chans), F32)),
        "spatial",
        2 * local_rows * chans * columns * (table.shape[0] + chans),
        16,
        in_specs=[hbm] + [vmem] * 6,
        out_specs=(hbm, hbm),
        scratch_shapes=[
            pltpu.SMEM(extents.shape, jnp.int32),
            pltpu.VMEM((local_rows * chans, table.shape[0]), BF16),
            pltpu.VMEM((local_rows, chans, columns), BF16),
            pltpu.VMEM((chans, chans), F32),
            pltpu.SemaphoreType.DMA((columns // step,)),
            pltpu.SemaphoreType.DMA,
            pltpu.SemaphoreType.DMA,
        ],
    )
    return (grad_input, grad_spectral, grad_weight)


def solution(mesh):
    return jax.shard_map(
        shards,
        mesh=mesh,
        in_specs=(
            P("batch", "rows", None, None),
            P("batch", "rows", None, None),
            P("batch", "rows", None, None),
            P(),
            P("rows", None, None),
            P("batch", None),
            P("batch", None),
        ),
        out_specs=(P("batch", "rows", None, None), P("rows", None, None), P()),
        check_vma=False,
    )
```

```python
import functools
import math

import jax
import jax.numpy as jnp
import numpy as np
from jax import lax
from jax.experimental import pallas as pl
from jax.experimental.pallas import tpu as pltpu
from jax.sharding import PartitionSpec as P

PA = 48
SLAB = 2
NR = 4096
MODES = 96
F32 = jnp.float32
BF16 = jnp.bfloat16
COLUMN_PARTS = 2


class Plan:
    def __init__(self, ranks, local_rows, channels, columns, held):
        self.ranks = ranks
        self.local_rows = local_rows
        self.channels = channels
        self.columns = columns
        self.held = held
        self.pairs = -(-PA // ranks)
        first = [(held * k) // PA for k in range(ranks)]
        last = [(held * (k + 1) - 1) // PA for k in range(ranks)]
        self.first = np.array(first, np.int32)
        self.steps = max(b - a for a, b in zip(first, last)) + 1
        self.exact = held == self.steps * PA and self.pairs * ranks == PA
        self.both = 2 * channels
        self.half = self.pairs * self.both
        self.group = 2 * local_rows
        self.share = channels // ranks
        self.scale = 1.0 / math.sqrt(NR * columns)

    def column_table(self):
        pair, part, odd, owner = np.meshgrid(
            np.arange(self.pairs),
            np.arange(2),
            np.arange(2),
            np.arange(self.ranks),
            indexing="ij",
        )
        freq = 2 * (self.pairs * owner + pair) + odd
        freq, part = freq.reshape(-1, 1), part.reshape(-1, 1)
        phase = (freq * np.arange(self.columns)[None, :]) % self.columns
        angle = 2.0 * math.pi * phase / self.columns
        table = np.where(part == 0, np.cos(angle), -np.sin(angle))
        return np.where(freq < MODES, table, 0.0).astype(np.float32).astype(jnp.bfloat16)

    def spread(self):
        out = np.zeros((self.ranks * self.group, self.group * self.ranks), np.float32)
        for owner in range(self.ranks):
            for e in range(self.group):
                out[owner * self.group + e, e * self.ranks + owner] = 1.0
        return out.astype(jnp.bfloat16)

    def gather_back(self):
        return self.spread().T

    def share_in(self):
        out = np.zeros((self.channels, self.ranks * 8), np.float32)
        for i in range(self.channels):
            base = (i // self.share) * 8 + i % self.share
            out[i, base] = 1.0
            out[i, base + self.share] = 1.0
        return out.astype(jnp.bfloat16)


def turn_table(freq, mode_part, mode_odd, positions, row_part, row_odd, mode_major):
    turn = lambda a, b: (a[:, None], b[None, :]) if mode_major else (a[None, :], b[:, None])
    f, pos = turn(jnp.asarray(freq), positions)
    mp, rp = turn(jnp.asarray(mode_part), jnp.asarray(row_part))
    mo, ro = turn(jnp.asarray(mode_odd), jnp.asarray(row_odd))
    phase = jnp.mod(f * pos + (mp - rp) * (NR // 4), NR)
    value = jnp.cos(phase.astype(F32) * (2.0 * math.pi / NR))
    return jnp.where(mo == ro, value, 0.0).astype(BF16)


def turn_tables(plan, slab_list):
    rows = plan.ranks * plan.local_rows
    row_index = np.arange(rows)
    positions = jnp.repeat(slab_list, SLAB) * SLAB + jnp.asarray(row_index % SLAB, jnp.int32)

    def modes(order):
        k, step, part, odd, low = np.meshgrid(
            *(np.arange(n) for n in (plan.ranks, plan.steps, 2, 2, 2)), indexing="ij"
        )
        freq = 2 * (plan.first[k] + step) + low - MODES // 2
        return [x.transpose(order).reshape(-1).astype(np.int32) for x in (freq, part, odd)]

    def rows_side(shape_order):
        odd, row, part = np.meshgrid(np.arange(2), row_index, np.arange(2), indexing="ij")
        odd, part = (x.transpose(shape_order).reshape(-1).astype(np.int32) for x in (odd, part))
        spread = jnp.broadcast_to(positions[None, :, None], (2, rows, 2))
        return spread.transpose(shape_order).reshape(-1), part, odd

    forward = turn_table(*modes((0, 1, 2, 3, 4)), *rows_side((0, 1, 2)), True)
    backward = turn_table(*modes((1, 0, 2, 3, 4)), *rows_side((2, 1, 0)), False)
    return forward, backward


LOG_PEAK = math.log2(2.0 * 0.3989422804014327)
NT = (((1,), (1,)), ((), ()))
TN = (((0,), (0,)), ((), ()))


def mask_rows(extent, start, width, rows):
    column = lax.broadcasted_iota(jnp.int32, (16, width), 1) + start
    few = jnp.where(column < extent, 1.0, 0.0).astype(BF16)
    return jnp.concatenate([few] * (rows // 16), axis=0)


def column_kernel(
    plan, ext_hbm, x_hbm, pre_hbm, cot_hbm, tab_hbm, spread_hbm, gp_hbm, out_ref,
    ext_ref, x_ref, pre_ref, cot_ref, lines_ref, tab_ref, spread_ref, stage_ref, in_sems,
    out_sems, misc_sems,
):
    chans, ranks = plan.channels, plan.ranks
    slots = plan.local_rows // SLAB
    part_width, width = plan.columns // COLUMN_PARTS, 256
    first = lax.axis_index("rows") * slots
    units = [
        (slot, begin) for slot in range(slots) for begin in range(0, plan.columns, part_width)
    ]
    loads = {}
    for slot, begin in units:
        rows, cols = pl.ds(slot * SLAB, SLAB), pl.ds(begin, part_width)
        loads[slot, begin] = [
            pltpu.make_async_copy(
                src.at[0, rows, :, cols],
                dst.at[slot, :, :, cols],
                in_sems.at[slot, begin // part_width, n],
            )
            for n, (src, dst) in enumerate(
                ((pre_hbm, pre_ref), (cot_hbm, cot_ref), (x_hbm, x_ref))
            )
        ]
    table = pltpu.make_async_copy(tab_hbm, tab_ref, misc_sems.at[1])
    saves = [
        [
            pltpu.make_async_copy(
                lines_ref.at[slot, pl.ds(row * plan.both + chans, chans)],
                gp_hbm.at[pl.ds((slot * SLAB + row) * chans, chans)],
                out_sems.at[slot, row],
            )
            for row in range(SLAB)
        ]
        for slot in range(slots)
    ]
    small = pltpu.make_async_copy(spread_hbm, spread_ref, misc_sems.at[0])
    extents = pltpu.make_async_copy(ext_hbm, ext_ref, misc_sems.at[2])
    extents.start()
    for slot, begin in units:
        for copy in loads[slot, begin]:
            copy.start()
        if (slot, begin) == units[COLUMN_PARTS - 1]:
            table.start()
    small.start()

    def prepare(slot, begin):
        extent = ext_ref[0, first + slot]
        for start in range(begin, begin + part_width, width):
            cols = slice(start, start + width)
            ones = mask_rows(extent, start, width, chans)
            halves = ones * BF16(0.5)
            for row in range(SLAB):
                value = pre_ref[slot, row, :, cols].astype(F32)
                turned = value * 0.7071067811865476
                bell = jnp.exp2(turned * turned * -1.4426950408889634 + LOG_PEAK)
                slope = value * bell + (1.0 + lax.erf(turned))
                half_cot = (cot_ref[slot, row, :, cols] * halves).astype(F32)
                base = row * plan.both
                lines_ref[slot, base : base + chans, cols] = x_ref[slot, row, :, cols] * ones
                base += chans
                lines_ref[slot, base : base + chans, cols] = (half_cot * slope).astype(BF16)

    def contract(slot):
        return lax.dot_general(
            tab_ref[...], lines_ref[slot], NT, preferred_element_type=F32
        )

    extents.wait()
    sums_of = {}
    for slot in range(slots):
        begins = range(0, plan.columns, part_width)
        if slot == 0:
            for begin in begins:
                for copy in loads[slot, begin]:
                    copy.wait()
                prepare(slot, begin)
            table.wait()
        else:
            for begin in begins:
                for copy in loads[slot, begin]:
                    copy.wait()
            for begin in begins:
                prepare(slot, begin)
            sums_of[slot - 1] = contract(slot - 1)
        for copy in saves[slot]:
            copy.start()
    sums_of[slots - 1] = contract(slots - 1)
    for slot in range(slots):
        for row in range(SLAB):
            spec = sums_of[slot][:, row * plan.both : (row + 1) * plan.both].astype(BF16)
            for pair in range(plan.pairs):
                for part in range(2):
                    for odd in range(2):
                        base = ((pair * 2 + part) * 2 + odd) * ranks
                        lanes = (odd * plan.pairs + pair) * plan.both
                        line = ((slot * SLAB + row) * 2 + part) * ranks
                        stage_ref[line : line + ranks, lanes : lanes + plan.both] = spec[
                            base : base + ranks
                        ]
    small.wait()
    out_ref[...] = jnp.dot(spread_ref[...], stage_ref[...], preferred_element_type=F32).astype(BF16)
    for copies in saves:
        for copy in copies:
            copy.wait()


def weight_kernel(w_ref, x_ref, gp_ref, out_ref, direct_ref):
    part = lax.dot_general(x_ref[0, 0], gp_ref[...], NT, preferred_element_type=F32)
    direct_ref[...] = jnp.dot(w_ref[...], gp_ref[...], preferred_element_type=F32).astype(BF16)

    @pl.when(pl.program_id(0) == 0)
    def _():
        out_ref[...] = part

    @pl.when(pl.program_id(0) > 0)
    def _():
        out_ref[...] += part


def in_two(total):
    high = total.astype(BF16).astype(F32)
    return high, (total - high).astype(BF16).astype(F32)


def row_kernel(plan, turn_ref, in_ref, out_ref):
    half = plan.half
    stacked = jnp.concatenate([in_ref[:, :half], in_ref[:, half:]], axis=0)
    sums = jnp.dot(turn_ref[...], stacked, preferred_element_type=F32)
    out_ref[...] = (sums * plan.scale).astype(BF16)


def out_pair(tile, chans):
    lane = lax.broadcasted_iota(jnp.int32, tile.shape, 1)
    row = lax.broadcasted_iota(jnp.int32, tile.shape, 0)
    across = pltpu.roll(tile, chans, axis=1)
    other = pltpu.roll(tile, 4, axis=0)
    return jnp.where(lane < chans, across, jnp.where(row < 4, other, -other))


def where_held(plan, owner, step, pair, offset):
    place = step * PA + plan.pairs * owner + pair - offset
    ok = (place >= 0) & (place < plan.held) & (plan.pairs * owner + pair < PA)
    return jnp.clip(place, 0, plan.held - 1), ok


def mode_offset(plan):
    k = lax.axis_index("rows")
    return lax.rem(k * plan.held, PA)


def slot_order(plan):
    order = []
    for step in range(plan.steps):
        order += [(step, pair) for pair in range(plan.pairs - plan.pairs % 2)]
    if plan.pairs % 2:
        order += [(step, plan.pairs - 1) for step in range(plan.steps)]
    return order


def mix_kernel(plan, samples, *refs):
    share_refs = refs[:samples]
    in_ref, head_ref, rest_hbm, out_hbm, rest_ref, out_ref, sems, spec_sem, order_sem = refs[samples:]
    chans, both, head = plan.channels, plan.both, head_ref.shape[0]
    rest = plan.steps * PA * chans - head if plan.exact else 0
    if rest:
        load = pltpu.make_async_copy(rest_hbm.at[pl.ds(head, rest)], rest_ref, spec_sem)
        load.start()
        pl.semaphore_signal(order_sem, 1)
        pl.semaphore_wait(order_sem, 1)
    total = share_refs[0][...]
    for ref in share_refs[1:]:
        total = total + ref[...]
    high, low = in_two(total)
    lane = lax.broadcasted_iota(jnp.int32, (8, both), 1)
    share = plan.share
    order = slot_order(plan)

    def left_of(owner, step):
        start = (owner * plan.steps + step) * 8
        tiles = [
            out_pair(in_ref[start : start + 8, p * both : (p + 1) * both].astype(F32), chans)
            for p in range(plan.pairs)
        ]
        return jnp.concatenate(tiles, axis=0).astype(BF16)

    def weights_of(base, count):
        if base + count <= head:
            return head_ref[base : base + count]
        return rest_ref[base - head : base - head + count]

    def put(owner, step, pair, piece):
        value, held = piece
        place = order.index((step, pair))
        if held != place % 2:
            value = pltpu.roll(value, chans, axis=1)
        lanes = slice(place * chans, (place + 1) * chans)
        half = slice((place % 2) * chans, (place % 2 + 1) * chans)
        out_ref[owner * 8 : owner * 8 + 8, lanes] = value[:, half].astype(BF16)

    def mix_general(owner):
        for step in range(plan.steps):
            left = left_of(owner, step)
            for p in range(plan.pairs):
                place, ok = where_held(plan, owner, step, p, mode_offset(plan))
                right = head_ref[pl.ds(pl.multiple_of(place * chans, chans), chans)]
                piece = lax.dot_general(
                    left[8 * p : 8 * p + 8], right, NT, preferred_element_type=F32
                )
                piece = jnp.where(ok, piece, 0.0)
                put(owner, step, p, (jnp.concatenate([piece, piece], axis=1), 0))

    def mix_two(owners, step):
        rows = 8 * plan.pairs
        lefts, rights = [], []
        for m, owner in enumerate(owners):
            left = left_of(owner, step)
            blank = jnp.zeros_like(left)
            lefts.append(
                jnp.concatenate([left if k == m else blank for k in range(len(owners))], axis=1)
            )
            base = (step * PA + owner * plan.pairs) * chans
            rights.append(weights_of(base, plan.pairs * chans))
        values = lax.dot_general(
            jnp.concatenate(lefts, axis=0), jnp.concatenate(rights, axis=1), NT,
            preferred_element_type=F32,
        )
        for m, owner in enumerate(owners):
            for p in range(0, plan.pairs, 2):
                piece = values[m * rows + 8 * p : m * rows + 8 * p + 8, (p // 2) * both :]
                if p + 1 < plan.pairs:
                    after = values[
                        m * rows + 8 * p + 8 : m * rows + 8 * p + 16, (p // 2) * both :
                    ]
                    tile = jnp.where(lane < chans, piece[:, :both], after[:, :both])
                    place = order.index((step, p)) * chans
                    out_ref[owner * 8 : owner * 8 + 8, place : place + both] = tile.astype(BF16)
                else:
                    single = piece[:, :chans]
                    put(owner, step, p, (jnp.concatenate([single, single], axis=1), 0))

    places = out_ref.shape[1] // chans
    for owner in range(plan.ranks):
        lines = slice(owner * 8, owner * 8 + 8)
        if places - 1 > len(order):
            out_ref[lines, len(order) * chans : (places - 1) * chans] = jnp.zeros(
                (8, (places - 1 - len(order)) * chans), BF16
            )
        rows = slice(owner * share, (owner + 1) * share)
        pieces = [high[rows], low[rows]]
        if 2 * share < 8:
            pieces.append(jnp.zeros((8 - 2 * share, chans), F32))
        out_ref[lines, (places - 1) * chans :] = jnp.concatenate(pieces, axis=0).astype(BF16)
    if plan.exact:
        waited = rest == 0
        for step in range(plan.steps):
            for owner in range(0, plan.ranks, 2):
                owners = range(owner, min(owner + 2, plan.ranks))
                end = (step * PA + (owners[-1] + 1) * plan.pairs) * chans
                if end > head and not waited:
                    load.wait()
                    waited = True
                mix_two(owners, step)
    else:
        for owner in range(plan.ranks):
            mix_general(owner)
    chunks = sems.shape[0]
    each = plan.ranks * 8 // chunks
    saves = []
    for chunk in range(chunks):
        span = pl.ds(chunk * each, each)
        copy = pltpu.make_async_copy(out_ref.at[span], out_hbm.at[span], sems.at[chunk])
        copy.start()
        saves.append(copy)
    for copy in saves:
        copy.wait()


def outer_kernel(plan, owners, samples, *refs):
    in_refs, out_ref = refs[:samples], refs[samples]
    chans = plan.channels
    swap = lax.axis_index("batch") != 0

    def body(local, carry):
        owner = pl.program_id(0) * owners + local
        for step in range(plan.steps):
            for pair in range(plan.pairs):
                start = pl.multiple_of(local * (8 * plan.steps) + 8 * step, 8)
                cols = slice(pair * plan.both, (pair + 1) * plan.both)
                tiles = [ref[pl.ds(start, 8), cols].astype(F32) for ref in in_refs]
                if samples == 2:
                    tiles = [
                        jnp.where(swap, tiles[1], tiles[0]),
                        jnp.where(swap, tiles[0], tiles[1]),
                    ]
                left = jnp.concatenate([t[:, :chans] for t in tiles], axis=0).astype(BF16)
                right = jnp.concatenate([out_pair(t, chans) for t in tiles], axis=0).astype(BF16)
                value = lax.dot_general(left, right, TN, preferred_element_type=F32)
                if plan.exact:
                    out_ref[step, local * plan.pairs + pair] = value
                else:
                    place, ok = where_held(plan, owner, step, pair, mode_offset(plan))

                    @pl.when(ok)
                    def _():
                        out_ref[0, place] = value
        return carry

    lax.fori_loop(0, owners, body, 0)


def adjoint_kernel(plan, turn_ref, in_ref, out_ref):
    chans = plan.channels
    order = slot_order(plan)
    parts = []
    for step in range(plan.steps):
        places = [order.index((step, pair)) for pair in range(plan.pairs)]
        parts.append(
            jnp.concatenate([in_ref[:, n * chans : (n + 1) * chans] for n in places], axis=1)
        )
    sums = jnp.dot(turn_ref[...], jnp.concatenate(parts, axis=0), preferred_element_type=F32)
    sums = sums * plan.scale
    real, imag = sums[: sums.shape[0] // 2], sums[sums.shape[0] // 2 :]
    pieces = []
    for pair in range(plan.pairs):
        cols = slice(pair * chans, (pair + 1) * chans)
        pieces += [real[:, cols], imag[:, cols]]
    out_ref[:, : plan.half] = jnp.concatenate(pieces, axis=1).astype(BF16)
    shared = in_ref[:, in_ref.shape[1] - chans :].astype(F32)
    summed = jnp.sum(shared.reshape(plan.ranks, 8, chans), axis=0)
    share = plan.share
    high, low = in_two(summed[:share] + summed[share : 2 * share])
    pieces = [high, low]
    if 2 * share < 8:
        pieces.append(jnp.zeros((8 - 2 * share, chans), F32))
    block = jnp.concatenate(pieces, axis=0)
    block = jnp.concatenate([block, jnp.zeros((8, plan.both - chans), F32)], axis=1)
    out_ref[:, plan.half :] = jnp.concatenate([block] * plan.ranks, axis=0).astype(BF16)


def spatial_kernel(
    plan, step, weight_scale, ext_hbm, in_ref, back_ref, share_ref, tab_ref, direct_ref,
    out_hbm, gw_hbm, ext_ref, left_ref, out_ref, gw_ref, sems, ext_sem, gw_sem,
):
    chans, rows = plan.channels, plan.local_rows
    block = 2 * plan.ranks
    slots = rows // SLAB
    first = lax.axis_index("rows") * slots
    extents = pltpu.make_async_copy(ext_hbm, ext_ref, ext_sem)
    extents.start()
    ordered = jnp.dot(back_ref[...], in_ref[:, : plan.half], preferred_element_type=F32)
    for row in range(rows):
        lines = ordered[row * block : (row + 1) * block]
        pieces = [lines[:, b * chans : (b + 1) * chans] for b in range(2 * plan.pairs)]
        stacked = jnp.concatenate(pieces, axis=0)
        left_ref[row * chans : (row + 1) * chans] = stacked.T.astype(BF16)
    shared = in_ref[:, plan.half : plan.half + chans]
    total = jnp.dot(share_ref[...], shared, preferred_element_type=F32)
    gw_ref[...] = total * weight_scale
    copies = [pltpu.make_async_copy(gw_ref, gw_hbm, gw_sem)]
    copies[0].start()
    extents.wait()
    for n in range(plan.columns // step):
        cols = slice(n * step, (n + 1) * step)
        spatial = jnp.dot(left_ref[...], tab_ref[:, cols], preferred_element_type=F32)
        for slot in range(slots):
            live = mask_rows(ext_ref[0, first + slot], n * step, step, chans)
            for row in range(slot * SLAB, (slot + 1) * SLAB):
                lines = slice(row * chans, (row + 1) * chans)
                value = spatial[lines] + direct_ref[lines, cols].astype(F32)
                out_ref[row, :, cols] = value.astype(BF16) * live
        copy = pltpu.make_async_copy(
            out_ref.at[:, :, pl.ds(n * step, step)],
            out_hbm.at[0, :, :, pl.ds(n * step, step)],
            sems.at[n],
        )
        copy.start()
        copies.append(copy)
    for copy in copies:
        copy.wait()


def whole(array):
    return pl.BlockSpec(array.shape, lambda *_: (0,) * array.ndim)


def call(body, args, outs, name, flops, mib, **kw):
    size = sum(a.size * a.dtype.itemsize for a in (*args, *outs))
    return pl.pallas_call(
        body,
        out_shape=outs,
        name=name,
        cost_estimate=pl.CostEstimate(flops=flops, bytes_accessed=size, transcendentals=0),
        compiler_params=pltpu.CompilerParams(vmem_limit_bytes=mib * 1024 * 1024),
        **kw,
    )(*args)


def stay(value):
    return pltpu.with_memory_space_constraint(value, pltpu.HBM)


def exchange(value):
    return lax.all_to_all(value, "rows", split_axis=0, concat_axis=0, tiled=True)


def every_sample(value, count):
    if count == 1:
        return [value]
    if count == 2:
        return [value, lax.ppermute(value, "batch", [(0, 1), (1, 0)])]
    gathered = lax.all_gather(value, "batch")
    return [gathered[i] for i in range(count)]


def shards(layer_input, pre_activation, cotangent, weight, spectral, slab_ids, extents):
    samples = lax.axis_size("batch")
    _, local_rows, chans, columns = layer_input.shape
    plan = Plan(lax.axis_size("rows"), local_rows, chans, columns, spectral.shape[0])
    ranks, active = plan.ranks, slab_ids.shape[1]
    sds = jax.ShapeDtypeStruct
    table = jnp.asarray(plan.column_table())
    forward_turn, backward_turn = turn_tables(plan, slab_ids[0])

    spread = jnp.asarray(plan.spread())
    lines, wide = ranks * plan.group, 2 * plan.half
    slots = local_rows // SLAB

    hbm = pl.BlockSpec(memory_space=pltpu.HBM)
    vmem = pl.BlockSpec(memory_space=pltpu.VMEM)
    stored = (slots, SLAB, chans, columns)
    grad_pre, sent = call(
        functools.partial(column_kernel, plan),
        (extents, layer_input, pre_activation, cotangent, table, spread),
        (sds((local_rows * chans, columns), BF16), sds((lines, wide), BF16)),
        "columns",
        2 * local_rows * 2 * chans * columns * 2 * MODES,
        62,
        in_specs=[hbm] * 6,
        out_specs=(hbm, vmem),
        scratch_shapes=[
            pltpu.SMEM(extents.shape, jnp.int32),
            pltpu.VMEM(stored, BF16),
            pltpu.VMEM(stored, BF16),
            pltpu.VMEM(stored, BF16),
            pltpu.VMEM((slots, 2 * SLAB * chans, columns), BF16),
            pltpu.VMEM(table.shape, BF16),
            pltpu.VMEM(spread.shape, BF16),
            pltpu.VMEM((plan.group * ranks, 2 * plan.half), BF16),
            pltpu.SemaphoreType.DMA((slots, COLUMN_PARTS, 3)),
            pltpu.SemaphoreType.DMA((slots, SLAB)),
            pltpu.SemaphoreType.DMA((3,)),
        ],
    )
    received = exchange(sent)
    local_weight, direct = call(
        weight_kernel,
        (weight, stay(layer_input), stay(grad_pre)),
        (sds((chans, chans), F32), sds(grad_pre.shape, BF16)),
        "weights",
        4 * layer_input.size * chans,
        16,
        grid=(local_rows,),
        in_specs=[
            pl.BlockSpec((chans, chans), lambda r: (0, 0)),
            pl.BlockSpec((1, 1, chans, columns), lambda r: (0, r, 0, 0)),
            pl.BlockSpec((chans, columns), lambda r: (r, 0)),
        ],
        out_specs=(
            pl.BlockSpec((chans, chans), lambda r: (0, 0)),
            pl.BlockSpec((chans, columns), lambda r: (r, 0)),
        ),
    )
    received, local_weight = lax.optimization_barrier((received, local_weight))
    shares = every_sample(local_weight, samples)
    if samples > 2:
        shares = [sum(shares[1:], shares[0])]

    mode_lines = ranks * plan.steps * 8
    sent = call(
        functools.partial(row_kernel, plan),
        (forward_turn, received),
        (sds((mode_lines, plan.half), BF16),),
        "rows",
        2 * forward_turn.size * plan.half,
        16,
    )[0]
    modes = exchange(sent)

    chunks = 4 if plan.exact and ranks % 4 == 0 else 1
    owners = ranks // chunks
    if plan.exact:
        held_shape, held_block = (plan.steps, PA), (plan.steps, owners * plan.pairs)
    else:
        held_shape, held_block = (1, plan.held), (1, plan.held)
    held_spec = pl.BlockSpec(
        held_block + (chans, plan.both), lambda n: (0, n if plan.exact else 0, 0, 0)
    )
    mode_block = pl.BlockSpec((owners * plan.steps * 8, plan.half), lambda n: (n, 0))
    mixed = plan.steps * plan.pairs
    back_width = -(-(mixed + 1) // 2) * plan.both
    flat = spectral.reshape(-1, plan.both)
    owners_two = ranks * plan.steps // 2
    head = (5 * owners_two // 3) * plan.pairs * chans if plan.exact else flat.shape[0]
    sent = call(
        functools.partial(mix_kernel, plan, len(shares)),
        (*shares, modes, flat[:head], stay(flat)),
        (sds((ranks * 8, back_width), BF16),),
        "mix",
        16 * spectral.size,
        16,
        in_specs=[vmem] * (len(shares) + 2) + [hbm],
        out_specs=(hbm,),
        scratch_shapes=[
            pltpu.VMEM((max(flat.shape[0] - head, 8), plan.both), BF16),
            pltpu.VMEM((ranks * 8, back_width), BF16),
            pltpu.SemaphoreType.DMA((chunks,)),
            pltpu.SemaphoreType.DMA,
            pltpu.SemaphoreType.REGULAR,
        ],
    )[0]
    returned = exchange(sent)

    every = every_sample(modes, samples)
    grad_spectral = call(
        functools.partial(outer_kernel, plan, owners, samples),
        tuple(every),
        (sds(held_shape + spectral.shape[1:], F32),),
        "outer",
        16 * samples * spectral.size,
        16,
        grid=(chunks,),
        in_specs=[mode_block] * samples,
        out_specs=(held_spec,),
    )[0].reshape(spectral.shape)

    weight_scale = 1.0 / math.sqrt(samples * active * SLAB * columns)
    sent = call(
        functools.partial(adjoint_kernel, plan),
        (backward_turn, returned),
        (sds((lines, plan.half + plan.both), BF16),),
        "adjoint",
        2 * backward_turn.size * plan.pairs * chans,
        16,
    )[0]
    local_back = exchange(sent)

    step = 512
    gather_back, share_in = jnp.asarray(plan.gather_back()), jnp.asarray(plan.share_in())
    grad_input, grad_weight = call(
        functools.partial(spatial_kernel, plan, step, weight_scale),
        (extents, local_back, gather_back, share_in, table, direct),
        (sds(layer_input.shape, BF16), sds((chans, chans), F32)),
        "spatial",
        2 * local_rows * chans * columns * table.shape[0],
        16,
        in_specs=[hbm] + [vmem] * 5,
        out_specs=(hbm, hbm),
        scratch_shapes=[
            pltpu.SMEM(extents.shape, jnp.int32),
            pltpu.VMEM((local_rows * chans, table.shape[0]), BF16),
            pltpu.VMEM((local_rows, chans, columns), BF16),
            pltpu.VMEM((chans, chans), F32),
            pltpu.SemaphoreType.DMA((columns // step,)),
            pltpu.SemaphoreType.DMA,
            pltpu.SemaphoreType.DMA,
        ],
    )
    return (grad_input, grad_spectral, grad_weight)


def solution(mesh):
    return jax.shard_map(
        shards,
        mesh=mesh,
        in_specs=(
            P("batch", "rows", None, None),
            P("batch", "rows", None, None),
            P("batch", "rows", None, None),
            P(),
            P("rows", None, None),
            P("batch", None),
            P("batch", None),
        ),
        out_specs=(P("batch", "rows", None, None), P("rows", None, None), P()),
        check_vma=False,
    )
```

```python
import functools
import math

import jax
import jax.numpy as jnp
import numpy as np
from jax import lax
from jax.experimental import pallas as pl
from jax.experimental.pallas import tpu as pltpu
from jax.sharding import PartitionSpec as P

PA = 48
SLAB = 2
NR = 4096
MODES = 96
F32 = jnp.float32
BF16 = jnp.bfloat16
COLUMN_PARTS = 2


class Plan:
    def __init__(self, ranks, local_rows, channels, columns, held):
        self.ranks = ranks
        self.local_rows = local_rows
        self.channels = channels
        self.columns = columns
        self.held = held
        self.pairs = -(-PA // ranks)
        first = [(held * k) // PA for k in range(ranks)]
        last = [(held * (k + 1) - 1) // PA for k in range(ranks)]
        self.first = np.array(first, np.int32)
        self.steps = max(b - a for a, b in zip(first, last)) + 1
        self.exact = held == self.steps * PA and self.pairs * ranks == PA
        self.both = 2 * channels
        self.half = self.pairs * self.both
        self.group = 2 * local_rows
        self.share = channels // ranks
        self.scale = 1.0 / math.sqrt(NR * columns)

    def column_table(self):
        pair, part, odd, owner = np.meshgrid(
            np.arange(self.pairs),
            np.arange(2),
            np.arange(2),
            np.arange(self.ranks),
            indexing="ij",
        )
        freq = 2 * (self.pairs * owner + pair) + odd
        freq, part = freq.reshape(-1, 1), part.reshape(-1, 1)
        phase = (freq * np.arange(self.columns)[None, :]) % self.columns
        angle = 2.0 * math.pi * phase / self.columns
        table = np.where(part == 0, np.cos(angle), -np.sin(angle))
        return np.where(freq < MODES, table, 0.0).astype(np.float32).astype(jnp.bfloat16)

    def spread(self):
        out = np.zeros((self.ranks * self.group, self.group * self.ranks), np.float32)
        for owner in range(self.ranks):
            for e in range(self.group):
                out[owner * self.group + e, e * self.ranks + owner] = 1.0
        return out.astype(jnp.bfloat16)

    def gather_back(self):
        return self.spread().T

    def share_in(self):
        out = np.zeros((self.channels, self.ranks * 8), np.float32)
        for i in range(self.channels):
            base = (i // self.share) * 8 + i % self.share
            out[i, base] = 1.0
            out[i, base + self.share] = 1.0
        return out.astype(jnp.bfloat16)


def turn_table(freq, mode_part, mode_odd, positions, row_part, row_odd, mode_major):
    turn = lambda a, b: (a[:, None], b[None, :]) if mode_major else (a[None, :], b[:, None])
    f, pos = turn(jnp.asarray(freq), positions)
    mp, rp = turn(jnp.asarray(mode_part), jnp.asarray(row_part))
    mo, ro = turn(jnp.asarray(mode_odd), jnp.asarray(row_odd))
    phase = jnp.mod(f * pos + (mp - rp) * (NR // 4), NR)
    value = jnp.cos(phase.astype(F32) * (2.0 * math.pi / NR))
    return jnp.where(mo == ro, value, 0.0).astype(BF16)


def turn_tables(plan, slab_list):
    rows = plan.ranks * plan.local_rows
    row_index = np.arange(rows)
    positions = jnp.repeat(slab_list, SLAB) * SLAB + jnp.asarray(row_index % SLAB, jnp.int32)

    def modes(order):
        k, step, part, odd, low = np.meshgrid(
            *(np.arange(n) for n in (plan.ranks, plan.steps, 2, 2, 2)), indexing="ij"
        )
        freq = 2 * (plan.first[k] + step) + low - MODES // 2
        return [x.transpose(order).reshape(-1).astype(np.int32) for x in (freq, part, odd)]

    def rows_side(shape_order):
        odd, row, part = np.meshgrid(np.arange(2), row_index, np.arange(2), indexing="ij")
        odd, part = (x.transpose(shape_order).reshape(-1).astype(np.int32) for x in (odd, part))
        spread = jnp.broadcast_to(positions[None, :, None], (2, rows, 2))
        return spread.transpose(shape_order).reshape(-1), part, odd

    forward = turn_table(*modes((0, 1, 2, 3, 4)), *rows_side((0, 1, 2)), True)
    backward = turn_table(*modes((1, 0, 2, 3, 4)), *rows_side((2, 1, 0)), False)
    return forward, backward


LOG_PEAK = math.log2(2.0 * 0.3989422804014327)
NT = (((1,), (1,)), ((), ()))
TN = (((0,), (0,)), ((), ()))


def mask_rows(extent, start, width, rows):
    column = lax.broadcasted_iota(jnp.int32, (16, width), 1) + start
    few = jnp.where(column < extent, 1.0, 0.0).astype(BF16)
    return jnp.concatenate([few] * (rows // 16), axis=0)


def column_kernel(
    plan, ext_hbm, x_hbm, pre_hbm, cot_hbm, tab_hbm, spread_hbm, gp_hbm, out_hbm,
    ext_ref, x_ref, pre_ref, cot_ref, lines_ref, tab_ref, spread_ref, stage_ref, out_ref, in_sems,
    out_sems, misc_sems, sent_sems,
):
    chans, ranks = plan.channels, plan.ranks
    slots = plan.local_rows // SLAB
    part_width, width = plan.columns // COLUMN_PARTS, 256
    first = lax.axis_index("rows") * slots
    units = [
        (slot, begin) for slot in range(slots) for begin in range(0, plan.columns, part_width)
    ]
    loads = {}
    for slot, begin in units:
        rows, cols = pl.ds(slot * SLAB, SLAB), pl.ds(begin, part_width)
        loads[slot, begin] = [
            pltpu.make_async_copy(
                src.at[0, rows, :, cols],
                dst.at[slot, :, :, cols],
                in_sems.at[slot, begin // part_width, n],
            )
            for n, (src, dst) in enumerate(
                ((pre_hbm, pre_ref), (cot_hbm, cot_ref), (x_hbm, x_ref))
            )
        ]
    table = pltpu.make_async_copy(tab_hbm, tab_ref, misc_sems.at[1])
    saves = [
        [
            pltpu.make_async_copy(
                lines_ref.at[slot, pl.ds(row * plan.both + chans, chans)],
                gp_hbm.at[pl.ds((slot * SLAB + row) * chans, chans)],
                out_sems.at[slot, row],
            )
            for row in range(SLAB)
        ]
        for slot in range(slots)
    ]
    small = pltpu.make_async_copy(spread_hbm, spread_ref, misc_sems.at[0])
    extents = pltpu.make_async_copy(ext_hbm, ext_ref, misc_sems.at[2])
    extents.start()
    for slot, begin in units:
        for copy in loads[slot, begin]:
            copy.start()
        if (slot, begin) == units[COLUMN_PARTS - 1]:
            table.start()
    small.start()

    def prepare(slot, begin):
        extent = ext_ref[0, first + slot]
        for start in range(begin, begin + part_width, width):
            cols = slice(start, start + width)
            ones = mask_rows(extent, start, width, chans)
            halves = ones * BF16(0.5)
            for row in range(SLAB):
                value = pre_ref[slot, row, :, cols].astype(F32)
                turned = value * 0.7071067811865476
                bell = jnp.exp2(turned * turned * -1.4426950408889634 + LOG_PEAK)
                slope = value * bell + (1.0 + lax.erf(turned))
                half_cot = (cot_ref[slot, row, :, cols] * halves).astype(F32)
                base = row * plan.both
                lines_ref[slot, base : base + chans, cols] = x_ref[slot, row, :, cols] * ones
                base += chans
                lines_ref[slot, base : base + chans, cols] = (half_cot * slope).astype(BF16)

    def contract(slot):
        return lax.dot_general(
            tab_ref[...], lines_ref[slot], NT, preferred_element_type=F32
        )

    extents.wait()
    sums_of = {}
    for slot in range(slots):
        begins = range(0, plan.columns, part_width)
        if slot == 0:
            for begin in begins:
                for copy in loads[slot, begin]:
                    copy.wait()
                prepare(slot, begin)
            table.wait()
        else:
            for begin in begins:
                for copy in loads[slot, begin]:
                    copy.wait()
            for begin in begins:
                prepare(slot, begin)
            sums_of[slot - 1] = contract(slot - 1)
        for copy in saves[slot]:
            copy.start()
    sums_of[slots - 1] = contract(slots - 1)
    for slot in range(slots):
        for row in range(SLAB):
            spec = sums_of[slot][:, row * plan.both : (row + 1) * plan.both].astype(BF16)
            for pair in range(plan.pairs):
                for part in range(2):
                    for odd in range(2):
                        base = ((pair * 2 + part) * 2 + odd) * ranks
                        lanes = (odd * plan.pairs + pair) * plan.both
                        line = ((slot * SLAB + row) * 2 + part) * ranks
                        stage_ref[line : line + ranks, lanes : lanes + plan.both] = spec[
                            base : base + ranks
                        ]
    small.wait()
    parts = sent_sems.shape[0]
    each = stage_ref.shape[1] // parts
    for n in range(parts):
        cols = slice(n * each, (n + 1) * each)
        out_ref[:, cols] = jnp.dot(
            spread_ref[...], stage_ref[:, cols], preferred_element_type=F32
        ).astype(BF16)
        span = pl.ds(n * each, each)
        copy = pltpu.make_async_copy(out_ref.at[:, span], out_hbm.at[:, span], sent_sems.at[n])
        copy.start()
        saves.append([copy])
    for copies in saves:
        for copy in copies:
            copy.wait()


def weight_kernel(x_ref, gp_ref, out_ref):
    part = lax.dot_general(x_ref[0, 0], gp_ref[...], NT, preferred_element_type=F32)

    @pl.when(pl.program_id(0) == 0)
    def _():
        out_ref[...] = part

    @pl.when(pl.program_id(0) > 0)
    def _():
        out_ref[...] += part


def in_two(total):
    high = total.astype(BF16).astype(F32)
    return high, (total - high).astype(BF16).astype(F32)


def row_kernel(plan, turn_ref, in_ref, out_hbm, out_ref, sems):
    half = plan.half
    stacked = jnp.concatenate([in_ref[:, :half], in_ref[:, half:]], axis=0)
    parts = sems.shape[0]
    each = out_ref.shape[0] // parts
    copies = []
    for n in range(parts):
        sums = jnp.dot(
            turn_ref[n * each : (n + 1) * each], stacked, preferred_element_type=F32
        )
        out_ref[n * each : (n + 1) * each] = (sums * plan.scale).astype(BF16)
        span = pl.ds(n * each, each)
        copy = pltpu.make_async_copy(out_ref.at[span], out_hbm.at[span], sems.at[n])
        copy.start()
        copies.append(copy)
    for copy in copies:
        copy.wait()


def out_pair(tile, chans):
    lane = lax.broadcasted_iota(jnp.int32, tile.shape, 1)
    row = lax.broadcasted_iota(jnp.int32, tile.shape, 0)
    across = pltpu.roll(tile, chans, axis=1)
    other = pltpu.roll(tile, 4, axis=0)
    return jnp.where(lane < chans, across, jnp.where(row < 4, other, -other))


def where_held(plan, owner, step, pair, offset):
    place = step * PA + plan.pairs * owner + pair - offset
    ok = (place >= 0) & (place < plan.held) & (plan.pairs * owner + pair < PA)
    return jnp.clip(place, 0, plan.held - 1), ok


def mode_offset(plan):
    k = lax.axis_index("rows")
    return lax.rem(k * plan.held, PA)


def slot_order(plan):
    order = []
    for step in range(plan.steps):
        order += [(step, pair) for pair in range(plan.pairs - plan.pairs % 2)]
    if plan.pairs % 2:
        order += [(step, plan.pairs - 1) for step in range(plan.steps)]
    return order


def mix_kernel(plan, samples, *refs):
    share_refs = refs[:samples]
    in_ref, head_ref, rest_hbm, out_hbm, rest_ref, out_ref, sems, spec_sem, order_sem = refs[samples:]
    chans, both, head = plan.channels, plan.both, head_ref.shape[0]
    rest = plan.steps * PA * chans - head if plan.exact else 0
    if rest:
        load = pltpu.make_async_copy(rest_hbm.at[pl.ds(head, rest)], rest_ref, spec_sem)
        load.start()
        pl.semaphore_signal(order_sem, 1)
        pl.semaphore_wait(order_sem, 1)
    total = share_refs[0][...]
    for ref in share_refs[1:]:
        total = total + ref[...]
    high, low = in_two(total)
    lane = lax.broadcasted_iota(jnp.int32, (8, both), 1)
    share = plan.share
    order = slot_order(plan)

    def left_of(owner, step):
        start = (owner * plan.steps + step) * 8
        tiles = [
            out_pair(in_ref[start : start + 8, p * both : (p + 1) * both].astype(F32), chans)
            for p in range(plan.pairs)
        ]
        return jnp.concatenate(tiles, axis=0).astype(BF16)

    def weights_of(base, count):
        if base + count <= head:
            return head_ref[base : base + count]
        return rest_ref[base - head : base - head + count]

    def put(owner, step, pair, piece):
        value, held = piece
        place = order.index((step, pair))
        if held != place % 2:
            value = pltpu.roll(value, chans, axis=1)
        lanes = slice(place * chans, (place + 1) * chans)
        half = slice((place % 2) * chans, (place % 2 + 1) * chans)
        out_ref[owner * 8 : owner * 8 + 8, lanes] = value[:, half].astype(BF16)

    def mix_general(owner):
        for step in range(plan.steps):
            left = left_of(owner, step)
            for p in range(plan.pairs):
                place, ok = where_held(plan, owner, step, p, mode_offset(plan))
                right = head_ref[pl.ds(pl.multiple_of(place * chans, chans), chans)]
                piece = lax.dot_general(
                    left[8 * p : 8 * p + 8], right, NT, preferred_element_type=F32
                )
                piece = jnp.where(ok, piece, 0.0)
                put(owner, step, p, (jnp.concatenate([piece, piece], axis=1), 0))

    def mix_two(owners, step):
        rows = 8 * plan.pairs
        lefts, rights = [], []
        for m, owner in enumerate(owners):
            left = left_of(owner, step)
            blank = jnp.zeros_like(left)
            lefts.append(
                jnp.concatenate([left if k == m else blank for k in range(len(owners))], axis=1)
            )
            base = (step * PA + owner * plan.pairs) * chans
            rights.append(weights_of(base, plan.pairs * chans))
        values = lax.dot_general(
            jnp.concatenate(lefts, axis=0), jnp.concatenate(rights, axis=1), NT,
            preferred_element_type=F32,
        )
        for m, owner in enumerate(owners):
            for p in range(0, plan.pairs, 2):
                piece = values[m * rows + 8 * p : m * rows + 8 * p + 8, (p // 2) * both :]
                if p + 1 < plan.pairs:
                    after = values[
                        m * rows + 8 * p + 8 : m * rows + 8 * p + 16, (p // 2) * both :
                    ]
                    tile = jnp.where(lane < chans, piece[:, :both], after[:, :both])
                    place = order.index((step, p)) * chans
                    out_ref[owner * 8 : owner * 8 + 8, place : place + both] = tile.astype(BF16)
                else:
                    single = piece[:, :chans]
                    put(owner, step, p, (jnp.concatenate([single, single], axis=1), 0))

    places = out_ref.shape[1] // chans
    for owner in range(plan.ranks):
        lines = slice(owner * 8, owner * 8 + 8)
        if places - 1 > len(order):
            out_ref[lines, len(order) * chans : (places - 1) * chans] = jnp.zeros(
                (8, (places - 1 - len(order)) * chans), BF16
            )
        rows = slice(owner * share, (owner + 1) * share)
        pieces = [high[rows], low[rows]]
        if 2 * share < 8:
            pieces.append(jnp.zeros((8 - 2 * share, chans), F32))
        out_ref[lines, (places - 1) * chans :] = jnp.concatenate(pieces, axis=0).astype(BF16)
    if plan.exact:
        waited = rest == 0
        for step in range(plan.steps):
            for owner in range(0, plan.ranks, 2):
                owners = range(owner, min(owner + 2, plan.ranks))
                end = (step * PA + (owners[-1] + 1) * plan.pairs) * chans
                if end > head and not waited:
                    load.wait()
                    waited = True
                mix_two(owners, step)
    else:
        for owner in range(plan.ranks):
            mix_general(owner)
    chunks = sems.shape[0]
    each = plan.ranks * 8 // chunks
    saves = []
    for chunk in range(chunks):
        span = pl.ds(chunk * each, each)
        copy = pltpu.make_async_copy(out_ref.at[span], out_hbm.at[span], sems.at[chunk])
        copy.start()
        saves.append(copy)
    for copy in saves:
        copy.wait()


def outer_kernel(plan, owners, samples, *refs):
    in_refs, out_ref = refs[:samples], refs[samples]
    chans = plan.channels
    swap = lax.axis_index("batch") != 0

    def body(local, carry):
        owner = pl.program_id(0) * owners + local
        for step in range(plan.steps):
            for pair in range(plan.pairs):
                start = pl.multiple_of(local * (8 * plan.steps) + 8 * step, 8)
                cols = slice(pair * plan.both, (pair + 1) * plan.both)
                tiles = [ref[pl.ds(start, 8), cols].astype(F32) for ref in in_refs]
                if samples == 2:
                    tiles = [
                        jnp.where(swap, tiles[1], tiles[0]),
                        jnp.where(swap, tiles[0], tiles[1]),
                    ]
                left = jnp.concatenate([t[:, :chans] for t in tiles], axis=0).astype(BF16)
                right = jnp.concatenate([out_pair(t, chans) for t in tiles], axis=0).astype(BF16)
                value = lax.dot_general(left, right, TN, preferred_element_type=F32)
                if plan.exact:
                    out_ref[step, local * plan.pairs + pair] = value
                else:
                    place, ok = where_held(plan, owner, step, pair, mode_offset(plan))

                    @pl.when(ok)
                    def _():
                        out_ref[0, place] = value
        return carry

    lax.fori_loop(0, owners, body, 0)


def adjoint_kernel(plan, turn_ref, in_ref, out_hbm, out_ref, sem):
    chans = plan.channels
    order = slot_order(plan)
    parts = []
    for step in range(plan.steps):
        places = [order.index((step, pair)) for pair in range(plan.pairs)]
        parts.append(
            jnp.concatenate([in_ref[:, n * chans : (n + 1) * chans] for n in places], axis=1)
        )
    sums = jnp.dot(turn_ref[...], jnp.concatenate(parts, axis=0), preferred_element_type=F32)
    sums = sums * plan.scale
    real, imag = sums[: sums.shape[0] // 2], sums[sums.shape[0] // 2 :]
    pieces = []
    for pair in range(plan.pairs):
        cols = slice(pair * chans, (pair + 1) * chans)
        pieces += [real[:, cols], imag[:, cols]]
    out_ref[:, : plan.half] = jnp.concatenate(pieces, axis=1).astype(BF16)
    shared = in_ref[:, in_ref.shape[1] - chans :].astype(F32)
    summed = jnp.sum(shared.reshape(plan.ranks, 8, chans), axis=0)
    share = plan.share
    high, low = in_two(summed[:share] + summed[share : 2 * share])
    pieces = [high, low]
    if 2 * share < 8:
        pieces.append(jnp.zeros((8 - 2 * share, chans), F32))
    block = jnp.concatenate(pieces, axis=0)
    block = jnp.concatenate([block, jnp.zeros((8, plan.both - chans), F32)], axis=1)
    out_ref[:, plan.half :] = jnp.concatenate([block] * plan.ranks, axis=0).astype(BF16)
    copy = pltpu.make_async_copy(out_ref, out_hbm, sem)
    copy.start()
    copy.wait()


def spatial_kernel(
    plan, step, weight_scale, ext_hbm, in_ref, back_ref, share_ref, w_ref, tab_ref, gp_ref,
    out_hbm, gw_hbm, ext_ref, left_ref, out_ref, gw_ref, sems, ext_sem, gw_sem,
):
    chans, rows = plan.channels, plan.local_rows
    block = 2 * plan.ranks
    slots = rows // SLAB
    first = lax.axis_index("rows") * slots
    extents = pltpu.make_async_copy(ext_hbm, ext_ref, ext_sem)
    extents.start()
    ordered = jnp.dot(back_ref[...], in_ref[:, : plan.half], preferred_element_type=F32)
    for row in range(rows):
        lines = ordered[row * block : (row + 1) * block]
        pieces = [lines[:, b * chans : (b + 1) * chans] for b in range(2 * plan.pairs)]
        stacked = jnp.concatenate(pieces, axis=0)
        left_ref[row * chans : (row + 1) * chans] = stacked.T.astype(BF16)
    shared = in_ref[:, plan.half : plan.half + chans]
    total = jnp.dot(share_ref[...], shared, preferred_element_type=F32)
    gw_ref[...] = total * weight_scale
    copies = [pltpu.make_async_copy(gw_ref, gw_hbm, gw_sem)]
    copies[0].start()
    extents.wait()
    for n in range(plan.columns // step):
        cols = slice(n * step, (n + 1) * step)
        spatial = jnp.dot(left_ref[...], tab_ref[:, cols], preferred_element_type=F32)
        for slot in range(slots):
            live = mask_rows(ext_ref[0, first + slot], n * step, step, chans)
            for row in range(slot * SLAB, (slot + 1) * SLAB):
                lines = slice(row * chans, (row + 1) * chans)
                direct = jnp.dot(w_ref[...], gp_ref[lines, cols], preferred_element_type=F32)
                out_ref[row, :, cols] = (spatial[lines] + direct).astype(BF16) * live
        copy = pltpu.make_async_copy(
            out_ref.at[:, :, pl.ds(n * step, step)],
            out_hbm.at[0, :, :, pl.ds(n * step, step)],
            sems.at[n],
        )
        copy.start()
        copies.append(copy)
    for copy in copies:
        copy.wait()


def whole(array):
    return pl.BlockSpec(array.shape, lambda *_: (0,) * array.ndim)


def call(body, args, outs, name, flops, mib, **kw):
    size = sum(a.size * a.dtype.itemsize for a in (*args, *outs))
    return pl.pallas_call(
        body,
        out_shape=outs,
        name=name,
        cost_estimate=pl.CostEstimate(flops=flops, bytes_accessed=size, transcendentals=0),
        compiler_params=pltpu.CompilerParams(vmem_limit_bytes=mib * 1024 * 1024),
        **kw,
    )(*args)


def stay(value):
    return pltpu.with_memory_space_constraint(value, pltpu.HBM)


def exchange(value):
    return lax.all_to_all(value, "rows", split_axis=0, concat_axis=0, tiled=True)


def every_sample(value, count):
    if count == 1:
        return [value]
    if count == 2:
        return [value, lax.ppermute(value, "batch", [(0, 1), (1, 0)])]
    gathered = lax.all_gather(value, "batch")
    return [gathered[i] for i in range(count)]


def shards(layer_input, pre_activation, cotangent, weight, spectral, slab_ids, extents):
    samples = lax.axis_size("batch")
    _, local_rows, chans, columns = layer_input.shape
    plan = Plan(lax.axis_size("rows"), local_rows, chans, columns, spectral.shape[0])
    ranks, active = plan.ranks, slab_ids.shape[1]
    sds = jax.ShapeDtypeStruct
    table = jnp.asarray(plan.column_table())
    forward_turn, backward_turn = turn_tables(plan, slab_ids[0])

    spread = jnp.asarray(plan.spread())
    lines, wide = ranks * plan.group, 2 * plan.half
    slots = local_rows // SLAB

    hbm = pl.BlockSpec(memory_space=pltpu.HBM)
    vmem = pl.BlockSpec(memory_space=pltpu.VMEM)
    stored = (slots, SLAB, chans, columns)
    grad_pre, sent = call(
        functools.partial(column_kernel, plan),
        (extents, layer_input, pre_activation, cotangent, table, spread),
        (sds((local_rows * chans, columns), BF16), sds((lines, wide), BF16)),
        "columns",
        2 * local_rows * 2 * chans * columns * 2 * MODES,
        62,
        in_specs=[hbm] * 6,
        out_specs=(hbm, hbm),
        scratch_shapes=[
            pltpu.SMEM(extents.shape, jnp.int32),
            pltpu.VMEM(stored, BF16),
            pltpu.VMEM(stored, BF16),
            pltpu.VMEM(stored, BF16),
            pltpu.VMEM((slots, 2 * SLAB * chans, columns), BF16),
            pltpu.VMEM(table.shape, BF16),
            pltpu.VMEM(spread.shape, BF16),
            pltpu.VMEM((plan.group * ranks, 2 * plan.half), BF16),
            pltpu.VMEM((lines, wide), BF16),
            pltpu.SemaphoreType.DMA((slots, COLUMN_PARTS, 3)),
            pltpu.SemaphoreType.DMA((slots, SLAB)),
            pltpu.SemaphoreType.DMA((3,)),
            pltpu.SemaphoreType.DMA((2 if plan.half % 128 == 0 else 1,)),
        ],
    )
    received = exchange(sent)
    local_weight = call(
        weight_kernel,
        (stay(layer_input), stay(grad_pre)),
        (sds((chans, chans), F32),),
        "weights",
        2 * layer_input.size * chans,
        16,
        grid=(local_rows,),
        in_specs=[
            pl.BlockSpec((1, 1, chans, columns), lambda r: (0, r, 0, 0)),
            pl.BlockSpec((chans, columns), lambda r: (r, 0)),
        ],
        out_specs=(pl.BlockSpec((chans, chans), lambda r: (0, 0)),),
    )[0]
    received, local_weight = lax.optimization_barrier((received, local_weight))
    shares = every_sample(local_weight, samples)
    if samples > 2:
        shares = [sum(shares[1:], shares[0])]

    mode_lines = ranks * plan.steps * 8
    sent = call(
        functools.partial(row_kernel, plan),
        (forward_turn, received),
        (sds((mode_lines, plan.half), BF16),),
        "rows",
        2 * forward_turn.size * plan.half,
        16,
        in_specs=[vmem] * 2,
        out_specs=(hbm,),
        scratch_shapes=[
            pltpu.VMEM((mode_lines, plan.half), BF16),
            pltpu.SemaphoreType.DMA((2,)),
        ],
    )[0]
    modes = exchange(sent)

    chunks = 4 if plan.exact and ranks % 4 == 0 else 1
    owners = ranks // chunks
    if plan.exact:
        held_shape, held_block = (plan.steps, PA), (plan.steps, owners * plan.pairs)
    else:
        held_shape, held_block = (1, plan.held), (1, plan.held)
    held_spec = pl.BlockSpec(
        held_block + (chans, plan.both), lambda n: (0, n if plan.exact else 0, 0, 0)
    )
    mode_block = pl.BlockSpec((owners * plan.steps * 8, plan.half), lambda n: (n, 0))
    mixed = plan.steps * plan.pairs
    back_width = -(-(mixed + 1) // 2) * plan.both
    flat = spectral.reshape(-1, plan.both)
    owners_two = ranks * plan.steps // 2
    head = (5 * owners_two // 3) * plan.pairs * chans if plan.exact else flat.shape[0]
    sent = call(
        functools.partial(mix_kernel, plan, len(shares)),
        (*shares, modes, flat[:head], stay(flat)),
        (sds((ranks * 8, back_width), BF16),),
        "mix",
        16 * spectral.size,
        16,
        in_specs=[vmem] * (len(shares) + 2) + [hbm],
        out_specs=(hbm,),
        scratch_shapes=[
            pltpu.VMEM((max(flat.shape[0] - head, 8), plan.both), BF16),
            pltpu.VMEM((ranks * 8, back_width), BF16),
            pltpu.SemaphoreType.DMA((chunks,)),
            pltpu.SemaphoreType.DMA,
            pltpu.SemaphoreType.REGULAR,
        ],
    )[0]
    returned = exchange(sent)

    every = every_sample(modes, samples)
    grad_spectral = call(
        functools.partial(outer_kernel, plan, owners, samples),
        tuple(every),
        (sds(held_shape + spectral.shape[1:], F32),),
        "outer",
        16 * samples * spectral.size,
        16,
        grid=(chunks,),
        in_specs=[mode_block] * samples,
        out_specs=(held_spec,),
    )[0].reshape(spectral.shape)

    weight_scale = 1.0 / math.sqrt(samples * active * SLAB * columns)
    sent = call(
        functools.partial(adjoint_kernel, plan),
        (backward_turn, returned),
        (sds((lines, plan.half + plan.both), BF16),),
        "adjoint",
        2 * backward_turn.size * plan.pairs * chans,
        16,
        in_specs=[vmem] * 2,
        out_specs=(hbm,),
        scratch_shapes=[
            pltpu.VMEM((lines, plan.half + plan.both), BF16),
            pltpu.SemaphoreType.DMA,
        ],
    )[0]
    local_back = exchange(sent)

    step = 512
    gather_back, share_in = jnp.asarray(plan.gather_back()), jnp.asarray(plan.share_in())
    grad_input, grad_weight = call(
        functools.partial(spatial_kernel, plan, step, weight_scale),
        (extents, local_back, gather_back, share_in, weight, table, grad_pre),
        (sds(layer_input.shape, BF16), sds((chans, chans), F32)),
        "spatial",
        2 * local_rows * chans * columns * (table.shape[0] + chans),
        16,
        in_specs=[hbm] + [vmem] * 6,
        out_specs=(hbm, hbm),
        scratch_shapes=[
            pltpu.SMEM(extents.shape, jnp.int32),
            pltpu.VMEM((local_rows * chans, table.shape[0]), BF16),
            pltpu.VMEM((local_rows, chans, columns), BF16),
            pltpu.VMEM((chans, chans), F32),
            pltpu.SemaphoreType.DMA((columns // step,)),
            pltpu.SemaphoreType.DMA,
            pltpu.SemaphoreType.DMA,
        ],
    )
    return (grad_input, grad_spectral, grad_weight)


def solution(mesh):
    return jax.shard_map(
        shards,
        mesh=mesh,
        in_specs=(
            P("batch", "rows", None, None),
            P("batch", "rows", None, None),
            P("batch", "rows", None, None),
            P(),
            P("rows", None, None),
            P("batch", None),
            P("batch", None),
        ),
        out_specs=(P("batch", "rows", None, None), P("rows", None, None), P()),
        check_vma=False,
    )
```

```python
import functools
import math

import jax
import jax.numpy as jnp
import numpy as np
from jax import lax
from jax.experimental import pallas as pl
from jax.experimental.pallas import tpu as pltpu
from jax.sharding import PartitionSpec as P

PA = 48
SLAB = 2
NR = 4096
MODES = 96
F32 = jnp.float32
BF16 = jnp.bfloat16
COLUMN_PARTS = 2


class Plan:
    def __init__(self, ranks, local_rows, channels, columns, held):
        self.ranks = ranks
        self.local_rows = local_rows
        self.channels = channels
        self.columns = columns
        self.held = held
        self.pairs = -(-PA // ranks)
        first = [(held * k) // PA for k in range(ranks)]
        last = [(held * (k + 1) - 1) // PA for k in range(ranks)]
        self.first = np.array(first, np.int32)
        self.steps = max(b - a for a, b in zip(first, last)) + 1
        self.exact = held == self.steps * PA and self.pairs * ranks == PA
        self.both = 2 * channels
        self.half = self.pairs * self.both
        self.group = 2 * local_rows
        self.share = channels // ranks
        self.scale = 1.0 / math.sqrt(NR * columns)

    def column_table(self):
        pair, part, odd, owner = np.meshgrid(
            np.arange(self.pairs),
            np.arange(2),
            np.arange(2),
            np.arange(self.ranks),
            indexing="ij",
        )
        freq = 2 * (self.pairs * owner + pair) + odd
        freq, part = freq.reshape(-1, 1), part.reshape(-1, 1)
        phase = (freq * np.arange(self.columns)[None, :]) % self.columns
        angle = 2.0 * math.pi * phase / self.columns
        table = np.where(part == 0, np.cos(angle), -np.sin(angle))
        return np.where(freq < MODES, table, 0.0).astype(np.float32).astype(jnp.bfloat16)

    def spread(self):
        out = np.zeros((self.ranks * self.group, self.group * self.ranks), np.float32)
        for owner in range(self.ranks):
            for e in range(self.group):
                out[owner * self.group + e, e * self.ranks + owner] = 1.0
        return out.astype(jnp.bfloat16)

    def gather_back(self):
        return self.spread().T

    def share_in(self):
        out = np.zeros((self.channels, self.ranks * 8), np.float32)
        for i in range(self.channels):
            base = (i // self.share) * 8 + i % self.share
            out[i, base] = 1.0
            out[i, base + self.share] = 1.0
        return out.astype(jnp.bfloat16)


def turn_table(freq, mode_part, mode_odd, positions, row_part, row_odd, mode_major):
    turn = lambda a, b: (a[:, None], b[None, :]) if mode_major else (a[None, :], b[:, None])
    f, pos = turn(jnp.asarray(freq), positions)
    mp, rp = turn(jnp.asarray(mode_part), jnp.asarray(row_part))
    mo, ro = turn(jnp.asarray(mode_odd), jnp.asarray(row_odd))
    phase = jnp.mod(f * pos + (mp - rp) * (NR // 4), NR)
    value = jnp.cos(phase.astype(F32) * (2.0 * math.pi / NR))
    return jnp.where(mo == ro, value, 0.0).astype(BF16)


def turn_tables(plan, slab_list):
    rows = plan.ranks * plan.local_rows
    row_index = np.arange(rows)
    positions = jnp.repeat(slab_list, SLAB) * SLAB + jnp.asarray(row_index % SLAB, jnp.int32)

    def modes(order):
        k, step, part, odd, low = np.meshgrid(
            *(np.arange(n) for n in (plan.ranks, plan.steps, 2, 2, 2)), indexing="ij"
        )
        freq = 2 * (plan.first[k] + step) + low - MODES // 2
        return [x.transpose(order).reshape(-1).astype(np.int32) for x in (freq, part, odd)]

    def rows_side(shape_order):
        odd, row, part = np.meshgrid(np.arange(2), row_index, np.arange(2), indexing="ij")
        odd, part = (x.transpose(shape_order).reshape(-1).astype(np.int32) for x in (odd, part))
        spread = jnp.broadcast_to(positions[None, :, None], (2, rows, 2))
        return spread.transpose(shape_order).reshape(-1), part, odd

    forward = turn_table(*modes((0, 1, 2, 3, 4)), *rows_side((0, 1, 2)), True)
    backward = turn_table(*modes((1, 0, 2, 3, 4)), *rows_side((2, 1, 0)), False)
    return forward, backward


LOG_PEAK = math.log2(2.0 * 0.3989422804014327)
NT = (((1,), (1,)), ((), ()))
TN = (((0,), (0,)), ((), ()))


def mask_rows(extent, start, width, rows):
    column = lax.broadcasted_iota(jnp.int32, (16, width), 1) + start
    few = jnp.where(column < extent, 1.0, 0.0).astype(BF16)
    return jnp.concatenate([few] * (rows // 16), axis=0)


def column_kernel(
    plan, ext_hbm, x_hbm, pre_hbm, cot_hbm, tab_hbm, spread_hbm, gp_hbm, out_hbm,
    ext_ref, x_ref, pre_ref, cot_ref, lines_ref, tab_ref, spread_ref, stage_ref, out_ref, in_sems,
    out_sems, misc_sems, sent_sems,
):
    chans, ranks = plan.channels, plan.ranks
    slots = plan.local_rows // SLAB
    part_width, width = plan.columns // COLUMN_PARTS, 256
    first = lax.axis_index("rows") * slots
    units = [
        (slot, begin) for slot in range(slots) for begin in range(0, plan.columns, part_width)
    ]
    loads = {}
    for slot, begin in units:
        rows, cols = pl.ds(slot * SLAB, SLAB), pl.ds(begin, part_width)
        loads[slot, begin] = [
            pltpu.make_async_copy(
                src.at[0, rows, :, cols],
                dst.at[slot, :, :, cols],
                in_sems.at[slot, begin // part_width, n],
            )
            for n, (src, dst) in enumerate(
                ((pre_hbm, pre_ref), (cot_hbm, cot_ref), (x_hbm, x_ref))
            )
        ]
    table = pltpu.make_async_copy(tab_hbm, tab_ref, misc_sems.at[1])
    saves = [
        [
            pltpu.make_async_copy(
                lines_ref.at[slot, pl.ds(row * plan.both + chans, chans)],
                gp_hbm.at[pl.ds((slot * SLAB + row) * chans, chans)],
                out_sems.at[slot, row],
            )
            for row in range(SLAB)
        ]
        for slot in range(slots)
    ]
    small = pltpu.make_async_copy(spread_hbm, spread_ref, misc_sems.at[0])
    extents = pltpu.make_async_copy(ext_hbm, ext_ref, misc_sems.at[2])
    extents.start()
    for slot, begin in units:
        for copy in loads[slot, begin]:
            copy.start()
        if (slot, begin) == units[COLUMN_PARTS - 1]:
            table.start()
    small.start()

    def prepare(slot, begin):
        extent = ext_ref[0, first + slot]
        for start in range(begin, begin + part_width, width):
            cols = slice(start, start + width)
            ones = mask_rows(extent, start, width, chans)
            halves = ones * BF16(0.5)
            for row in range(SLAB):
                value = pre_ref[slot, row, :, cols].astype(F32)
                turned = value * 0.7071067811865476
                bell = jnp.exp2(turned * turned * -1.4426950408889634 + LOG_PEAK)
                slope = value * bell + (1.0 + lax.erf(turned))
                half_cot = (cot_ref[slot, row, :, cols] * halves).astype(F32)
                base = row * plan.both
                lines_ref[slot, base : base + chans, cols] = x_ref[slot, row, :, cols] * ones
                base += chans
                lines_ref[slot, base : base + chans, cols] = (half_cot * slope).astype(BF16)

    def contract(slot):
        return lax.dot_general(
            tab_ref[...], lines_ref[slot], NT, preferred_element_type=F32
        )

    extents.wait()
    sums_of = {}
    for slot in range(slots):
        begins = range(0, plan.columns, part_width)
        if slot == 0:
            for begin in begins:
                for copy in loads[slot, begin]:
                    copy.wait()
                prepare(slot, begin)
            table.wait()
        else:
            for begin in begins:
                for copy in loads[slot, begin]:
                    copy.wait()
            for begin in begins:
                prepare(slot, begin)
            sums_of[slot - 1] = contract(slot - 1)
        for copy in saves[slot]:
            copy.start()
    sums_of[slots - 1] = contract(slots - 1)
    for slot in range(slots):
        for row in range(SLAB):
            spec = sums_of[slot][:, row * plan.both : (row + 1) * plan.both].astype(BF16)
            for pair in range(plan.pairs):
                for part in range(2):
                    for odd in range(2):
                        base = ((pair * 2 + part) * 2 + odd) * ranks
                        lanes = (odd * plan.pairs + pair) * plan.both
                        line = ((slot * SLAB + row) * 2 + part) * ranks
                        stage_ref[line : line + ranks, lanes : lanes + plan.both] = spec[
                            base : base + ranks
                        ]
    small.wait()
    parts = sent_sems.shape[0]
    each = stage_ref.shape[1] // parts
    for n in range(parts):
        cols = slice(n * each, (n + 1) * each)
        out_ref[:, cols] = jnp.dot(
            spread_ref[...], stage_ref[:, cols], preferred_element_type=F32
        ).astype(BF16)
        span = pl.ds(n * each, each)
        copy = pltpu.make_async_copy(out_ref.at[:, span], out_hbm.at[:, span], sent_sems.at[n])
        copy.start()
        saves.append([copy])
    for copies in saves:
        for copy in copies:
            copy.wait()


def weight_kernel(w_ref, x_ref, gp_ref, out_ref, direct_ref):
    part = lax.dot_general(x_ref[0, 0], gp_ref[...], NT, preferred_element_type=F32)
    direct_ref[...] = jnp.dot(w_ref[...], gp_ref[...], preferred_element_type=F32).astype(BF16)

    @pl.when(pl.program_id(0) == 0)
    def _():
        out_ref[...] = part

    @pl.when(pl.program_id(0) > 0)
    def _():
        out_ref[...] += part


def in_two(total):
    high = total.astype(BF16).astype(F32)
    return high, (total - high).astype(BF16).astype(F32)


def row_kernel(plan, turn_ref, in_ref, out_hbm, out_ref, sems):
    half = plan.half
    stacked = jnp.concatenate([in_ref[:, :half], in_ref[:, half:]], axis=0)
    parts = sems.shape[0]
    each = out_ref.shape[0] // parts
    copies = []
    for n in range(parts):
        sums = jnp.dot(
            turn_ref[n * each : (n + 1) * each], stacked, preferred_element_type=F32
        )
        out_ref[n * each : (n + 1) * each] = (sums * plan.scale).astype(BF16)
        span = pl.ds(n * each, each)
        copy = pltpu.make_async_copy(out_ref.at[span], out_hbm.at[span], sems.at[n])
        copy.start()
        copies.append(copy)
    for copy in copies:
        copy.wait()


def out_pair(tile, chans):
    lane = lax.broadcasted_iota(jnp.int32, tile.shape, 1)
    row = lax.broadcasted_iota(jnp.int32, tile.shape, 0)
    across = pltpu.roll(tile, chans, axis=1)
    other = pltpu.roll(tile, 4, axis=0)
    return jnp.where(lane < chans, across, jnp.where(row < 4, other, -other))


def where_held(plan, owner, step, pair, offset):
    place = step * PA + plan.pairs * owner + pair - offset
    ok = (place >= 0) & (place < plan.held) & (plan.pairs * owner + pair < PA)
    return jnp.clip(place, 0, plan.held - 1), ok


def mode_offset(plan):
    k = lax.axis_index("rows")
    return lax.rem(k * plan.held, PA)


def slot_order(plan):
    order = []
    for step in range(plan.steps):
        order += [(step, pair) for pair in range(plan.pairs - plan.pairs % 2)]
    if plan.pairs % 2:
        order += [(step, plan.pairs - 1) for step in range(plan.steps)]
    return order


def mix_kernel(plan, samples, *refs):
    share_refs = refs[:samples]
    in_ref, head_ref, rest_hbm, out_hbm, rest_ref, out_ref, sems, spec_sem, order_sem = refs[samples:]
    chans, both, head = plan.channels, plan.both, head_ref.shape[0]
    rest = plan.steps * PA * chans - head if plan.exact else 0
    if rest:
        load = pltpu.make_async_copy(rest_hbm.at[pl.ds(head, rest)], rest_ref, spec_sem)
        load.start()
        pl.semaphore_signal(order_sem, 1)
        pl.semaphore_wait(order_sem, 1)
    total = share_refs[0][...]
    for ref in share_refs[1:]:
        total = total + ref[...]
    high, low = in_two(total)
    lane = lax.broadcasted_iota(jnp.int32, (8, both), 1)
    share = plan.share
    order = slot_order(plan)

    def left_of(owner, step):
        start = (owner * plan.steps + step) * 8
        tiles = [
            out_pair(in_ref[start : start + 8, p * both : (p + 1) * both].astype(F32), chans)
            for p in range(plan.pairs)
        ]
        return jnp.concatenate(tiles, axis=0).astype(BF16)

    def weights_of(base, count):
        if base + count <= head:
            return head_ref[base : base + count]
        return rest_ref[base - head : base - head + count]

    def put(owner, step, pair, piece):
        value, held = piece
        place = order.index((step, pair))
        if held != place % 2:
            value = pltpu.roll(value, chans, axis=1)
        lanes = slice(place * chans, (place + 1) * chans)
        half = slice((place % 2) * chans, (place % 2 + 1) * chans)
        out_ref[owner * 8 : owner * 8 + 8, lanes] = value[:, half].astype(BF16)

    def mix_general(owner):
        for step in range(plan.steps):
            left = left_of(owner, step)
            for p in range(plan.pairs):
                place, ok = where_held(plan, owner, step, p, mode_offset(plan))
                right = head_ref[pl.ds(pl.multiple_of(place * chans, chans), chans)]
                piece = lax.dot_general(
                    left[8 * p : 8 * p + 8], right, NT, preferred_element_type=F32
                )
                piece = jnp.where(ok, piece, 0.0)
                put(owner, step, p, (jnp.concatenate([piece, piece], axis=1), 0))

    def mix_two(owners, step):
        rows = 8 * plan.pairs
        lefts, rights = [], []
        for m, owner in enumerate(owners):
            left = left_of(owner, step)
            blank = jnp.zeros_like(left)
            lefts.append(
                jnp.concatenate([left if k == m else blank for k in range(len(owners))], axis=1)
            )
            base = (step * PA + owner * plan.pairs) * chans
            rights.append(weights_of(base, plan.pairs * chans))
        values = lax.dot_general(
            jnp.concatenate(lefts, axis=0), jnp.concatenate(rights, axis=1), NT,
            preferred_element_type=F32,
        )
        for m, owner in enumerate(owners):
            for p in range(0, plan.pairs, 2):
                piece = values[m * rows + 8 * p : m * rows + 8 * p + 8, (p // 2) * both :]
                if p + 1 < plan.pairs:
                    after = values[
                        m * rows + 8 * p + 8 : m * rows + 8 * p + 16, (p // 2) * both :
                    ]
                    tile = jnp.where(lane < chans, piece[:, :both], after[:, :both])
                    place = order.index((step, p)) * chans
                    out_ref[owner * 8 : owner * 8 + 8, place : place + both] = tile.astype(BF16)
                else:
                    single = piece[:, :chans]
                    put(owner, step, p, (jnp.concatenate([single, single], axis=1), 0))

    places = out_ref.shape[1] // chans
    for owner in range(plan.ranks):
        lines = slice(owner * 8, owner * 8 + 8)
        if places - 1 > len(order):
            out_ref[lines, len(order) * chans : (places - 1) * chans] = jnp.zeros(
                (8, (places - 1 - len(order)) * chans), BF16
            )
        rows = slice(owner * share, (owner + 1) * share)
        pieces = [high[rows], low[rows]]
        if 2 * share < 8:
            pieces.append(jnp.zeros((8 - 2 * share, chans), F32))
        out_ref[lines, (places - 1) * chans :] = jnp.concatenate(pieces, axis=0).astype(BF16)
    if plan.exact:
        waited = rest == 0
        for step in range(plan.steps):
            for owner in range(0, plan.ranks, 2):
                owners = range(owner, min(owner + 2, plan.ranks))
                end = (step * PA + (owners[-1] + 1) * plan.pairs) * chans
                if end > head and not waited:
                    load.wait()
                    waited = True
                mix_two(owners, step)
    else:
        for owner in range(plan.ranks):
            mix_general(owner)
    chunks = sems.shape[0]
    each = plan.ranks * 8 // chunks
    saves = []
    for chunk in range(chunks):
        span = pl.ds(chunk * each, each)
        copy = pltpu.make_async_copy(out_ref.at[span], out_hbm.at[span], sems.at[chunk])
        copy.start()
        saves.append(copy)
    for copy in saves:
        copy.wait()


def outer_kernel(plan, owners, samples, *refs):
    in_refs, out_ref = refs[:samples], refs[samples]
    chans = plan.channels
    swap = lax.axis_index("batch") != 0

    def body(local, carry):
        owner = pl.program_id(0) * owners + local
        for step in range(plan.steps):
            for pair in range(plan.pairs):
                start = pl.multiple_of(local * (8 * plan.steps) + 8 * step, 8)
                cols = slice(pair * plan.both, (pair + 1) * plan.both)
                tiles = [ref[pl.ds(start, 8), cols].astype(F32) for ref in in_refs]
                if samples == 2:
                    tiles = [
                        jnp.where(swap, tiles[1], tiles[0]),
                        jnp.where(swap, tiles[0], tiles[1]),
                    ]
                left = jnp.concatenate([t[:, :chans] for t in tiles], axis=0).astype(BF16)
                right = jnp.concatenate([out_pair(t, chans) for t in tiles], axis=0).astype(BF16)
                value = lax.dot_general(left, right, TN, preferred_element_type=F32)
                if plan.exact:
                    out_ref[step, local * plan.pairs + pair] = value
                else:
                    place, ok = where_held(plan, owner, step, pair, mode_offset(plan))

                    @pl.when(ok)
                    def _():
                        out_ref[0, place] = value
        return carry

    lax.fori_loop(0, owners, body, 0)


def adjoint_kernel(plan, turn_ref, in_ref, out_hbm, out_ref, sem):
    chans = plan.channels
    order = slot_order(plan)
    parts = []
    for step in range(plan.steps):
        places = [order.index((step, pair)) for pair in range(plan.pairs)]
        parts.append(
            jnp.concatenate([in_ref[:, n * chans : (n + 1) * chans] for n in places], axis=1)
        )
    sums = jnp.dot(turn_ref[...], jnp.concatenate(parts, axis=0), preferred_element_type=F32)
    sums = sums * plan.scale
    real, imag = sums[: sums.shape[0] // 2], sums[sums.shape[0] // 2 :]
    pieces = []
    for pair in range(plan.pairs):
        cols = slice(pair * chans, (pair + 1) * chans)
        pieces += [real[:, cols], imag[:, cols]]
    out_ref[:, : plan.half] = jnp.concatenate(pieces, axis=1).astype(BF16)
    shared = in_ref[:, in_ref.shape[1] - chans :].astype(F32)
    summed = jnp.sum(shared.reshape(plan.ranks, 8, chans), axis=0)
    share = plan.share
    high, low = in_two(summed[:share] + summed[share : 2 * share])
    pieces = [high, low]
    if 2 * share < 8:
        pieces.append(jnp.zeros((8 - 2 * share, chans), F32))
    block = jnp.concatenate(pieces, axis=0)
    block = jnp.concatenate([block, jnp.zeros((8, plan.both - chans), F32)], axis=1)
    out_ref[:, plan.half :] = jnp.concatenate([block] * plan.ranks, axis=0).astype(BF16)
    copy = pltpu.make_async_copy(out_ref, out_hbm, sem)
    copy.start()
    copy.wait()


def spatial_kernel(
    plan, step, weight_scale, ext_hbm, in_ref, back_ref, share_ref, tab_ref, direct_ref,
    out_hbm, gw_hbm, ext_ref, left_ref, out_ref, gw_ref, sems, ext_sem, gw_sem,
):
    chans, rows = plan.channels, plan.local_rows
    block = 2 * plan.ranks
    slots = rows // SLAB
    first = lax.axis_index("rows") * slots
    extents = pltpu.make_async_copy(ext_hbm, ext_ref, ext_sem)
    extents.start()
    ordered = jnp.dot(back_ref[...], in_ref[:, : plan.half], preferred_element_type=F32)
    for row in range(rows):
        lines = ordered[row * block : (row + 1) * block]
        pieces = [lines[:, b * chans : (b + 1) * chans] for b in range(2 * plan.pairs)]
        stacked = jnp.concatenate(pieces, axis=0)
        left_ref[row * chans : (row + 1) * chans] = stacked.T.astype(BF16)
    shared = in_ref[:, plan.half : plan.half + chans]
    total = jnp.dot(share_ref[...], shared, preferred_element_type=F32)
    gw_ref[...] = total * weight_scale
    copies = [pltpu.make_async_copy(gw_ref, gw_hbm, gw_sem)]
    copies[0].start()
    extents.wait()
    for n in range(plan.columns // step):
        cols = slice(n * step, (n + 1) * step)
        spatial = jnp.dot(left_ref[...], tab_ref[:, cols], preferred_element_type=F32)
        for slot in range(slots):
            live = mask_rows(ext_ref[0, first + slot], n * step, step, chans)
            for row in range(slot * SLAB, (slot + 1) * SLAB):
                lines = slice(row * chans, (row + 1) * chans)
                value = spatial[lines] + direct_ref[lines, cols].astype(F32)
                out_ref[row, :, cols] = value.astype(BF16) * live
        copy = pltpu.make_async_copy(
            out_ref.at[:, :, pl.ds(n * step, step)],
            out_hbm.at[0, :, :, pl.ds(n * step, step)],
            sems.at[n],
        )
        copy.start()
        copies.append(copy)
    for copy in copies:
        copy.wait()


def whole(array):
    return pl.BlockSpec(array.shape, lambda *_: (0,) * array.ndim)


def call(body, args, outs, name, flops, mib, **kw):
    size = sum(a.size * a.dtype.itemsize for a in (*args, *outs))
    return pl.pallas_call(
        body,
        out_shape=outs,
        name=name,
        cost_estimate=pl.CostEstimate(flops=flops, bytes_accessed=size, transcendentals=0),
        compiler_params=pltpu.CompilerParams(vmem_limit_bytes=mib * 1024 * 1024),
        **kw,
    )(*args)


def stay(value):
    return pltpu.with_memory_space_constraint(value, pltpu.HBM)


def exchange(value):
    return lax.all_to_all(value, "rows", split_axis=0, concat_axis=0, tiled=True)


def every_sample(value, count):
    if count == 1:
        return [value]
    if count == 2:
        return [value, lax.ppermute(value, "batch", [(0, 1), (1, 0)])]
    gathered = lax.all_gather(value, "batch")
    return [gathered[i] for i in range(count)]


def shards(layer_input, pre_activation, cotangent, weight, spectral, slab_ids, extents):
    samples = lax.axis_size("batch")
    _, local_rows, chans, columns = layer_input.shape
    plan = Plan(lax.axis_size("rows"), local_rows, chans, columns, spectral.shape[0])
    ranks, active = plan.ranks, slab_ids.shape[1]
    sds = jax.ShapeDtypeStruct
    table = jnp.asarray(plan.column_table())
    forward_turn, backward_turn = turn_tables(plan, slab_ids[0])

    spread = jnp.asarray(plan.spread())
    lines, wide = ranks * plan.group, 2 * plan.half
    slots = local_rows // SLAB

    hbm = pl.BlockSpec(memory_space=pltpu.HBM)
    vmem = pl.BlockSpec(memory_space=pltpu.VMEM)
    stored = (slots, SLAB, chans, columns)
    grad_pre, sent = call(
        functools.partial(column_kernel, plan),
        (extents, layer_input, pre_activation, cotangent, table, spread),
        (sds((local_rows * chans, columns), BF16), sds((lines, wide), BF16)),
        "columns",
        2 * local_rows * 2 * chans * columns * 2 * MODES,
        62,
        in_specs=[hbm] * 6,
        out_specs=(hbm, hbm),
        scratch_shapes=[
            pltpu.SMEM(extents.shape, jnp.int32),
            pltpu.VMEM(stored, BF16),
            pltpu.VMEM(stored, BF16),
            pltpu.VMEM(stored, BF16),
            pltpu.VMEM((slots, 2 * SLAB * chans, columns), BF16),
            pltpu.VMEM(table.shape, BF16),
            pltpu.VMEM(spread.shape, BF16),
            pltpu.VMEM((plan.group * ranks, 2 * plan.half), BF16),
            pltpu.VMEM((lines, wide), BF16),
            pltpu.SemaphoreType.DMA((slots, COLUMN_PARTS, 3)),
            pltpu.SemaphoreType.DMA((slots, SLAB)),
            pltpu.SemaphoreType.DMA((3,)),
            pltpu.SemaphoreType.DMA((2 if plan.half % 128 == 0 else 1,)),
        ],
    )
    received = exchange(sent)
    local_weight, direct = call(
        weight_kernel,
        (weight, stay(layer_input), stay(grad_pre)),
        (sds((chans, chans), F32), sds(grad_pre.shape, BF16)),
        "weights",
        4 * layer_input.size * chans,
        16,
        grid=(local_rows,),
        in_specs=[
            pl.BlockSpec((chans, chans), lambda r: (0, 0)),
            pl.BlockSpec((1, 1, chans, columns), lambda r: (0, r, 0, 0)),
            pl.BlockSpec((chans, columns), lambda r: (r, 0)),
        ],
        out_specs=(
            pl.BlockSpec((chans, chans), lambda r: (0, 0)),
            pl.BlockSpec((chans, columns), lambda r: (r, 0)),
        ),
    )
    received, local_weight = lax.optimization_barrier((received, local_weight))
    shares = every_sample(local_weight, samples)
    if samples > 2:
        shares = [sum(shares[1:], shares[0])]

    mode_lines = ranks * plan.steps * 8
    sent = call(
        functools.partial(row_kernel, plan),
        (forward_turn, received),
        (sds((mode_lines, plan.half), BF16),),
        "rows",
        2 * forward_turn.size * plan.half,
        16,
        in_specs=[vmem] * 2,
        out_specs=(hbm,),
        scratch_shapes=[
            pltpu.VMEM((mode_lines, plan.half), BF16),
            pltpu.SemaphoreType.DMA((2,)),
        ],
    )[0]
    modes = exchange(sent)

    chunks = 4 if plan.exact and ranks % 4 == 0 else 1
    owners = ranks // chunks
    if plan.exact:
        held_shape, held_block = (plan.steps, PA), (plan.steps, owners * plan.pairs)
    else:
        held_shape, held_block = (1, plan.held), (1, plan.held)
    held_spec = pl.BlockSpec(
        held_block + (chans, plan.both), lambda n: (0, n if plan.exact else 0, 0, 0)
    )
    mode_block = pl.BlockSpec((owners * plan.steps * 8, plan.half), lambda n: (n, 0))
    mixed = plan.steps * plan.pairs
    back_width = -(-(mixed + 1) // 2) * plan.both
    flat = spectral.reshape(-1, plan.both)
    owners_two = ranks * plan.steps // 2
    head = (5 * owners_two // 3) * plan.pairs * chans if plan.exact else flat.shape[0]
    sent = call(
        functools.partial(mix_kernel, plan, len(shares)),
        (*shares, modes, flat[:head], stay(flat)),
        (sds((ranks * 8, back_width), BF16),),
        "mix",
        16 * spectral.size,
        16,
        in_specs=[vmem] * (len(shares) + 2) + [hbm],
        out_specs=(hbm,),
        scratch_shapes=[
            pltpu.VMEM((max(flat.shape[0] - head, 8), plan.both), BF16),
            pltpu.VMEM((ranks * 8, back_width), BF16),
            pltpu.SemaphoreType.DMA((chunks,)),
            pltpu.SemaphoreType.DMA,
            pltpu.SemaphoreType.REGULAR,
        ],
    )[0]
    returned = exchange(sent)

    every = every_sample(modes, samples)
    grad_spectral = call(
        functools.partial(outer_kernel, plan, owners, samples),
        tuple(every),
        (sds(held_shape + spectral.shape[1:], F32),),
        "outer",
        16 * samples * spectral.size,
        16,
        grid=(chunks,),
        in_specs=[mode_block] * samples,
        out_specs=(held_spec,),
    )[0].reshape(spectral.shape)

    weight_scale = 1.0 / math.sqrt(samples * active * SLAB * columns)
    sent = call(
        functools.partial(adjoint_kernel, plan),
        (backward_turn, returned),
        (sds((lines, plan.half + plan.both), BF16),),
        "adjoint",
        2 * backward_turn.size * plan.pairs * chans,
        16,
        in_specs=[vmem] * 2,
        out_specs=(hbm,),
        scratch_shapes=[
            pltpu.VMEM((lines, plan.half + plan.both), BF16),
            pltpu.SemaphoreType.DMA,
        ],
    )[0]
    local_back = exchange(sent)

    step = 512
    gather_back, share_in = jnp.asarray(plan.gather_back()), jnp.asarray(plan.share_in())
    grad_input, grad_weight = call(
        functools.partial(spatial_kernel, plan, step, weight_scale),
        (extents, local_back, gather_back, share_in, table, direct),
        (sds(layer_input.shape, BF16), sds((chans, chans), F32)),
        "spatial",
        2 * local_rows * chans * columns * table.shape[0],
        16,
        in_specs=[hbm] + [vmem] * 5,
        out_specs=(hbm, hbm),
        scratch_shapes=[
            pltpu.SMEM(extents.shape, jnp.int32),
            pltpu.VMEM((local_rows * chans, table.shape[0]), BF16),
            pltpu.VMEM((local_rows, chans, columns), BF16),
            pltpu.VMEM((chans, chans), F32),
            pltpu.SemaphoreType.DMA((columns // step,)),
            pltpu.SemaphoreType.DMA,
            pltpu.SemaphoreType.DMA,
        ],
    )
    return (grad_input, grad_spectral, grad_weight)


def solution(mesh):
    return jax.shard_map(
        shards,
        mesh=mesh,
        in_specs=(
            P("batch", "rows", None, None),
            P("batch", "rows", None, None),
            P("batch", "rows", None, None),
            P(),
            P("rows", None, None),
            P("batch", None),
            P("batch", None),
        ),
        out_specs=(P("batch", "rows", None, None), P("rows", None, None), P()),
        check_vma=False,
    )
```
